32 devices in a mesh: dp: 8 (over z, y), mp: 4 (over x, core).
Axes of the slice: x: 2, y: 2, z: 4, core: 2. Of those that a mesh axis runs over, the one named last changes fastest.
Arguments:
- states: bfloat16 [32768, 512], P(('dp', 'mp')), may hold values from -6 to 6
- cotangent: bfloat16 [32768, 512], P(('dp', 'mp')), may hold values from -6 to 6
- halting: int32 [32768], P(('dp', 'mp')), may hold values 0 or 1
- lengths: int32 [16], P('dp'), may hold values from 1 to 2048, 20480 in all
- attention_weights: float32 [4, 512, 512], P(None, 'dp', 'mp'), may hold values from -3 to 3, as said below
- inner_weight: float32 [512, 2048], P('dp', 'mp'), may hold values from -0.25 to 0.25
- outer_weight: float32 [2048, 512], P('dp', 'mp'), may hold values from -0.125 to 0.125
- norm_gains: float32 [2, 512], replicated, may hold values from 0.5 to 1.5
- norm_biases: float32 [2, 512], replicated, may hold values from -3 to 3
- attention_left: float32 [4, 512, 512], P(None, 'dp', 'mp'), may hold values from -5.869539e-07 to 6.836954e-06, as said below
- attention_right: float32 [4, 512, 512], P(None, 'dp', 'mp'), may hold values from -5.869539e-07 to 6.836954e-06, as said below
- inner_left: float32 [512, 512], P('dp', 'mp'), may hold values from -1.17390774e-06 to 2.6173908e-05, as said below
- inner_right: float32 [2048, 2048], P('dp', 'mp'), may hold values from -5.869539e-07 to 6.836954e-06, as said below
- outer_left: float32 [2048, 2048], P('dp', 'mp'), may hold values from -5.869539e-07 to 6.836954e-06, as said below
- outer_right: float32 [512, 512], P('dp', 'mp'), may hold values from -1.17390774e-06 to 2.6173908e-05, as said below
- attention_left_root: float32 [4, 512, 512], P(None, 'dp'), may hold values from -5.3125 to 36.425198, as said below
- attention_right_root: float32 [4, 512, 512], P(None, None, 'mp'), may hold values from -5.3125 to 36.425198, as said below
- inner_left_root: float32 [512, 512], P('dp'), may hold values from -3.7565048 to 25.756505, as said below
- inner_right_root: float32 [2048, 2048], P(None, 'mp'), may hold values from -2.65625 to 33.768948, as said below
- outer_left_root: float32 [2048, 2048], P('dp'), may hold values from -2.65625 to 33.768948, as said below
- outer_right_root: float32 [512, 512], P(None, 'mp'), may hold values from -3.7565048 to 25.756505, as said below
Outputs:
- output_states: bfloat16 [32768, 512], P(('dp', 'mp'))
- states_grad: bfloat16 [32768, 512], P(('dp', 'mp'))
- grad_norm: float32 [], replicated
- attention_grad: float32 [4, 512, 512], P(None, 'dp', 'mp')
- inner_grad: float32 [512, 2048], P('dp', 'mp')
- outer_grad: float32 [2048, 512], P('dp', 'mp')
- norm_grad: float32 [2048], P(('dp', 'mp'))
- attention_new: float32 [4, 512, 512], P(None, 'dp', 'mp')
- inner_new: float32 [512, 2048], P('dp', 'mp')
- outer_new: float32 [2048, 512], P('dp', 'mp')
- norm_new: float32 [2048], P(('dp', 'mp'))
- attention_left_new: float32 [4, 512, 512], P(None, 'dp', 'mp')
- attention_right_new: float32 [4, 512, 512], P(None, 'dp', 'mp')
- inner_left_new: float32 [512, 512], P('dp', 'mp')
- inner_right_new: float32 [2048, 2048], P('dp', 'mp')
- outer_left_new: float32 [2048, 2048], P('dp', 'mp')
- outer_right_new: float32 [512, 512], P('dp', 'mp')
The draws below stay inside these ranges and needn't reach their ends.
Inputs may be any that keep to these rules, and one draw needn't show every extreme that they name: `lengths`: positions at or beyond a sequence's length are padding; every sequence has at least one real token. `attention_weights`: query, key and value projections, then the output projection. `attention_left`: symmetric. `attention_right`: symmetric. `inner_left`: symmetric. `inner_right`: symmetric. `outer_left`: symmetric. `outer_right`: symmetric. `attention_left_root`: symmetric. `attention_right_root`: symmetric. `inner_left_root`: symmetric. `inner_right_root`: symmetric. `outer_left_root`: symmetric. `outer_right_root`: symmetric.
All inputs are finite; a program needn't handle non-finite values. No bound on the sum of `halting` or of `lengths` on one device may be relied on, other than what follows from the above.
Results may differ from the reference program's by a relative error of at most 0.012.
The reference program's roundings to bfloat16 on the way count: a program that leaves them out, or rounds other values in their place, can miss the bound.
Values may be sent and summed in bfloat16 or wider, within the bound.
A program may use at most 192 MiB of HBM per device.

```python
import math
import jax
import jax.numpy as jnp
import numpy as np
from jax import lax

D = 512
HEADS = 8
DH = 64
FF = 2048
SEQ = 2048
SEQ_GRP = 2
SEQS = 16
TOKENS = 32768


def symmetric_noise(key, count, size):
    raw = jnp.clip(jax.random.normal(key, (count, size, size), jnp.float32), -6.0, 6.0)
    return (raw + jnp.swapaxes(raw, 1, 2)) * 0.70710678


def identity_stack(count, size):
    places = jnp.arange(size)
    square = (places[:, None] == places[None, :]).astype(jnp.float32)
    return jnp.broadcast_to(square, (count, size, size))


def grad_square():
    return 0.0001 / TOKENS


def statistic(key, count, size, other):
    level = other * grad_square()
    spread = math.sqrt(other) * grad_square()
    key_multiple, key_noise = jax.random.split(key)
    multiple = jax.random.uniform(key_multiple, (count, 1, 1), jnp.float32, 1.0, 4.0)
    return multiple * level * identity_stack(count, size) + spread * symmetric_noise(key_noise, count, size)


def inverse_root(key, count, size, other):
    level = (other * grad_square()) ** (-0.25)
    key_diagonal, key_noise = jax.random.split(key)
    diagonal = jax.random.uniform(key_diagonal, (count, size, 1), jnp.float32, 0.7, 1.1)
    noise = symmetric_noise(key_noise, count, size) * (0.5 / math.sqrt(size))
    return level * (identity_stack(count, size) * diagonal + noise)


def draw_attention_weights(key, part):
    key = jax.random.fold_in(key, 101)
    base = jnp.clip(jax.random.normal(key, (4, D, D), jnp.float32), -6.0, 6.0)
    in_scale = 1.0 / math.sqrt(D)
    out_scale = 1.0 / math.sqrt(max(D * 16 // SEQ, 1))
    member = jnp.arange(4)[:, None, None]
    return base * jnp.where(member == 3, out_scale, in_scale)


def draw_attention_left(key, part):
    return statistic(jax.random.fold_in(key, 211), 4, D, D)


def draw_attention_right(key, part):
    return statistic(jax.random.fold_in(key, 223), 4, D, D)


def draw_inner_left(key, part):
    return statistic(jax.random.fold_in(key, 227), 1, D, FF)[0]


def draw_inner_right(key, part):
    return statistic(jax.random.fold_in(key, 229), 1, FF, D)[0]


def draw_outer_left(key, part):
    return statistic(jax.random.fold_in(key, 233), 1, FF, D)[0]


def draw_outer_right(key, part):
    return statistic(jax.random.fold_in(key, 239), 1, D, FF)[0]


def draw_attention_left_root(key, part):
    return inverse_root(jax.random.fold_in(key, 307), 4, D, D)


def draw_attention_right_root(key, part):
    return inverse_root(jax.random.fold_in(key, 311), 4, D, D)


def draw_inner_left_root(key, part):
    return inverse_root(jax.random.fold_in(key, 313), 1, D, FF)[0]


def draw_inner_right_root(key, part):
    return inverse_root(jax.random.fold_in(key, 317), 1, FF, D)[0]


def draw_outer_left_root(key, part):
    return inverse_root(jax.random.fold_in(key, 331), 1, FF, D)[0]


def draw_outer_right_root(key, part):
    return inverse_root(jax.random.fold_in(key, 337), 1, D, FF)[0]


def with_ends(drawn, rng, smallest, largest):
    longest = drawn.shape.index(max(drawn.shape))
    spots = []
    for shift in (0, 1):
        where = [jax.random.randint(jax.random.fold_in(rng, axis), (), 0, length) for axis, length in enumerate(drawn.shape)]
        where[longest] = (where[longest] + shift) % drawn.shape[longest]
        spots.append(tuple(where))
    return drawn.at[spots[0]].set(smallest).at[spots[1]].set(largest)


def level_of(rng, extent, cuts, least, largest):
    loudness = 1.0
    for position, blocks in cuts:
        draws = jax.random.uniform(jax.random.fold_in(jax.random.fold_in(rng, 6), position), (blocks,), jnp.float32, least / len(cuts), largest / len(cuts))
        loudness = loudness * jnp.repeat(jnp.exp(draws), extent[position] // blocks).reshape((-1,) + (1,) * (len(extent) - 1 - position))
    return loudness


def length_profile(count, total, bound, slope):
    loads = [(1 << 20) // math.isqrt(grade ** slope) + 1 for grade in range(2, count + 1)]
    surplus, counts = total - bound - (count - 1), [1] * (count - 1)
    while surplus > 0:
        free = [i for i in range(count - 1) if counts[i] < bound]
        mass, remaining = sum([loads[i] for i in free]), surplus
        for i in free:
            extra = min(bound - counts[i], max(1, remaining * loads[i] // mass), surplus)
            counts[i] = counts[i] + extra
            surplus = surplus - extra
    return np.array([bound] + counts)


def uneven(stream_key, amount, total, limit, slope):
    if amount == 2:
        one = jax.random.randint(stream_key, (), max(1, total - limit), min(limit, total - 1) + 1)
        return jnp.stack([one, total - one])
    tallies = jnp.asarray(length_profile(amount, total, limit, slope), jnp.int32)
    couples = (amount - 1) // 2
    giver, taker = tallies[1:1 + 2 * couples:2], tallies[2:2 + 2 * couples:2]
    margin = jnp.minimum(giver - 1, limit - taker)
    moved = jax.random.randint(jax.random.fold_in(stream_key, 1), (couples,), 0, 1 << 20) % (margin + 1)
    tallies = tallies.at[1:1 + 2 * couples:2].set(giver - moved).at[2:2 + 2 * couples:2].set(taker + moved)
    return tallies[jax.random.permutation(jax.random.fold_in(stream_key, 2), amount)]


def centred(rng, dims, deviation, limit, cuts=(), kind=jnp.bfloat16):
    loudness = level_of(rng, dims, cuts, -0.22, 0.18) if cuts else 1.0
    values = jax.random.normal(rng, dims, jnp.float32) * deviation * loudness
    return jnp.minimum(jnp.maximum(values, -limit), limit).astype(kind)


def setup_inputs(seed: int = 0) -> dict:
    key_of = jax.random.split(jax.random.key(seed), 22)
    states = centred(key_of[0], (TOKENS, D), 1.0, 6.0, ((0, 32),))
    cotangent = centred(key_of[1], (TOKENS, D), 1.0, 6.0, ((0, 32),))
    halting = with_ends((jax.random.randint(key_of[2], (TOKENS,), 0, 4) < 3).astype(jnp.int32), jax.random.fold_in(key_of[2], 1), 0, 1)
    lengths = uneven(key_of[3], SEQS, SEQS * SEQ * 5 // 8, SEQ, 2).astype(jnp.int32)
    attention_weights = draw_attention_weights(jax.random.fold_in(key_of[21], 71), 0)
    inner_weight = centred(key_of[5], (D, FF), D ** -0.5, 0.25, ((0, 8), (1, 4)), jnp.float32)
    outer_weight = centred(key_of[6], (FF, D), FF ** -0.5, 0.125, ((0, 8), (1, 4)), jnp.float32)
    norm_gains = jnp.clip(1.0 + 0.1 * jax.random.normal(key_of[7], (2, D), jnp.float32), 0.5, 1.5)
    norm_biases = centred(key_of[8], (2, D), 0.3, 3.0, (), jnp.float32)
    attention_left = draw_attention_left(jax.random.fold_in(key_of[21], 71), 0)
    attention_right = draw_attention_right(jax.random.fold_in(key_of[21], 71), 0)
    inner_left = draw_inner_left(jax.random.fold_in(key_of[21], 71), 0)
    inner_right = draw_inner_right(jax.random.fold_in(key_of[21], 71), 0)
    outer_left = draw_outer_left(jax.random.fold_in(key_of[21], 71), 0)
    outer_right = draw_outer_right(jax.random.fold_in(key_of[21], 71), 0)
    attention_left_root = draw_attention_left_root(jax.random.fold_in(key_of[21], 71), 0)
    attention_right_root = draw_attention_right_root(jax.random.fold_in(key_of[21], 71), 0)
    inner_left_root = draw_inner_left_root(jax.random.fold_in(key_of[21], 71), 0)
    inner_right_root = draw_inner_right_root(jax.random.fold_in(key_of[21], 71), 0)
    outer_left_root = draw_outer_left_root(jax.random.fold_in(key_of[21], 71), 0)
    outer_right_root = draw_outer_right_root(jax.random.fold_in(key_of[21], 71), 0)
    return dict(states=states, cotangent=cotangent, halting=halting, lengths=lengths, attention_weights=attention_weights, inner_weight=inner_weight, outer_weight=outer_weight, norm_gains=norm_gains, norm_biases=norm_biases, attention_left=attention_left, attention_right=attention_right, inner_left=inner_left, inner_right=inner_right, outer_left=outer_left, outer_right=outer_right, attention_left_root=attention_left_root, attention_right_root=attention_right_root, inner_left_root=inner_left_root, inner_right_root=inner_right_root, outer_left_root=outer_left_root, outer_right_root=outer_right_root)


@jax.custom_vjp
def low(v):
    return lax.optimization_barrier(v.astype(jnp.bfloat16)).astype(jnp.float32)

@jax.custom_vjp
def low_back(v):
    return v

def low_keep(v):
    return (low(v), None)

def low_pass(kept, grad):
    return (grad,)

def back_keep(v):
    return (v, None)

def back_low(kept, grad):
    return (low(grad),)
low.defvjp(low_keep, low_pass)
low_back.defvjp(back_keep, back_low)
precise = lax.Precision.HIGHEST
epsilon = 1e-06
step_rate = 1.0

def smooth_unit(values):
    return jax.nn.gelu(values, approximate=True)

def layer_norm(residual, norm_gain, norm_bias):
    centered = residual - lax.optimization_barrier(jnp.mean(residual, axis=-1, keepdims=True))
    variance = lax.optimization_barrier(jnp.mean(centered * centered, axis=-1, keepdims=True))
    return centered * lax.rsqrt(variance + epsilon) * norm_gain + norm_bias

def attend_block(query_block, keys_all, values_all, key_valid):
    scores = jnp.einsum('sqhd,skhd->shqk', query_block, keys_all, precision=precise) * DH ** (-0.5)
    scores = low_back(scores)
    scores = jnp.where(key_valid[:, None, None, :], scores, -1e+30)
    softmax_out = low(jax.nn.softmax(scores, axis=-1))
    return jnp.einsum('shqk,skhd->sqhd', softmax_out, values_all, precision=precise)

def attention(queries, keys_all, values_all, key_valid):
    block_rows = min(512, SEQ)
    offsets = jnp.arange(SEQ // block_rows, dtype=jnp.int32) * block_rows

    def visit_block(offset):
        query_block = lax.dynamic_slice_in_dim(queries, offset, block_rows, 1)
        return attend_block(query_block, keys_all, values_all, key_valid)
    results = lax.map(jax.checkpoint(visit_block), offsets)
    return jnp.moveaxis(results, 0, 1).reshape(queries.shape)

def forward(hidden, attention_weights, inner_weight, outer_weight, norm_gains, norm_biases, halt_group, length_group):
    group_rows = hidden.shape[0]
    attention_low = low(attention_weights)
    inner_low = low(inner_weight)
    outer_low = low(outer_weight)

    def project(matrix):
        product = jnp.dot(hidden, matrix, precision=precise)
        return low_back(low(product)).reshape(SEQ_GRP, SEQ, HEADS, DH)
    queries = project(attention_low[0])
    keys_all = project(attention_low[1])
    values_all = project(attention_low[2])
    positions = jnp.arange(SEQ, dtype=jnp.int32)
    key_valid = positions[None, :] < length_group[:, None]
    mixed = attention(queries, keys_all, values_all, key_valid).reshape(group_rows, D)
    mixed = low_back(low(mixed))
    attended = low_back(jnp.dot(mixed, attention_low[3], precision=precise))
    normed = layer_norm(hidden + attended, norm_gains[0], norm_biases[0])
    inner = low_back(jnp.dot(low(normed), inner_low, precision=precise))
    activated = low(smooth_unit(inner))
    branch = low_back(jnp.dot(activated, outer_low, precision=precise))
    final = layer_norm(normed + branch, norm_gains[1], norm_biases[1])
    return jnp.where(halt_group[:, None] == 1, final, hidden)

def shampoo(weight, gradient, left_stat, right_stat, left_root, right_root):
    left_new = 0.5 * left_stat + 0.5 * jnp.dot(gradient, gradient.T, precision=precise)
    right_new = 0.5 * right_stat + 0.5 * jnp.dot(gradient.T, gradient, precision=precise)
    update = jnp.dot(jnp.dot(left_root, gradient, precision=precise), right_root, precision=precise)
    return (weight - step_rate * update, left_new, right_new)

def reference(states, cotangent, halting, lengths, attention_weights, inner_weight, outer_weight, norm_gains, norm_biases, attention_left, attention_right, inner_left, inner_right, outer_left, outer_right, attention_left_root, attention_right_root, inner_left_root, inner_right_root, outer_left_root, outer_right_root):
    group_rows = SEQ_GRP * SEQ
    group_count = states.shape[0] // group_rows
    hidden_all = states.astype(jnp.float32).reshape(group_count, group_rows, D)
    upstream_all = cotangent.astype(jnp.float32).reshape(group_count, group_rows, D)
    halt_all = halting.reshape(group_count, group_rows)
    length_all = lengths.reshape(group_count, SEQ_GRP)
    zeros_start = (jnp.zeros_like(attention_weights), jnp.zeros_like(inner_weight), jnp.zeros_like(outer_weight), jnp.zeros_like(norm_gains), jnp.zeros_like(norm_biases))

    def visit_group(running, items):
        hidden, upstream, halt_group, length_group = items

        def local_forward(hidden_in, attention_in, inner_in, outer_in, gains_in, biases_in):
            return forward(hidden_in, attention_in, inner_in, outer_in, gains_in, biases_in, halt_group, length_group)
        result, pullback = jax.vjp(local_forward, hidden, attention_weights, inner_weight, outer_weight, norm_gains, norm_biases)
        gradients = pullback(upstream)
        running = tuple((summed + portion for summed, portion in zip(running, gradients[1:])))
        return (running, (result.astype(jnp.bfloat16), gradients[0].astype(jnp.bfloat16)))
    totals, (output_rows, grad_rows) = lax.scan(visit_group, zeros_start, (hidden_all, upstream_all, halt_all, length_all))
    inv_tokens = 1.0 / TOKENS
    grad_attention, grad_inner, grad_outer, grad_gains, grad_biases = tuple((item * inv_tokens for item in totals))
    output_states = output_rows.reshape(states.shape)
    states_grad = grad_rows.reshape(states.shape)
    norm_raw = jnp.concatenate([grad_gains.reshape(-1), grad_biases.reshape(-1)])
    squares = jnp.sum(grad_attention * grad_attention) + jnp.sum(grad_inner * grad_inner) + jnp.sum(grad_outer * grad_outer) + jnp.sum(norm_raw * norm_raw)
    grad_norm = jnp.sqrt(squares)
    clip_limit = 0.01 * math.sqrt((4 * D * D + 2 * D * FF + 4 * D) / TOKENS)
    factor = jnp.minimum(1.0, clip_limit / grad_norm)
    attention_grad = grad_attention * factor
    inner_grad = grad_inner * factor
    outer_grad = grad_outer * factor
    norm_grad = norm_raw * factor
    new_list = []
    left_list = []
    right_list = []
    for member in range(4):
        weight_new, left_new, right_new = shampoo(attention_weights[member], attention_grad[member], attention_left[member], attention_right[member], attention_left_root[member], attention_right_root[member])
        new_list.append(weight_new)
        left_list.append(left_new)
        right_list.append(right_new)
    attention_new = jnp.stack(new_list)
    attention_left_new = jnp.stack(left_list)
    attention_right_new = jnp.stack(right_list)
    inner_new, inner_left_new, inner_right_new = shampoo(inner_weight, inner_grad, inner_left, inner_right, inner_left_root, inner_right_root)
    outer_new, outer_left_new, outer_right_new = shampoo(outer_weight, outer_grad, outer_left, outer_right, outer_left_root, outer_right_root)
    flat_params = jnp.concatenate([norm_gains.reshape(-1), norm_biases.reshape(-1)])
    norm_new = flat_params - 20.0 * math.sqrt(TOKENS) * norm_grad
    return (output_states, states_grad, grad_norm, attention_grad, inner_grad, outer_grad, norm_grad, attention_new, inner_new, outer_new, norm_new, attention_left_new, attention_right_new, inner_left_new, inner_right_new, outer_left_new, outer_right_new)
```

```python
import functools
import math

import jax
import jax.numpy as jnp
from jax import lax
from jax.experimental import pallas as pl
from jax.experimental.pallas import tpu as pltpu
from jax.sharding import PartitionSpec as P

D = 512
HEADS = 8
DH = 64
FF = 2048
SEQ = 2048
SEQ_GRP = 2
PAIR = 2 * DH
QUERY_ROWS = 256
KEY_ROWS = 256
TOKEN_ROWS = 256

F32 = jnp.float32
BF16 = jnp.bfloat16
epsilon = 1e-06
step_rate = 1.0
NN = (((1,), (0,)), ((), ()))
NT = (((1,), (1,)), ((), ()))
TN = (((0,), (0,)), ((), ()))
VMEM_LIMIT = 56 * 1024 * 1024


def mm(left, right, dims=NN):
    return lax.dot_general(left, right, dims, preferred_element_type=F32)


def split2(value):
    high = value.astype(BF16)
    return high, (value - high.astype(F32)).astype(BF16)


def split3(value):
    high = value.astype(BF16).astype(F32)
    rest = value - high
    middle = rest.astype(BF16).astype(F32)
    return high, middle, rest - middle


MESH = pl.DeviceIdType.MESH


class Place:
    def __init__(self, far_count):
        data_rank = lax.axis_index("dp")
        self.far_count = far_count
        self.model = lax.axis_index("mp")
        self.far, self.near = data_rank // 2, data_rank % 2
        side, core = self.model // 2, self.model % 2
        self.beside = 2 * (1 - side) + core
        self.twin = 2 * side + 1 - core
        self.twin_beside = 2 * (1 - side) + 1 - core
        self.to_beside = {"mp": self.beside}
        self.to_twin = {"mp": self.twin}
        self.to_near = {"dp": 2 * self.far + 1 - self.near}

    def other_far(self, step):
        return (self.far + step) % self.far_count

    def to_far(self, step):
        return {"dp": 2 * self.other_far(step) + self.near}

    def meet(self, far=True, near=True, beside=True, twin=True):
        barrier = pltpu.get_barrier_semaphore()
        partners = [self.to_far(step) for step in range(1, self.far_count)] if far else []
        partners += [self.to_near] * near + [self.to_beside] * beside + [self.to_twin] * twin
        for partner in partners:
            pl.semaphore_signal(barrier, inc=1, device_id=partner, device_id_type=MESH)
        pl.semaphore_wait(barrier, len(partners))


class Wires:
    def __init__(self, send_sems, recv_sems):
        self.sems = (send_sems, recv_sems)
        self.used = 0

    def copy(self, source, target, partner):
        index = self.used
        self.used += 1
        return pltpu.make_async_remote_copy(
            src_ref=source,
            dst_ref=target,
            send_sem=self.sems[0].at[index],
            recv_sem=self.sems[1].at[index],
            device_id=partner,
            device_id_type=MESH,
        )


def start_all(copies):
    for copy in copies:
        copy.start()


def wait_all(copies):
    for copy in copies:
        copy.wait()


def columns(index, size):
    return pl.ds(pl.multiple_of(index * size, size), size)


def gather_stages(wires, place, shard, full, near_first):
    size = shard.shape[-1]

    def block(index):
        return columns(index, size)

    mine, side = block(place.model), block(place.beside)

    def pair(near, cols, partner):
        view = full.at[:, near, :, cols]
        return wires.copy(view, view, partner)

    def slab(cols, partner):
        view = full.at[:, :, :, cols]
        return wires.copy(view, view, partner)

    home = full.at[place.far, place.near, :, mine]
    stages = [[wires.copy(shard, home, place.to_far(step)) for step in range(1, place.far_count)]]
    if near_first:
        stages.append([pair(place.near, mine, place.to_near)])
        stages.append([slab(mine, place.to_beside)])
    else:
        stages.append([pair(place.near, mine, place.to_beside)])
        stages.append([pair(place.near, mine, place.to_near), pair(place.near, side, place.to_near)])
    stages.append([slab(mine, place.to_twin), slab(side, place.to_twin)])
    return home, stages


def gather_copies(far_count):
    return far_count - 1 + 5


REDUCE_BUFFERS = 8


def reduce_copies(far_count):
    return far_count - 1 + 6


def reduce_scratch(far_count, rows, cols):
    return [
        pltpu.VMEM((2, 2, far_count, rows, cols), F32),
        pltpu.VMEM((2, 2, far_count, rows, cols), BF16),
    ] + [
        pltpu.VMEM(shape, BF16)
        for shape in ((2, far_count, rows, cols), (far_count, rows, cols), (far_count, rows, cols))
        for _ in range(2)
    ]


class Reducer:
    def __init__(self, wires, place, partial, low, buffers, load_sems, near_first):
        acc, got, out1, in1, out2, in2, out3, in3 = buffers
        self.place, self.near_first = place, near_first
        self.acc, self.got = acc, got
        self.out, self.arrived = (out1, out2, out3), (in1, in2, in3)
        size = acc.shape[-1]
        kept = (place.model, place.beside)
        given = (place.twin, place.twin_beside)
        self.load = []
        first = []
        for slot in range(2):
            for near in range(2):
                self.load.append(
                    pltpu.make_async_copy(
                        partial.at[:, near, :, columns(kept[slot], size)],
                        acc.at[slot, near],
                        load_sems.at[2 * slot + near],
                    )
                )
                first.append(
                    wires.copy(low.at[:, near, :, columns(given[slot], size)], got.at[slot, near], place.to_twin)
                )
        order = (place.to_near, place.to_beside) if near_first else (place.to_beside, place.to_near)
        self.copies = [first, [wires.copy(out1, in1, order[0])], [wires.copy(out2, in2, order[1])]]
        self.copies.append(
            [
                wires.copy(out3.at[place.other_far(step)], in3.at[step], place.to_far(step))
                for step in range(1, place.far_count)
            ]
        )

    def begin(self):
        start_all(self.load + self.copies[0])

    def advance(self, number):
        place, acc = self.place, self.acc
        near, away = place.near, 1 - place.near
        fars = range(place.far_count)
        wait_all(self.copies[number])
        if number == 0:
            wait_all(self.load)
            for slot in range(2):
                for side in range(2):
                    for far in fars:
                        acc[slot, side, far] += self.got[slot, side, far].astype(F32)
            for part in range(2):
                for far in fars:
                    value = acc[part, away, far] if self.near_first else acc[1, part, far]
                    self.out[0][part, far] = value.astype(BF16)
        elif number == 1:
            for part in range(2):
                for far in fars:
                    if self.near_first:
                        acc[part, near, far] += self.arrived[0][part, far].astype(F32)
                    else:
                        acc[0, part, far] += self.arrived[0][part, far].astype(F32)
            for far in fars:
                value = acc[1, near, far] if self.near_first else acc[0, away, far]
                self.out[1][far] = value.astype(BF16)
        else:
            for far in fars:
                value = acc[0, near, far] + self.arrived[1][far].astype(F32)
                acc[0, near, far] = value
                self.out[2][far] = value.astype(BF16)
        start_all(self.copies[number + 1])

    def finish(self):
        wait_all(self.copies[3])
        total = self.acc[0, self.place.near, self.place.far]
        for step in range(1, self.place.far_count):
            total = total + self.arrived[2][step].astype(F32)
        return total


class Spread:
    def __init__(self, wires, place, tile, stages, slots, far_last):
        self.place, self.tile, self.stages, self.slots = place, tile, stages, slots
        far = [
            wires.copy(tile, slots.at[place.far], place.to_far(step)) for step in range(1, place.far_count)
        ]
        pairs = [
            [wires.copy(tile, stages.at[number], partner)]
            for number, partner in enumerate((place.to_twin, place.to_beside, place.to_near))
        ]
        self.copies = pairs + [far] if far_last else [far] + pairs[::-1]
        self.kinds = [0, 1, 2, 3] if far_last else [3, 2, 1, 0]

    def begin(self):
        start_all(self.copies[0])

    def advance(self, number):
        wait_all(self.copies[number])
        kind = self.kinds[number]
        if kind == 3:
            self.slots[self.place.far] = self.tile[...]
            total = self.slots[0]
            for far in range(1, self.place.far_count):
                total = total + self.slots[far]
            self.tile[...] = total
        else:
            self.tile[...] += self.stages[kind]
        if number < 3:
            start_all(self.copies[number + 1])


def spread_copies(far_count):
    return far_count - 1 + 3


def spread_scratch(far_count, shape):
    return [pltpu.VMEM(shape, F32), pltpu.VMEM((3,) + shape, F32), pltpu.VMEM((far_count,) + shape, F32)]


def any_spec():
    return pl.BlockSpec(memory_space=pl.ANY)


def vmem_spec():
    return pl.BlockSpec(memory_space=pltpu.VMEM)


def project_kernel(
    far_count,
    states_ref,
    states_any,
    weights_ref,
    weights_out,
    queries_ref,
    keys_any,
    values_any,
    twin_states,
    shard,
    full,
    own,
    send_sems,
    recv_sems,
    local_sems,
):
    place = Place(far_count)
    wires = Wires(send_sems, recv_sems)
    members = shard.shape[0]
    rows = states_ref.shape[0]
    plans = [
        gather_stages(wires, place, shard.at[member], full.at[member], near_first=member < 2)
        for member in range(members)
    ]
    shard[...] = weights_ref[...].astype(BF16)
    place.meet()
    fill = [
        pltpu.make_async_copy(shard.at[member], plans[member][0], local_sems.at[member]) for member in range(members)
    ]
    start_all(fill)
    for number in range(4):
        for _, stages in plans:
            start_all(stages[number])
        if number == 0:
            swap_states = wires.copy(states_any, twin_states, place.to_twin)
            swap_states.start()
            wait_all(fill)
        for _, stages in plans:
            wait_all(stages[number])
    outward = pltpu.make_async_copy(full, weights_out, local_sems.at[0])
    outward.start()
    swaps = []
    for number, target in ((1, keys_any), (2, values_any)):
        weight = full[number].reshape(D, D)
        own[number - 1] = mm(states_ref[...], weight).astype(BF16)
        local = pltpu.make_async_copy(own.at[number - 1], target.at[pl.ds(0, rows)], local_sems.at[number])
        local.start()
        swap = wires.copy(own.at[number - 1], target.at[pl.ds(rows, rows)], place.to_twin)
        swap.start()
        swaps += [local, swap]
    weight = full[0].reshape(D, D)
    queries_ref[...] = (mm(states_ref[...], weight).astype(BF16) * DH ** (-0.5)).astype(BF16)
    wait_all(swaps + [swap_states, outward])


def project(states, attention_weights, far_count):
    rows = states.shape[0]
    members = 3
    shard_rows, shard_cols = attention_weights.shape[1:]
    copies = members * gather_copies(far_count) + 3
    return pl.pallas_call(
        functools.partial(project_kernel, far_count),
        name="project",
        in_specs=[vmem_spec(), any_spec(), vmem_spec()],
        out_specs=[any_spec(), vmem_spec(), any_spec(), any_spec(), any_spec()],
        out_shape=[
            jax.ShapeDtypeStruct((members, far_count, 2, shard_rows, D), BF16),
            jax.ShapeDtypeStruct((rows, D), BF16),
            jax.ShapeDtypeStruct((2 * rows, D), BF16),
            jax.ShapeDtypeStruct((2 * rows, D), BF16),
            jax.ShapeDtypeStruct((rows, D), BF16),
        ],
        scratch_shapes=[
            pltpu.VMEM((members, shard_rows, shard_cols), BF16),
            pltpu.VMEM((members, far_count, 2, shard_rows, D), BF16),
            pltpu.VMEM((2, rows, D), BF16),
            pltpu.SemaphoreType.DMA((copies,)),
            pltpu.SemaphoreType.DMA((copies,)),
            pltpu.SemaphoreType.DMA((3,)),
        ],
        compiler_params=pltpu.CompilerParams(
            vmem_limit_bytes=VMEM_LIMIT, collective_id=0, has_side_effects=True
        ),
    )(states, states, attention_weights[:members])


def own_lanes(parity):
    lane = lax.broadcasted_iota(jnp.int32, (1, PAIR), 1)
    return (lane < DH) if parity == 0 else (lane >= DH)


def lane_in_half():
    return lax.broadcasted_iota(jnp.int32, (1, PAIR), 1) % DH


def blend(parity, own, extra):
    return jnp.where(own_lanes(parity), own.astype(F32), extra.astype(F32)).astype(BF16)


def attention_forward_kernel(
    far_count,
    q_ref,
    k_ref,
    v_ref,
    kx_ref,
    inner_shard,
    outer_shard,
    wo_shard,
    mixed_ref,
    qx_ref,
    inner_full,
    outer_full,
    wo_full,
    ka,
    va,
    score_a,
    score_b,
    send_sems,
    recv_sems,
    local_sems,
):
    rows = q_ref.shape[0]
    step = pl.program_id(0)
    place_here = Place(far_count)
    wires = Wires(send_sems, recv_sems)
    shards = (inner_shard, outer_shard, wo_shard)
    plans = [
        gather_stages(wires, place_here, shard, full, near_first)
        for shard, full, near_first in zip(shards, (inner_full, outer_full, wo_full), (True, False, True))
    ]
    fill = [
        pltpu.make_async_copy(shard, home, local_sems.at[number])
        for number, (shard, (home, _)) in enumerate(zip(shards, plans))
    ]

    def stage(number):
        return [copy for _, stages in plans for copy in stages[number]]

    def at(place_step, place_index, index, wait, start):
        if index != place_index:
            return

        @pl.when(step == place_step)
        def _():
            if wait is not None:
                wait_all(stage(wait))
            if start is not None:
                start_all(stage(start))

    @pl.when(step == 0)
    def _():
        place_here.meet()
        start_all(fill + stage(0))
        wait_all(fill)

    place = lane_in_half()
    first = jnp.where(place == 0, 1.0, 0.0)
    ones = jnp.where(place <= 3, 1.0, 0.0)
    for parity in range(2):
        ka[parity] = blend(parity, k_ref[...], kx_ref[...])
        va[parity] = blend(parity, v_ref[...], ones)
    steps = [(parity, block) for block in range(rows // QUERY_ROWS) for parity in range(2)]
    scratch = (score_a, score_b)

    def score(index):
        parity, block = steps[index]
        queries = blend(parity, q_ref[pl.ds(block * QUERY_ROWS, QUERY_ROWS), :], first)
        scratch[index % 2][...] = mm(ka[parity], queries, NT)

    score(0)
    held = [None, None]
    logs = [None, None]
    row = lax.broadcasted_iota(jnp.int32, (PAIR, 1), 0)
    for index, (parity, block) in enumerate(steps):
        at(1, 4, index, 0, 1)
        at(2, 2, index, 1, 2)
        at(3, 5, index, 2, 3)
        if index + 1 < len(steps):
            score(index + 1)
        scores = scratch[index % 2][...]
        row_max = jnp.max(scores, axis=0, keepdims=True)
        shifted = jnp.exp(scores - row_max).astype(BF16)
        product = mm(va[parity], shifted, TN)
        sum_row = DH if parity == 0 else 0
        total = product[sum_row : sum_row + 1, :]
        held[parity] = product / total
        logs[parity] = row_max + jnp.log(total)
        if parity == 1:
            window = pl.ds(block * QUERY_ROWS, QUERY_ROWS)
            both = jnp.concatenate([held[0][:DH], held[1][DH:]], axis=0)
            mixed_ref[window, :] = both.T
            parts = split3(-jnp.where(row < DH, logs[1], logs[0]))
            spot = row % DH
            extra = jnp.where(spot == 0, 1.0, 0.0)
            for number, part in enumerate(parts):
                extra = jnp.where(spot == number + 1, part, extra)
            qx_ref[window, :] = extra.T.astype(BF16)
    at(3, 8, 8, 3, None)


def attention_forward(queries, keys, values, key_extra, inner_shard, outer_shard, wo_shard, far_count):
    rows, width = queries.shape
    total = keys.shape[0]
    by_query = pl.BlockSpec((rows, PAIR), lambda j: (0, j))
    by_key = pl.BlockSpec((total, PAIR), lambda j: (0, j))
    whole = pl.BlockSpec((total, PAIR), lambda j: (0, 0))
    shards = (inner_shard, outer_shard, wo_shard)
    fulls = [
        jax.ShapeDtypeStruct((far_count, 2, shard.shape[0], full_cols), BF16)
        for shard, full_cols in zip(shards, (FF, D, D))
    ]
    copies = 3 * gather_copies(far_count)
    outs = pl.pallas_call(
        functools.partial(attention_forward_kernel, far_count),
        name="attention_forward",
        grid=(width // PAIR,),
        in_specs=[by_query, by_key, by_key, whole] + [any_spec()] * 3,
        out_specs=[by_query, by_query] + [any_spec()] * 3,
        out_shape=[
            jax.ShapeDtypeStruct((rows, width), F32),
            jax.ShapeDtypeStruct((rows, width), BF16),
        ]
        + fulls,
        scratch_shapes=[
            pltpu.VMEM((2, total, PAIR), BF16),
            pltpu.VMEM((2, total, PAIR), BF16),
            pltpu.VMEM((total, QUERY_ROWS), F32),
            pltpu.VMEM((total, QUERY_ROWS), F32),
            pltpu.SemaphoreType.DMA((copies,)),
            pltpu.SemaphoreType.DMA((copies,)),
            pltpu.SemaphoreType.DMA((3,)),
        ],
        compiler_params=pltpu.CompilerParams(
            vmem_limit_bytes=VMEM_LIMIT, collective_id=1, has_side_effects=True
        ),
    )(queries, keys, values, key_extra, *shards)
    return outs[0], outs[1], outs[2].reshape(D, FF), outs[3].reshape(FF, D), outs[4].reshape(D, D)


def attention_backward_kernel(
    far_count,
    inv_tokens,
    q_ref,
    qx_ref,
    k_ref,
    v_ref,
    kx_ref,
    do_ref,
    dox_ref,
    own_states,
    twin_states,
    inner_raw,
    outer_raw,
    wo_raw,
    inner_low,
    outer_low,
    wo_low,
    norm_raw,
    dq_ref,
    dk_ref,
    dv_ref,
    dw_ref,
    dw_low,
    inner_piece,
    outer_piece,
    wo_piece,
    norm_total,
    qa,
    da,
    ka,
    va,
    dqt,
    *rest,
):
    step = pl.program_id(0)
    rows = q_ref.shape[0]
    total = k_ref.shape[0]
    place_here = Place(far_count)
    buffers, rest = rest[: 3 * REDUCE_BUFFERS], rest[3 * REDUCE_BUFFERS :]
    tile, tile_stages, tile_slots, send_sems, recv_sems, load_sems = rest
    wires = Wires(send_sems, recv_sems)
    partials = (inner_raw, outer_raw, wo_raw)
    lows = (inner_low, outer_low, wo_low)
    reducers = [
        Reducer(
            wires,
            place_here,
            partials[number],
            lows[number],
            buffers[number * REDUCE_BUFFERS : (number + 1) * REDUCE_BUFFERS],
            load_sems.at[number],
            near_first=number == 1,
        )
        for number in range(3)
    ]
    spread = Spread(wires, place_here, tile, tile_stages, tile_slots, far_last=True)

    def at(here, index, number):
        if index != here[1]:
            return

        @pl.when(step == here[0])
        def _():
            for reducer in reducers:
                reducer.advance(number)
            spread.advance(number)

    @pl.when(step == 0)
    def _():
        place_here.meet()
        tile[...] = norm_raw[...]
        for reducer in reducers:
            reducer.begin()
        spread.begin()

    place = lane_in_half()
    ones = jnp.where(place <= 3, 1.0, 0.0)
    for parity in range(2):
        ka[parity] = blend(parity, k_ref[...], kx_ref[...])
        va[parity] = blend(parity, v_ref[...], ones)
        qa[parity] = blend(parity, q_ref[...], qx_ref[...])
        da[parity] = blend(parity, do_ref[...], dox_ref[...])
    dqt[...] = jnp.zeros_like(dqt)
    pair_cols = columns(step, PAIR)
    for block in range(total // KEY_ROWS):
        at((0, 5), block, 0)
        at((2, 0), block, 1)
        at((2, 6), block, 2)
        window = pl.ds(block * KEY_ROWS, KEY_ROWS)
        key_grads = []
        value_grads = []
        for parity in range(2):
            key_block = ka[parity, window, :]
            probs = jnp.exp(mm(key_block, qa[parity], NT))
            d_probs = mm(va[parity, window, :], da[parity], NT)
            d_scores = (probs * d_probs).astype(BF16)
            value_grads.append(mm(probs.astype(BF16), da[parity]))
            key_grads.append(mm(d_scores, qa[parity]))
            dqt[parity] += mm(key_block, d_scores, TN)
        dk_ref[window, pair_cols] = jnp.where(own_lanes(0), key_grads[0], key_grads[1]).astype(BF16)
        dv_ref[window, pair_cols] = jnp.where(own_lanes(0), value_grads[0], value_grads[1]).astype(BF16)
    both = jnp.concatenate([dqt[0, :DH], dqt[1, DH:]], axis=0) * DH ** (-0.5)
    dq_ref[:, pair_cols] = both.T.astype(BF16)

    @pl.when(step == pl.num_programs(0) - 1)
    def _():
        own, twin = own_states[...], twin_states[...]
        for number, grad in enumerate((dq_ref, dk_ref, dv_ref)):
            product = mm(own, grad[:rows, :], TN)
            if number:
                product = product + mm(twin, grad[rows:, :], TN)
            dw_ref[number] = product
            dw_low[number] = product.astype(BF16)
        for reducer, piece in zip(reducers, (inner_piece, outer_piece, wo_piece)):
            piece[...] = reducer.finish() * inv_tokens
        spread.advance(3)
        norm_total[...] = tile[...] * inv_tokens


def attention_backward(
    queries, query_extra, keys, values, key_extra, d_mixed, d_extra, states, twin_states, raws, lows, norm_rows, counts
):
    rows, width = queries.shape
    total = keys.shape[0]
    data_count, model_count = counts
    far_count = data_count // 2
    by_query = pl.BlockSpec((rows, PAIR), lambda j: (0, j))
    by_key = pl.BlockSpec((total, PAIR), lambda j: (0, j))

    def whole(shape):
        return pl.BlockSpec(shape, lambda j: (0,) * len(shape))

    def seen(array):
        return array.reshape(far_count, 2, array.shape[0] // data_count, array.shape[1])

    pieces = [(raw.shape[0] // data_count, raw.shape[1] // model_count) for raw in raws]
    copies = 3 * reduce_copies(far_count) + spread_copies(far_count)
    out_shape = [
        jax.ShapeDtypeStruct((rows, width), BF16),
        jax.ShapeDtypeStruct((total, width), BF16),
        jax.ShapeDtypeStruct((total, width), BF16),
        jax.ShapeDtypeStruct((3, width, width), F32),
        jax.ShapeDtypeStruct((3, width, width), BF16),
    ]
    out_shape += [jax.ShapeDtypeStruct(piece, F32) for piece in pieces]
    out_shape.append(jax.ShapeDtypeStruct(norm_rows.shape, F32))
    scratch = [
        pltpu.VMEM((2, rows, PAIR), BF16),
        pltpu.VMEM((2, rows, PAIR), BF16),
        pltpu.VMEM((2, total, PAIR), BF16),
        pltpu.VMEM((2, total, PAIR), BF16),
        pltpu.VMEM((2, PAIR, rows), F32),
    ]
    for piece in pieces:
        scratch += reduce_scratch(far_count, *piece)
    scratch += spread_scratch(far_count, norm_rows.shape)
    scratch += [
        pltpu.SemaphoreType.DMA((copies,)),
        pltpu.SemaphoreType.DMA((copies,)),
        pltpu.SemaphoreType.DMA((3, 4)),
    ]
    return pl.pallas_call(
        functools.partial(attention_backward_kernel, far_count, 1.0 / (rows * data_count * model_count)),
        name="attention_backward",
        grid=(width // PAIR,),
        in_specs=[by_query, by_query, by_key, by_key, whole((total, PAIR)), by_query, by_query]
        + [whole((rows, width))] * 2
        + [any_spec()] * 6
        + [whole(norm_rows.shape)],
        out_specs=[whole(item.shape) for item in out_shape],
        out_shape=out_shape,
        scratch_shapes=scratch,
        compiler_params=pltpu.CompilerParams(
            vmem_limit_bytes=VMEM_LIMIT, collective_id=2, has_side_effects=True
        ),
    )(
        queries,
        query_extra,
        keys,
        values,
        key_extra,
        d_mixed,
        d_extra,
        states,
        twin_states,
        *[seen(raw) for raw in raws],
        *[seen(low) for low in lows],
        norm_rows,
    )


def root_products(grad, left_root, right_root, data_rank, counts, model_rank, left_out, right_out, update_out, room):
    data_count, model_count = counts
    far_count, _, shard_rows, width = grad.shape
    height = data_count * shard_rows
    part = far_count // model_count
    rows_here = grad[data_rank // 2, data_rank % 2]
    rows_there = grad[pl.ds(model_rank * part, part)].reshape(height // model_count, width)
    left_out[...] = mm(rows_here, rows_there, NT)
    size = width // model_count
    share = width // data_count
    whole = grad[...].reshape(height, width)
    cols_there = grad[:, :, :, columns(model_rank, size)].reshape(height, size)
    if share % 128 == 0:
        cols_here = grad[:, :, :, columns(data_rank, share)].reshape(height, share)
        right_out[...] = mm(cols_here, cols_there, TN)
    else:
        group = data_count // model_count
        cols_here = grad[:, :, :, columns(data_rank // group, size)].reshape(height, size)
        room[:size, :size] = mm(cols_here, cols_there, TN)
        right_out[...] = room[pl.ds(pl.multiple_of((data_rank % group) * share, share), share), :size]
    high, low = split2(left_root)
    once = mm(high, whole) + mm(low, whole)
    once_high, once_low = split2(once)
    root_high, root_low = split2(right_root)
    update_out[...] = mm(once_high, root_high) + mm(once_high, root_low) + mm(once_low, root_high)


def update_kernel(
    far_count,
    counts,
    inv_tokens,
    inner_piece,
    outer_piece,
    wo_piece,
    dw_any,
    dw_low_any,
    dq_ref,
    dk_ref,
    dv_ref,
    weights_ref,
    skip_ref,
    *rest,
):
    roots_any, rest = rest[:6], rest[6:]
    (
        late_out,
        squares_out,
        own_out,
        twin_in,
        attention_left_out,
        attention_right_out,
        attention_update_out,
        inner_left_out,
        inner_right_out,
        inner_update_out,
        outer_left_out,
        outer_right_out,
        outer_update_out,
    ), rest = rest[:13], rest[13:]
    buffers, rest = rest[: 3 * REDUCE_BUFFERS], rest[3 * REDUCE_BUFFERS :]
    roots, rest = rest[:6], rest[6:]
    (
        attention_shard,
        inner_shard,
        outer_shard,
        attention_full,
        inner_full,
        outer_full,
        room,
        twin_out,
        tile,
        tile_stages,
        tile_slots,
        send_sems,
        recv_sems,
        load_sems,
        local_sems,
    ) = rest
    place = Place(far_count)
    wires = Wires(send_sems, recv_sems)
    rows = dq_ref.shape[0]
    data_rank = 2 * place.far + place.near
    reducers = [
        Reducer(
            wires,
            place,
            dw_any.at[member],
            dw_low_any.at[member],
            buffers[member * REDUCE_BUFFERS : (member + 1) * REDUCE_BUFFERS],
            load_sems.at[member],
            near_first=member == 2,
        )
        for member in range(3)
    ]
    early = [
        gather_stages(wires, place, inner_shard, inner_full, True),
        gather_stages(wires, place, outer_shard, outer_full, False),
        gather_stages(wires, place, attention_shard.at[3], attention_full.at[3], True),
    ]
    late = [
        gather_stages(wires, place, attention_shard.at[member], attention_full.at[member], member < 2)
        for member in range(3)
    ]
    squares = Spread(wires, place, tile, tile_stages, tile_slots, far_last=False)
    swap = wires.copy(twin_out, twin_in, place.to_twin)
    fetch = [
        pltpu.make_async_copy(source, target, local_sems.at[number])
        for number, (source, target) in enumerate(zip(roots_any, roots))
    ]

    def stage(plans, number):
        return [copy for _, stages in plans for copy in stages[number]]

    inner_shard[...] = inner_piece[...].astype(BF16)
    outer_shard[...] = outer_piece[...].astype(BF16)
    attention_shard[3] = wo_piece[...].astype(BF16)
    place.meet()
    for reducer in reducers:
        reducer.begin()
    start_all(stage(early, 0))
    start_all(fetch)
    mine = (place.far, place.near, slice(None), columns(place.model, inner_shard.shape[-1]))
    inner_full[mine] = inner_shard[...]
    mine = mine[:3] + (columns(place.model, outer_shard.shape[-1]),)
    outer_full[mine] = outer_shard[...]
    attention_full[(3,) + mine] = attention_shard[3]
    twin_out[...] = (
        mm(dk_ref[rows:, :], weights_ref[1], NT) + mm(dv_ref[rows:, :], weights_ref[2], NT)
    ).astype(BF16)
    swap.start()
    for reducer in reducers:
        reducer.advance(0)
    own_out[...] = (
        skip_ref[...]
        + mm(dq_ref[...], weights_ref[0], NT)
        + mm(dk_ref[:rows, :], weights_ref[1], NT)
        + mm(dv_ref[:rows, :], weights_ref[2], NT)
    )
    for reducer in reducers:
        reducer.advance(1)
    wait_all(stage(early, 0))
    start_all(stage(early, 1))
    for reducer in reducers:
        reducer.advance(2)
    wait_all(stage(early, 1))
    start_all(stage(early, 2))

    def square(piece):
        return jnp.sum(jnp.sum(piece * piece, axis=0, keepdims=True), axis=1, keepdims=True)

    total = square(inner_piece[...]) + square(outer_piece[...]) + square(wo_piece[...])
    for member, reducer in enumerate(reducers):
        piece = reducer.finish() * inv_tokens
        late_out[member] = piece
        low = piece.astype(BF16)
        attention_shard[member] = low
        attention_full[(member,) + mine] = low
        total = total + square(piece)
    tile[...] = jnp.broadcast_to(total, tile.shape)
    start_all(stage(late, 0))
    squares.begin()
    wait_all(fetch)
    wait_all(stage(late, 0))
    start_all(stage(late, 1))
    squares.advance(0)
    wait_all(stage(early, 2))
    start_all(stage(early, 3))
    wait_all(stage(late, 1))
    start_all(stage(late, 2))
    squares.advance(1)
    wait_all(stage(early, 3))
    common = (data_rank, counts, place.model)
    root_products(
        inner_full, roots[2][...], roots[3][...], *common, inner_left_out, inner_right_out, inner_update_out, room
    )
    wait_all(stage(late, 2))
    start_all(stage(late, 3))
    squares.advance(2)
    root_products(
        outer_full, roots[4][...], roots[5][...], *common, outer_left_out, outer_right_out, outer_update_out, room
    )
    wait_all(stage(late, 3))
    squares.advance(3)
    squares_out[...] = tile[...]
    for member in range(4):
        root_products(
            attention_full.at[member],
            roots[0][member],
            roots[1][member],
            *common,
            attention_left_out.at[member],
            attention_right_out.at[member],
            attention_update_out.at[member],
            room,
        )
    swap.wait()


def update(pieces, dw, dw_low, grads, weights, skip, roots, counts):
    data_count, model_count = counts
    far_count = data_count // 2
    rows = skip.shape[0]
    inner_piece, outer_piece, wo_piece = pieces

    def seen(array):
        return array.reshape(3, far_count, 2, D // data_count, D)

    def products(lead, height, width):
        return [
            jax.ShapeDtypeStruct(lead + shape, F32)
            for shape in (
                (height // data_count, height // model_count),
                (width // data_count, width // model_count),
                (height // data_count, width // model_count),
            )
        ]

    tile = (8, 128)
    out_shape = [
        jax.ShapeDtypeStruct((3,) + wo_piece.shape, F32),
        jax.ShapeDtypeStruct(tile, F32),
        jax.ShapeDtypeStruct((rows, D), F32),
        jax.ShapeDtypeStruct((rows, D), BF16),
    ]
    out_shape += products((4,), D, D) + products((), D, FF) + products((), FF, D)
    scratch = []
    for _ in range(3):
        scratch += reduce_scratch(far_count, *wo_piece.shape)
    scratch += [pltpu.VMEM(root.shape, F32) for root in roots]
    scratch += [
        pltpu.VMEM((4,) + wo_piece.shape, BF16),
        pltpu.VMEM(inner_piece.shape, BF16),
        pltpu.VMEM(outer_piece.shape, BF16),
        pltpu.VMEM((4, far_count, 2, D // data_count, D), BF16),
        pltpu.VMEM((far_count, 2, D // data_count, FF), BF16),
        pltpu.VMEM((far_count, 2, FF // data_count, D), BF16),
        pltpu.VMEM((FF // model_count, FF // model_count), F32),
        pltpu.VMEM((rows, D), BF16),
    ]
    scratch += spread_scratch(far_count, tile)
    copies = 3 * reduce_copies(far_count) + 6 * gather_copies(far_count) + spread_copies(far_count) + 1
    scratch += [
        pltpu.SemaphoreType.DMA((copies,)),
        pltpu.SemaphoreType.DMA((copies,)),
        pltpu.SemaphoreType.DMA((3, 4)),
        pltpu.SemaphoreType.DMA((6,)),
    ]
    return pl.pallas_call(
        functools.partial(update_kernel, far_count, counts, 1.0 / (rows * data_count * model_count)),
        name="update",
        in_specs=[vmem_spec()] * 3 + [any_spec()] * 2 + [vmem_spec()] * 5 + [any_spec()] * 6,
        out_specs=[vmem_spec()] * len(out_shape),
        out_shape=out_shape,
        scratch_shapes=scratch,
        compiler_params=pltpu.CompilerParams(
            vmem_limit_bytes=VMEM_LIMIT, collective_id=3, has_side_effects=True
        ),
    )(*pieces, seen(dw), seen(dw_low), *grads, weights, skip, *roots)


def finish_kernel(limit, rate, squares_ref, norm_ref, own_ref, twin_ref, late_ref, *rest):
    (inner_piece, outer_piece, wo_piece, norm_piece, norm_param), rest = rest[:5], rest[5:]
    stats, rest = rest[:6], rest[6:]
    products, rest = rest[:6], rest[6:]
    weights, rest = rest[:3], rest[3:]
    updates, rest = rest[:3], rest[3:]
    (states_out, norm_out, attention_grad, inner_grad, outer_grad, norm_grad), rest = rest[:6], rest[6:]
    weights_new, norm_new, stats_new = rest[:3], rest[3], rest[4:]
    norms = norm_ref[0:4, :]
    norm_square = jnp.sum(jnp.sum(norms * norms, axis=0, keepdims=True), axis=1, keepdims=True)
    grad_norm = jnp.sqrt(squares_ref[0:1, 0:1] + norm_square)
    norm_out[...] = grad_norm
    factor = jnp.minimum(1.0, limit / grad_norm)
    states_out[...] = (own_ref[...] + twin_ref[...].astype(F32)).astype(BF16)
    for member in range(3):
        attention_grad[member] = late_ref[member] * factor
    attention_grad[3] = wo_piece[...] * factor
    inner_grad[...] = inner_piece[...] * factor
    outer_grad[...] = outer_piece[...] * factor
    clipped = norm_piece[...] * factor
    norm_grad[...] = clipped
    norm_new[...] = norm_param[...] - rate * clipped
    for weight, change, out in zip(weights, updates, weights_new):
        out[...] = weight[...] - (step_rate * factor) * change[...]
    for stat, product, out in zip(stats, products, stats_new):
        out[...] = 0.5 * stat[...] + (0.5 * factor * factor) * product[...]


def finish(token_total, squares, norm_rows, own, twin, late, pieces, norm_piece, norm_param, stats, products, weights, updates):
    limit = 0.01 * math.sqrt((4 * D * D + 2 * D * FF + 4 * D) / token_total)
    rate = 20.0 * math.sqrt(token_total)
    inner_piece, outer_piece, _ = pieces
    shapes = [
        jax.ShapeDtypeStruct(own.shape, BF16),
        jax.ShapeDtypeStruct((1, 1), F32),
        jax.ShapeDtypeStruct(weights[0].shape, F32),
        jax.ShapeDtypeStruct(inner_piece.shape, F32),
        jax.ShapeDtypeStruct(outer_piece.shape, F32),
        jax.ShapeDtypeStruct(norm_piece.shape, F32),
    ]
    shapes += [jax.ShapeDtypeStruct(weight.shape, F32) for weight in weights]
    shapes.append(jax.ShapeDtypeStruct(norm_piece.shape, F32))
    shapes += [jax.ShapeDtypeStruct(stat.shape, F32) for stat in stats]
    operands = (squares, norm_rows, own, twin, late, *pieces, norm_piece, norm_param)
    operands += (*stats, *products, *weights, *updates)
    return pl.pallas_call(
        functools.partial(finish_kernel, limit, rate),
        name="finish",
        in_specs=[vmem_spec()] * len(operands),
        out_specs=[vmem_spec()] * len(shapes),
        out_shape=shapes,
        compiler_params=pltpu.CompilerParams(vmem_limit_bytes=VMEM_LIMIT),
    )(*operands)


def middle_kernel(
    mixed_ref,
    states_ref,
    cotangent_ref,
    halting_ref,
    wo_ref,
    inner_ref,
    outer_ref,
    gains_ref,
    biases_ref,
    swap_ref,
    out_ref,
    dm_ref,
    dx_ref,
    skip_ref,
    inner_raw,
    outer_raw,
    wo_raw,
    norm_raw,
    inner_low,
    outer_low,
    wo_low,
    gelu_slope,
):
    @pl.when(pl.program_id(0) == 0)
    def _():
        inner_raw[...] = jnp.zeros_like(inner_raw)
        outer_raw[...] = jnp.zeros_like(outer_raw)
        wo_raw[...] = jnp.zeros_like(wo_raw)
        norm_raw[...] = jnp.zeros_like(norm_raw)

    def mean(value):
        return jnp.mean(value, axis=-1, keepdims=True)

    def total(value):
        return jnp.sum(value, axis=0, keepdims=True)

    def normalize(residual):
        centered = residual - mean(residual)
        scale = lax.rsqrt(mean(centered * centered) + epsilon)
        return centered * scale, scale

    def norm_back(d_out, gain, unit, scale):
        d_unit = d_out * gain
        return (d_unit - mean(d_unit) - unit * mean(d_unit * unit)) * scale

    mixed = mixed_ref[...]
    mixed_low = mixed.astype(BF16)
    hidden = states_ref[...].astype(F32)
    upstream = cotangent_ref[...].astype(F32)
    running = halting_ref[...] == 1
    gain1, gain2 = gains_ref[0:1, :], gains_ref[1:2, :]
    unit1, scale1 = normalize(hidden + mm(mixed_low, wo_ref[...]))
    normed = unit1 * gain1 + biases_ref[0:1, :]
    normed_low = normed.astype(BF16)
    inner = mm(normed_low, inner_ref[...])
    rate = math.sqrt(2.0 / math.pi)
    square = inner * inner
    bend = jnp.tanh(rate * inner * (1.0 + 0.044715 * square))
    half = 0.5 * (1.0 + bend)
    activated = (inner * half).astype(BF16)
    gelu_slope[...] = half + 0.5 * inner * (1.0 - bend * bend) * (rate * (1.0 + 3 * 0.044715 * square))
    unit2, scale2 = normalize(normed + mm(activated, outer_ref[...]))
    final = unit2 * gain2 + biases_ref[1:2, :]
    out_ref[...] = jnp.where(running, final, hidden).astype(BF16)
    d_final = jnp.where(running, upstream, 0.0)
    d_resid2 = norm_back(d_final, gain2, unit2, scale2)
    d_branch = d_resid2.astype(BF16)
    outer_raw[...] += mm(activated, d_branch, TN)
    d_inner = (mm(d_branch, outer_ref[...], NT) * gelu_slope[...]).astype(BF16)
    inner_raw[...] += mm(normed_low, d_inner, TN)
    d_normed = d_resid2 + mm(d_inner, inner_ref[...], NT)
    d_resid1 = norm_back(d_normed, gain1, unit1, scale1)
    d_attended = d_resid1.astype(BF16)
    wo_raw[...] += mm(mixed_low, d_attended, TN)
    d_mixed = mm(d_attended, wo_ref[...], NT).astype(BF16)
    dm_ref[...] = d_mixed
    skip_ref[...] = jnp.where(running, 0.0, upstream) + d_resid1
    norm_raw[0:1, :] += total(d_normed * unit1)
    norm_raw[1:2, :] += total(d_final * unit2)
    norm_raw[2:3, :] += total(d_normed)
    norm_raw[3:4, :] += total(d_final)
    high, low = split2(d_mixed.astype(F32) * mixed)
    delta = mm(high, swap_ref[...]) + mm(low, swap_ref[...])
    parts = split3(-delta)
    place = lax.broadcasted_iota(jnp.int32, (1, D), 1) % DH
    extra = jnp.zeros_like(delta)
    for number, part in enumerate(parts):
        extra = jnp.where(place == number + 1, part, extra)
    dx_ref[...] = extra.astype(BF16)

    @pl.when(pl.program_id(0) == pl.num_programs(0) - 1)
    def _():
        inner_low[...] = inner_raw[...].astype(BF16)
        outer_low[...] = outer_raw[...].astype(BF16)
        wo_low[...] = wo_raw[...].astype(BF16)


def middle(mixed, states, cotangent, halting, wo, inner, outer, gains, biases):
    rows = mixed.shape[0]
    head = jnp.arange(D) // DH
    swap = (head[:, None] == (head ^ 1)[None, :]).astype(BF16)

    def by_token(width):
        return pl.BlockSpec((TOKEN_ROWS, width), lambda i: (i, 0))

    def fixed(shape):
        return pl.BlockSpec(shape, lambda i: (0, 0))

    return pl.pallas_call(
        middle_kernel,
        name="middle",
        grid=(rows // TOKEN_ROWS,),
        in_specs=[
            by_token(D),
            by_token(D),
            by_token(D),
            by_token(1),
            fixed((D, D)),
            fixed((D, FF)),
            fixed((FF, D)),
            fixed((2, D)),
            fixed((2, D)),
            fixed((D, D)),
        ],
        out_specs=[
            by_token(D),
            by_token(D),
            by_token(D),
            by_token(D),
            fixed((D, FF)),
            fixed((FF, D)),
            fixed((D, D)),
            fixed((8, D)),
            fixed((D, FF)),
            fixed((FF, D)),
            fixed((D, D)),
        ],
        out_shape=[
            jax.ShapeDtypeStruct((rows, D), BF16),
            jax.ShapeDtypeStruct((rows, D), BF16),
            jax.ShapeDtypeStruct((rows, D), BF16),
            jax.ShapeDtypeStruct((rows, D), F32),
            jax.ShapeDtypeStruct((D, FF), F32),
            jax.ShapeDtypeStruct((FF, D), F32),
            jax.ShapeDtypeStruct((D, D), F32),
            jax.ShapeDtypeStruct((8, D), F32),
            jax.ShapeDtypeStruct((D, FF), BF16),
            jax.ShapeDtypeStruct((FF, D), BF16),
            jax.ShapeDtypeStruct((D, D), BF16),
        ],
        scratch_shapes=[pltpu.VMEM((TOKEN_ROWS, FF), F32)],
        compiler_params=pltpu.CompilerParams(vmem_limit_bytes=VMEM_LIMIT),
    )(mixed, states, cotangent, halting[:, None], wo, inner, outer, gains, biases, swap)


def per_device(
    states,
    cotangent,
    halting,
    lengths,
    attention_weights,
    inner_weight,
    outer_weight,
    norm_gains,
    norm_biases,
    attention_left,
    attention_right,
    inner_left,
    inner_right,
    outer_left,
    outer_right,
    attention_left_root,
    attention_right_root,
    inner_left_root,
    inner_right_root,
    outer_left_root,
    outer_right_root,
):
    data_count = lax.axis_size("dp")
    model_count = lax.axis_size("mp")
    data_rank = lax.axis_index("dp")
    model_rank = lax.axis_index("mp")
    counts = (data_count, model_count)
    ranks = (data_rank, model_rank)
    rows = states.shape[0]
    token_total = rows * data_count * model_count
    far_count = data_count // 2
    weights, queries, keys, values, twin_states = project(states, attention_weights, far_count)
    attention_full = weights.reshape(3, D, D)
    length = lax.dynamic_index_in_dim(lengths, model_rank // 2, 0, keepdims=False)
    own_half = model_rank % 2
    index = jnp.arange(SEQ, dtype=jnp.int32)
    position = jnp.where(index < rows, index + own_half * rows, index - own_half * rows)
    bias = jnp.where(position < length, 0.0, -1e30)[:, None]
    place = (jnp.arange(PAIR) % DH)[None, :]
    key_extra = jnp.where(place == 0, bias, jnp.where(place <= 3, 1.0, 0.0)).astype(BF16)

    mixed, query_extra, inner_full, outer_full, wo_full = attention_forward(
        queries,
        keys,
        values,
        key_extra,
        inner_weight.astype(BF16),
        outer_weight.astype(BF16),
        attention_weights[3].astype(BF16),
        far_count,
    )
    output_states, d_mixed, d_extra, skip, *raws, norm_rows, inner_low, outer_low, wo_low = middle(
        mixed, states, cotangent, halting, wo_full, inner_full, outer_full, norm_gains, norm_biases
    )
    lows = (inner_low, outer_low, wo_low)
    d_queries, d_keys, d_values, dw, dw_low, *pieces, norm_total = attention_backward(
        queries, query_extra, keys, values, key_extra, d_mixed, d_extra, states, twin_states, raws, lows, norm_rows, counts
    )
    roots = (
        attention_left_root,
        attention_right_root,
        inner_left_root,
        inner_right_root,
        outer_left_root,
        outer_right_root,
    )
    late, squares, own, twin, *products = update(
        pieces, dw, dw_low, (d_queries, d_keys, d_values), attention_full, skip, roots, counts
    )
    norm_share = 4 * D // (data_count * model_count)
    flat_rank = data_rank * model_count + model_rank

    def share_of(flat):
        return lax.dynamic_slice_in_dim(flat, flat_rank * norm_share, norm_share, 0)[None]

    flat_params = jnp.concatenate([norm_gains.reshape(-1), norm_biases.reshape(-1)])
    outs = finish(
        token_total,
        squares,
        norm_total,
        own,
        twin,
        late,
        pieces,
        share_of(norm_total[:4].reshape(-1)),
        share_of(flat_params),
        (attention_left, attention_right, inner_left, inner_right, outer_left, outer_right),
        (products[0], products[1], products[3], products[4], products[6], products[7]),
        (attention_weights, inner_weight, outer_weight),
        (products[2], products[5], products[8]),
    )
    states_grad, grad_norm, attention_grad, inner_grad, outer_grad, norm_grad = outs[:6]
    attention_new, inner_new, outer_new, norm_new = outs[6:10]
    return (
        output_states,
        states_grad,
        grad_norm.reshape(()),
        attention_grad,
        inner_grad,
        outer_grad,
        norm_grad.reshape(-1),
        attention_new,
        inner_new,
        outer_new,
        norm_new.reshape(-1),
        *outs[10:],
    )


def solution(mesh):
    grid = P("dp", "mp")
    stack = P(None, "dp", "mp")
    tokens = P(("dp", "mp"), None)
    flat = P(("dp", "mp"))
    return jax.shard_map(
        per_device,
        mesh=mesh,
        in_specs=(tokens, tokens, flat, P("dp"), stack, grid, grid, P(), P())
        + (stack, stack, grid, grid, grid, grid)
        + (P(None, "dp", None), P(None, None, "mp"), P("dp", None), P(None, "mp"), P("dp", None), P(None, "mp")),
        out_specs=(tokens, tokens, P(), stack, grid, grid, flat, stack, grid, grid, flat)
        + (stack, stack, grid, grid, grid, grid),
        check_vma=False,
    )
```

```python
import functools
import math

import jax
import jax.numpy as jnp
from jax import lax
from jax.experimental import pallas as pl
from jax.experimental.pallas import tpu as pltpu
from jax.sharding import PartitionSpec as P

D = 512
HEADS = 8
DH = 64
FF = 2048
SEQ = 2048
SEQ_GRP = 2
PAIR = 2 * DH
QUERY_ROWS = 256
KEY_ROWS = 256
TOKEN_ROWS = 256

F32 = jnp.float32
BF16 = jnp.bfloat16
epsilon = 1e-06
step_rate = 1.0
NN = (((1,), (0,)), ((), ()))
NT = (((1,), (1,)), ((), ()))
TN = (((0,), (0,)), ((), ()))
VMEM_LIMIT = 56 * 1024 * 1024
BACKWARD_VMEM = 60 * 1024 * 1024


def mm(left, right, dims=NN):
    return lax.dot_general(left, right, dims, preferred_element_type=F32)


def split2(value):
    high = value.astype(BF16)
    return high, (value - high.astype(F32)).astype(BF16)


def split3(value):
    high = value.astype(BF16).astype(F32)
    rest = value - high
    middle = rest.astype(BF16).astype(F32)
    return high, middle, rest - middle


MESH = pl.DeviceIdType.MESH


class Place:
    def __init__(self, far_count):
        data_rank = lax.axis_index("dp")
        self.far_count = far_count
        self.model = lax.axis_index("mp")
        self.far, self.near = data_rank // 2, data_rank % 2
        self.data_rank = 2 * self.far + self.near
        side, core = self.model // 2, self.model % 2
        self.side, self.core = side, core
        self.beside = 2 * (1 - side) + core
        self.twin = 2 * side + 1 - core
        self.twin_beside = 2 * (1 - side) + 1 - core
        self.to_beside = {"mp": self.beside}
        self.to_twin = {"mp": self.twin}
        self.to_near = {"dp": 2 * self.far + 1 - self.near}

    def other_far(self, step):
        return (self.far + step) % self.far_count

    def to_far(self, step):
        return {"dp": 2 * self.other_far(step) + self.near}

    def meet(self):
        barrier = pltpu.get_barrier_semaphore()
        partners = [self.to_far(step) for step in range(1, self.far_count)]
        partners += [self.to_near, self.to_beside, self.to_twin]
        for partner in partners:
            pl.semaphore_signal(barrier, inc=1, device_id=partner, device_id_type=MESH)
        pl.semaphore_wait(barrier, len(partners))


class Wires:
    def __init__(self, send_sems, recv_sems):
        self.sems = (send_sems, recv_sems)
        self.used = 0

    def copy(self, source, target, partner):
        index = self.used
        self.used += 1
        return pltpu.make_async_remote_copy(
            src_ref=source,
            dst_ref=target,
            send_sem=self.sems[0].at[index],
            recv_sem=self.sems[1].at[index],
            device_id=partner,
            device_id_type=MESH,
        )


def start_all(copies):
    for copy in copies:
        copy.start()


def wait_all(copies):
    for copy in copies:
        copy.wait()


def columns(index, size):
    return pl.ds(pl.multiple_of(index * size, size), size)


class Chunk:
    def __init__(self, rows, cols, row_size, col_size):
        self.rows, self.cols, self.row_size, self.col_size = rows, cols, row_size, col_size

    def columns(self, index):
        offset = pl.multiple_of(index * self.col_size + self.cols[0], math.gcd(self.col_size, max(self.cols[0], 128)))
        return pl.ds(offset, self.cols[1])

    @property
    def row_window(self):
        return pl.ds(*self.rows)

    @property
    def shape(self):
        return self.rows[1], self.cols[1]


def whole_chunk(rows, cols):
    return Chunk((0, rows), (0, cols), rows, cols)


class Staged:
    def __init__(self, active, twin_stage):
        self.active, self.twin_stage = active, twin_stage
        self.stages = []

    def start(self, number):
        copies = self.stages[number]
        if self.active is None:
            start_all(copies)
        elif number != self.twin_stage:
            pl.when(self.active)(lambda: start_all(copies))
        else:
            pl.when(self.sends)(lambda: start_all(copies))

    def wait(self, number):
        copies = self.stages[number]
        if self.active is None:
            wait_all(copies)
        elif number != self.twin_stage:
            pl.when(self.active)(lambda: wait_all(copies))
        else:

            @pl.when(self.sends)
            def _():
                for copy in copies:
                    copy.wait_send()

            @pl.when(jnp.logical_not(self.sends))
            def _():
                for copy in copies:
                    copy.wait_recv()


class Gather(Staged):
    def __init__(self, wires, place, full, order, chunk, active=None):
        super().__init__(active, len(order) - 1)
        self.sends = active
        mine, side = chunk.columns(place.model), chunk.columns(place.beside)
        self.home = full.at[place.far, place.near, chunk.row_window, mine]
        fars, nears, cols = place.far, place.near, [mine]

        def send(col, partner):
            view = full.at[fars, nears, chunk.row_window, col]
            return wires.copy(view, view, partner)

        for letter in order:
            if letter == "x":
                self.stages.append([send(mine, place.to_beside)])
                cols = [mine, side]
            elif letter == "y":
                self.stages.append([send(col, place.to_near) for col in cols])
                nears = slice(None)
            elif letter == "c":
                self.stages.append([send(col, place.to_twin) for col in cols])
            else:
                ways = [place.to_far(step) for step in range(1, place.far_count)]
                self.stages.append([send(col, way) for col in cols for way in ways])
                fars = slice(None)

    def begin(self):
        self.start(0)

    def advance(self, number):
        self.wait(number)
        if number + 1 < len(self.stages):
            self.start(number + 1)


GATHER_STEPS = 4


def gather_copies(far_count):
    return far_count + 6


def reduce_plan(order, far_count, rows, cols):
    slots, nears, fars = 2, 2, far_count
    plan = []
    for letter in order:
        if letter == "x":
            plan.append((letter, slots, nears, fars, (nears, fars, rows, cols)))
            slots = 1
        elif letter == "y":
            plan.append((letter, slots, nears, fars, (slots, fars, rows, cols)))
            nears = 1
        else:
            plan.append((letter, slots, nears, fars, (far_count, slots, nears, rows, cols)))
            fars = 1
    return plan


REDUCE_BUFFERS = 8
REDUCE_STEPS = 4


def reduce_copies(far_count):
    return far_count + 6


def reduce_scratch(order, far_count, rows, cols):
    shape = (2, 2, far_count, rows, cols)
    buffers = [pltpu.VMEM(shape, F32), pltpu.VMEM(shape, BF16)]
    for *_, shape in reduce_plan(order, far_count, rows, cols):
        buffers += [pltpu.VMEM(shape, BF16), pltpu.VMEM(shape, BF16)]
    return buffers


class Reducer(Staged):
    def __init__(self, wires, place, buffers, order, low=None, chunk=None, given=None, active=None):
        super().__init__(active, 0)
        self.sends = None if active is None else jnp.logical_not(active)
        self.place = place
        self.acc, self.got = buffers[:2]
        self.out, self.arrived = buffers[2::2], buffers[3::2]
        rows, size = self.acc.shape[-2:]
        self.plan = reduce_plan(order, place.far_count, rows, size)
        self.chunk = chunk
        self.kept = (place.model, place.beside)
        if given is not None:
            first = [wires.copy(given, self.got, place.to_twin)]
        else:
            twins = (place.twin, place.twin_beside)
            first = [
                wires.copy(
                    low.at[:, near, chunk.row_window, chunk.columns(twins[slot])],
                    self.got.at[slot, near],
                    place.to_twin,
                )
                for slot in range(2)
                for near in range(2)
            ]
        self.stages = [first]
        for (letter, *_), out, arrived in zip(self.plan, self.out, self.arrived):
            if letter == "z":
                stage = [
                    wires.copy(out.at[place.other_far(step)], arrived.at[step], place.to_far(step))
                    for step in range(1, place.far_count)
                ]
            else:
                stage = [wires.copy(out, arrived, place.to_beside if letter == "x" else place.to_near)]
            self.stages.append(stage)

    def loads(self, partial, load_sems):
        return [
            pltpu.make_async_copy(
                partial.at[:, near, self.chunk.row_window, self.chunk.columns(self.kept[slot])],
                self.acc.at[slot, near],
                load_sems.at[2 * slot + near],
            )
            for slot in range(2)
            for near in range(2)
        ]

    def begin(self):
        self.start(0)

    def held(self, number):
        letter, slots, nears, fars, _ = self.plan[number]
        place = self.place
        return (
            letter,
            range(slots),
            range(2) if nears == 2 else (place.near,),
            range(place.far_count) if fars > 1 else (place.far,),
        )

    def prepare(self, number):
        letter, slots, nears, fars = self.held(number)
        place, acc, out = self.place, self.acc, self.out[number]
        if letter == "x":
            for i, near in enumerate(nears):
                for j, far in enumerate(fars):
                    out[i, j] = acc[1, near, far].astype(BF16)
        elif letter == "y":
            for slot in slots:
                for j, far in enumerate(fars):
                    out[slot, j] = acc[slot, 1 - place.near, far].astype(BF16)
        else:
            for slot in slots:
                for i, near in enumerate(nears):
                    for far in fars:
                        out[far, slot, i] = acc[slot, near, far].astype(BF16)

    def absorb(self, number):
        letter, slots, nears, fars = self.held(number)
        place, acc, arrived = self.place, self.acc, self.arrived[number]
        if letter == "x":
            for i, near in enumerate(nears):
                for j, far in enumerate(fars):
                    acc[0, near, far] += arrived[i, j].astype(F32)
        elif letter == "y":
            for slot in slots:
                for j, far in enumerate(fars):
                    acc[slot, place.near, far] += arrived[slot, j].astype(F32)
        else:
            for slot in slots:
                for i, near in enumerate(nears):
                    total = acc[slot, near, place.far]
                    for step in range(1, place.far_count):
                        total = total + arrived[step, slot, i].astype(F32)
                    acc[slot, near, place.far] = total

    def advance(self, number):
        self.wait(number)

        def add():
            if number == 0:
                for slot in range(2):
                    for near in range(2):
                        for far in range(self.place.far_count):
                            self.acc[slot, near, far] += self.got[slot, near, far].astype(F32)
            else:
                self.absorb(number - 1)
            if number < len(self.plan):
                self.prepare(number)

        if self.active is None:
            add()
        else:
            pl.when(self.active)(add)
        if number < len(self.plan):
            self.start(number + 1)

    def result(self):
        return self.acc[0, self.place.near, self.place.far]


class Spread:
    def __init__(self, wires, place, tile, stages, slots):
        self.place, self.tile, self.stages, self.slots = place, tile, stages, slots
        self.copies = [
            [wires.copy(tile, stages.at[number], partner)]
            for number, partner in enumerate((place.to_twin, place.to_beside, place.to_near))
        ]
        self.copies.append(
            [wires.copy(tile, slots.at[place.far], place.to_far(step)) for step in range(1, place.far_count)]
        )

    def begin(self):
        start_all(self.copies[0])

    def advance(self, number):
        wait_all(self.copies[number])
        if number == 3:
            self.slots[self.place.far] = self.tile[...]
            total = self.slots[0]
            for far in range(1, self.place.far_count):
                total = total + self.slots[far]
            self.tile[...] = total
        else:
            self.tile[...] += self.stages[number]
            start_all(self.copies[number + 1])


def spread_copies(far_count):
    return far_count - 1 + 3


def spread_scratch(far_count, shape):
    return [pltpu.VMEM(shape, F32), pltpu.VMEM((3,) + shape, F32), pltpu.VMEM((far_count,) + shape, F32)]


def any_spec():
    return pl.BlockSpec(memory_space=pl.ANY)


def vmem_spec():
    return pl.BlockSpec(memory_space=pltpu.VMEM)


def smem_spec():
    return pl.BlockSpec(memory_space=pltpu.SMEM)


def own_lanes(parity):
    lane = lax.broadcasted_iota(jnp.int32, (1, PAIR), 1)
    return (lane < DH) if parity == 0 else (lane >= DH)


def lane_in_half():
    return lax.broadcasted_iota(jnp.int32, (1, PAIR), 1) % DH


def blend(parity, own, extra):
    mine = jnp.where(own_lanes(parity), 1.0, 0.0)
    return own * mine.astype(BF16) + extra * (1.0 - mine).astype(BF16)


def slot_calls(step, width, calls):
    def at(sub_step):
        for slot, call in calls:
            if slot % width == sub_step:
                pl.when(step == slot // width)(call)

    return at


PROJECT_ORDERS = ("zxyc", "zyxc", "zxyc")
FORWARD_ORDERS = ("zxyc", "zyxc", "zyxc")
FORWARD_SLOTS = ((0, 8, 23), (0, 8, 24), (1, 9, 24))


def front_kernel(
    far_count,
    states_ref,
    states_any,
    attention_ref,
    inner_ref,
    outer_ref,
    lengths_ref,
    mixed_ref,
    qx_ref,
    extra_ref,
    weights_out,
    queries_out,
    keys_out,
    values_out,
    twin_out,
    inner_full,
    outer_full,
    wo_full,
    full,
    queries,
    keys,
    values,
    twin_states,
    twin_queries,
    inner_low,
    outer_low,
    wo_low,
    ka,
    va,
    score_a,
    score_b,
    send_sems,
    recv_sems,
    local_sems,
):
    rows = states_ref.shape[0]
    step = pl.program_id(0)
    here = Place(far_count)
    wires = Wires(send_sems, recv_sems)
    shard = full.shape[-2], full.shape[-1] // 4
    projections = [
        Gather(wires, here, full.at[member], PROJECT_ORDERS[member], whole_chunk(*shard)) for member in range(3)
    ]
    fulls, lows = (inner_full, outer_full, wo_full), (inner_low, outer_low, wo_low)
    gathers = [
        Gather(wires, here, target, order, whole_chunk(*low.shape))
        for target, low, order in zip(fulls, lows, FORWARD_ORDERS)
    ]
    fill = [
        pltpu.make_async_copy(low, gather.home, local_sems.at[number])
        for number, (low, gather) in enumerate(zip(lows, gathers))
    ]
    swap_states = wires.copy(states_any, twin_states, here.to_twin)
    swaps = []
    for number, block in enumerate((here.model, here.beside)):
        cols = columns(block, PAIR)
        for kept in (keys, values):
            for start, end in ((0, rows), (rows, 0)):
                swaps.append(
                    wires.copy(kept.at[pl.ds(start, rows), cols], kept.at[pl.ds(end, rows), cols], here.to_twin)
                )
        swaps.append(wires.copy(twin_queries.at[number], queries.at[:, cols], here.to_twin))
    outward = [
        pltpu.make_async_copy(source, target, local_sems.at[3 + number])
        for number, (source, target) in enumerate(
            ((queries, queries_out), (keys, keys_out), (values, values_out), (twin_states, twin_out), (full, weights_out))
        )
    ]

    @pl.when(step == 0)
    def _():
        for member in range(3):
            full[member, here.far, here.near, :, columns(here.model, shard[1])] = attention_ref[member].astype(BF16)
        inner_low[...] = inner_ref[...].astype(BF16)
        outer_low[...] = outer_ref[...].astype(BF16)
        wo_low[...] = attention_ref[3].astype(BF16)
        start_all(fill)
        here.meet()
        for gather in projections:
            gather.begin()
        swap_states.start()
        index = lax.broadcasted_iota(jnp.int32, (2 * rows, 1), 0)
        half = here.model % 2
        position = jnp.where(index < rows, index + half * rows, index - half * rows)
        bias = jnp.where(position < lengths_ref[here.side], 0.0, -1e30)
        lane = lane_in_half()
        extra_ref[...] = jnp.where(lane == 0, bias, jnp.where(lane <= 3, 1.0, 0.0)).astype(BF16)
        wait_all(fill)
        for gather in projections:
            gather.advance(0)
        for gather in gathers:
            gather.begin()
        for gather in projections:
            gather.advance(1)
        swap_states.wait()
        for gather in projections:
            gather.advance(2)
        for member, kept in ((1, keys), (2, values), (0, queries)):
            both = jnp.concatenate(
                [full[member, :, :, :, columns(block, PAIR)].reshape(D, PAIR) for block in (here.model, here.beside)],
                axis=1,
            )
            own = mm(states_ref[...], both).astype(BF16)
            twin = mm(twin_states[...], both).astype(BF16)
            if member == 0:
                own = (own * DH ** (-0.5)).astype(BF16)
                twin = (twin * DH ** (-0.5)).astype(BF16)
            for number, block in enumerate((here.model, here.beside)):
                cols = columns(block, PAIR)
                kept[:rows, cols] = own[:, number * PAIR : (number + 1) * PAIR]
                if member:
                    kept[rows:, cols] = twin[:, number * PAIR : (number + 1) * PAIR]
                else:
                    twin_queries[number] = twin[:, number * PAIR : (number + 1) * PAIR]
        start_all(swaps)

    @pl.when(step == 2)
    def _():
        wait_all(swaps)
        for gather in projections:
            gather.advance(3)
        start_all(outward)

    calls = [
        (slot, functools.partial(gather.advance, number))
        for gather, slots in zip(gathers, FORWARD_SLOTS)
        for number, slot in enumerate(slots)
    ]
    at = slot_calls(step, 2 * (rows // QUERY_ROWS), calls)
    pair_cols = columns(2 * (step % 2) + (step // 2 + here.core) % 2, PAIR)
    place = lane_in_half()
    first = jnp.where(place == 0, 1.0, 0.0).astype(BF16)
    ones = jnp.where(place <= 3, 1.0, 0.0).astype(BF16)
    for parity in range(2):
        ka[parity] = blend(parity, keys[:, pair_cols], extra_ref[...])
        va[parity] = blend(parity, values[:, pair_cols], ones)
    steps = [(parity, block) for block in range(rows // QUERY_ROWS) for parity in range(2)]
    scratch = (score_a, score_b)

    def score(index):
        parity, block = steps[index]
        part = blend(parity, queries[pl.ds(block * QUERY_ROWS, QUERY_ROWS), pair_cols], first)
        scratch[index % 2][...] = mm(ka[parity], part, NT)

    score(0)
    held = [None, None]
    logs = [None, None]
    row = lax.broadcasted_iota(jnp.int32, (PAIR, 1), 0)
    for index, (parity, block) in enumerate(steps):
        at(index)
        if index + 1 < len(steps):
            score(index + 1)
        scores = scratch[index % 2][...]
        row_max = jnp.max(scores, axis=0, keepdims=True)
        shifted = jnp.exp(scores - row_max).astype(BF16)
        product = mm(va[parity], shifted, TN)
        sum_row = DH if parity == 0 else 0
        total = product[sum_row : sum_row + 1, :]
        held[parity] = product / total
        logs[parity] = row_max + jnp.log(total)
        if parity == 1:
            window = pl.ds(block * QUERY_ROWS, QUERY_ROWS)
            both = jnp.concatenate([held[0][:DH], held[1][DH:]], axis=0)
            mixed_ref[window, pair_cols] = both.T
            parts = split3(-jnp.where(row < DH, logs[1], logs[0]))
            spot = row % DH
            extra = jnp.where(spot == 0, 1.0, 0.0)
            for number, part in enumerate(parts):
                extra = jnp.where(spot == number + 1, part, extra)
            qx_ref[window, pair_cols] = extra.T.astype(BF16)

    @pl.when(step == pl.num_programs(0) - 1)
    def _():
        for gather in gathers:
            gather.advance(GATHER_STEPS - 1)
        wait_all(outward)


def once(shape):
    return pl.BlockSpec(shape, lambda j: (0,) * len(shape), pipeline_mode=pl.Buffered(1))


def front(states, attention_weights, inner_shard, outer_shard, lengths, far_count):
    rows, width = states.shape
    total = 2 * rows
    shard_rows = attention_weights.shape[1]
    fulls = [
        jax.ShapeDtypeStruct((far_count, 2, height, wide), BF16)
        for height, wide in ((inner_shard.shape[0], FF), (outer_shard.shape[0], D), (shard_rows, D))
    ]
    copies = 6 * gather_copies(far_count) + 11
    weights_shape = (3, far_count, 2, shard_rows, D)
    return pl.pallas_call(
        functools.partial(front_kernel, far_count),
        name="front",
        grid=(width // PAIR,),
        in_specs=[once(states.shape), any_spec()]
        + [once(item.shape) for item in (attention_weights, inner_shard, outer_shard)]
        + [smem_spec()],
        out_specs=[once((rows, width)), once((rows, width)), once((total, PAIR))] + [any_spec()] * 8,
        out_shape=[
            jax.ShapeDtypeStruct((rows, width), F32),
            jax.ShapeDtypeStruct((rows, width), BF16),
            jax.ShapeDtypeStruct((total, PAIR), BF16),
            jax.ShapeDtypeStruct(weights_shape, BF16),
            jax.ShapeDtypeStruct((rows, width), BF16),
            jax.ShapeDtypeStruct((total, width), BF16),
            jax.ShapeDtypeStruct((total, width), BF16),
            jax.ShapeDtypeStruct((rows, width), BF16),
        ]
        + fulls,
        scratch_shapes=[
            pltpu.VMEM(weights_shape, BF16),
            pltpu.VMEM((rows, width), BF16),
            pltpu.VMEM((total, width), BF16),
            pltpu.VMEM((total, width), BF16),
            pltpu.VMEM((rows, width), BF16),
            pltpu.VMEM((2, rows, PAIR), BF16),
            pltpu.VMEM(inner_shard.shape, BF16),
            pltpu.VMEM(outer_shard.shape, BF16),
            pltpu.VMEM(attention_weights.shape[1:], BF16),
            pltpu.VMEM((2, total, PAIR), BF16),
            pltpu.VMEM((2, total, PAIR), BF16),
            pltpu.VMEM((total, QUERY_ROWS), F32),
            pltpu.VMEM((total, QUERY_ROWS), F32),
            pltpu.SemaphoreType.DMA((copies,)),
            pltpu.SemaphoreType.DMA((copies,)),
            pltpu.SemaphoreType.DMA((8,)),
        ],
        compiler_params=pltpu.CompilerParams(
            vmem_limit_bytes=VMEM_LIMIT, collective_id=1, has_side_effects=True
        ),
    )(states, states, attention_weights, inner_shard, outer_shard, lengths)


EARLY = (
    (0, 0, "yxz", "zxyc"),
    (1, 0, "xyz", "zyxc"),
    (2, None, "xyz", "zyxc"),
    (0, 1, "yxz", "zxyc"),
    (1, 1, "xyz", "zyxc"),
)
LATE_REDUCE = ("yxz", "xyz", "yxz")
LATE_GATHER = ("zxyc", "zyxc", "zxyc")
SCHEDULE = (
    (0, 0, 0), (0, 1, 0), (5, 0, 1), (5, 1, 1), (11, 0, 2), (11, 1, 2),
    (11, 2, 0), (11, 3, 0), (11, 4, 0), (15, 2, 1), (16, 0, 3), (16, 1, 3),
    (16, 3, 1), (16, 4, 1), (19, 2, 2), (19, 5, 1), (19, 6, 1), (19, 7, 1),
    (21, 0, 4), (21, 1, 4), (23, 4, 2), (23, 6, 2), (24, 2, 3), (24, 3, 2),
    (24, 5, 2), (24, 7, 2), (26, 0, 5), (26, 1, 5), (26, 6, 3), (27, 2, 4),
    (27, 4, 3), (28, 5, 3), (28, 7, 3), (29, 6, 4), (30, 1, 6), (30, 3, 3),
    (31, 0, 6), (31, 2, 5), (32, 6, 5), (32, 5, 4), (32, 7, 4), (32, 4, 4),
    (32, -1, 0), (32, -1, 1), (32, 3, 4), (32, 2, 6), (32, 10, 1), (32, 8, 1),
    (32, 9, 1), (32, 6, 6), (32, 5, 5), (32, 1, 7), (32, 7, 5), (32, 4, 5),
    (32, 3, 5), (32, 1, 8), (32, 0, 7), (32, 10, 2), (32, 5, 6), (32, 7, 6),
    (32, 8, 2), (32, 4, 6), (32, 6, 7), (32, 9, 2), (32, 0, 8), (32, 2, 7),
    (32, 10, 3), (32, 8, 3), (32, 6, 8), (32, 5, 7), (32, 7, 7), (32, 9, 3),
    (32, 2, 8), (32, 3, 6), (32, 10, 4), (32, 8, 4), (32, 5, 8), (32, 7, 8),
    (32, 9, 4), (32, -1, 11), (32, 4, 7), (32, 10, 5), (32, 8, 5), (32, -1, 12),
    (32, 9, 5), (32, 3, 7), (32, 4, 8), (32, -1, 2), (32, -1, 3), (32, -1, 13),
    (32, -1, 4), (32, 10, 6), (32, 8, 6), (32, 9, 6), (32, -1, 5), (32, 3, 8),
    (32, -1, 6), (32, -1, 14), (32, -1, 7), (32, -1, 8), (32, -1, 9), (32, 9, 7),
    (32, -1, 15), (32, 10, 7), (32, 8, 7), (32, 9, 8), (32, 10, 8), (32, 8, 8),
    (32, -1, 10),
)
NORM_SLOTS = (4, 7, 12, 16)


def early_chunks(shapes):
    chunks = []
    for array, half, *_ in EARLY:
        rows, cols = shapes[array]
        if half is None:
            chunks.append(whole_chunk(rows, cols))
        elif array == 0:
            chunks.append(Chunk((0, rows), (half * cols // 2, cols // 2), rows, cols))
        else:
            chunks.append(Chunk((half * rows // 2, rows // 2), (0, cols), rows, cols))
    return chunks


def product_steps(grad, left_root, right_root, place, counts, left_out, right_out, update_out, room, held):
    data_count, model_count = counts
    far_count, _, shard_rows, width = grad.shape
    height = data_count * shard_rows
    part = far_count // model_count
    size = width // model_count
    share = width // data_count

    def left():
        rows_here = grad[place.far, place.near]
        rows_there = grad[pl.ds(place.model * part, part)].reshape(height // model_count, width)
        left_out[...] = mm(rows_here, rows_there, NT)

    def right():
        cols_there = grad[:, :, :, columns(place.model, size)].reshape(height, size)
        if share % 128 == 0:
            cols_here = grad[:, :, :, columns(place.data_rank, share)].reshape(height, share)
            right_out[...] = mm(cols_here, cols_there, TN)
        else:
            group = data_count // model_count
            cols_here = grad[:, :, :, columns(place.data_rank // group, size)].reshape(height, size)
            room[:size, :size] = mm(cols_here, cols_there, TN)
            window = pl.ds(pl.multiple_of((place.data_rank % group) * share, share), share)
            right_out[...] = room[window, :size]

    def once():
        whole = grad[...].reshape(height, width)
        high, low = split2(left_root[...])
        held[...] = mm(high, whole) + mm(low, whole)

    def twice():
        chunk = min(512, width)
        total = jnp.zeros(update_out.shape, F32)
        for start in range(0, width, chunk):
            high, low = split2(held[:, start : start + chunk])
            root_high, root_low = split2(right_root[start : start + chunk, :])
            total = total + (mm(high, root_high) + mm(high, root_low) + mm(low, root_high))
        update_out[...] = total

    return [left, right, once, twice]


def backward_kernel(
    far_count,
    counts,
    inv_tokens,
    q_ref,
    qx_ref,
    k_ref,
    v_ref,
    kx_ref,
    do_ref,
    dox_ref,
    own_states,
    twin_states,
    weights_ref,
    norm_raw,
    skip_any,
    inner_raw,
    outer_raw,
    wo_raw,
    inner_low,
    outer_low,
    wo_low,
    *rest,
):
    roots_any, rest = rest[:6], rest[6:]
    (inner_piece, outer_piece, wo_piece, norm_total, late_out, squares_out, own_any, twin_in), rest = rest[:8], rest[8:]
    products, rest = rest[:9], rest[9:]
    (qa, da, ka, va, dqt, dq, dk, dv, states_t, late_low, own_sum, twin_out), rest = rest[:12], rest[12:]
    count = len(EARLY) * REDUCE_BUFFERS
    early_buffers, rest = rest[:count], rest[count:]
    late_buffers, rest = rest[: 3 * REDUCE_BUFFERS], rest[3 * REDUCE_BUFFERS :]
    roots, rest = rest[:6], rest[6:]
    (attention_full, inner_full, outer_full, room, held_small, held_wide, held_tall), rest = rest[:7], rest[7:]
    tile, tile_stages, tile_slots, norm_tile, norm_stages, norm_slots = rest[:6]
    send_sems, recv_sems, load_sems, local_sems = rest[6:]

    step = pl.program_id(0)
    rows = q_ref.shape[0]
    total = k_ref.shape[0]
    place = Place(far_count)
    wires = Wires(send_sems, recv_sems)
    partials, lows = (inner_raw, outer_raw, wo_raw), (inner_low, outer_low, wo_low)
    pieces = (inner_piece, outer_piece, wo_piece)
    fulls = (inner_full, outer_full, attention_full.at[3])
    chunks = early_chunks([piece.shape for piece in pieces])
    reducers = []
    gathers = []
    loads = []
    for number, (array, _, reduce_order, gather_order) in enumerate(EARLY):
        buffers = early_buffers[number * REDUCE_BUFFERS : (number + 1) * REDUCE_BUFFERS]
        reducer = Reducer(wires, place, buffers, reduce_order, low=lows[array], chunk=chunks[number])
        reducers.append(reducer)
        loads.append(reducer.loads(partials[array], load_sems.at[number]))
        gathers.append(Gather(wires, place, fulls[array], gather_order, chunks[number]))
    late_shape = wo_piece.shape
    late_reducers = []
    late_gathers = []
    for late_set in range(2):
        active = place.core == late_set
        late_reducers.append(
            [
                Reducer(
                    wires,
                    place,
                    late_buffers[member * REDUCE_BUFFERS : (member + 1) * REDUCE_BUFFERS],
                    LATE_REDUCE[member],
                    given=late_low.at[member],
                    active=active,
                )
                for member in range(3)
            ]
        )
        late_gathers.append(
            [
                Gather(
                    wires, place, attention_full.at[member], LATE_GATHER[member], whole_chunk(*late_shape), active=active
                )
                for member in range(3)
            ]
        )
    norms = Spread(wires, place, norm_tile, norm_stages, norm_slots)
    squares = Spread(wires, place, tile, tile_stages, tile_slots)
    swap = wires.copy(twin_out, twin_in, place.to_twin)
    fetch = [
        pltpu.make_async_copy(source, target, local_sems.at[number])
        for number, (source, target) in enumerate(zip((*roots_any, skip_any), (*roots, own_sum)))
    ]
    outward = pltpu.make_async_copy(own_sum, own_any, local_sems.at[0])

    def early_call(number, number_of_step):
        array, chunk = EARLY[number][0], chunks[number]
        if number_of_step == 0:

            def call():
                reducers[number].begin()
                start_all(loads[number])

        elif number_of_step <= REDUCE_STEPS:

            def call():
                if number_of_step == 1:
                    wait_all(loads[number])
                reducers[number].advance(number_of_step - 1)
                if number_of_step == REDUCE_STEPS:
                    piece = reducers[number].result() * inv_tokens
                    pieces[array][chunk.row_window, pl.ds(*chunk.cols)] = piece
                    gathers[number].home[...] = piece.astype(BF16)
                    gathers[number].begin()

        else:

            def call():
                gathers[number].advance(number_of_step - REDUCE_STEPS - 1)

        return call

    def late_products():
        slot = (step + place.side) % 2
        wide = jnp.concatenate([dk[:, pair_cols], dv[:, pair_cols]], axis=1)
        both = mm(states_t[...], wide)
        values = (mm(states_t[:, :rows], dq[:, pair_cols]), both[:, :PAIR], both[:, PAIR:])
        active = place.core == step // 2
        for member, value in enumerate(values):
            parts = value.reshape(far_count, 2, *late_shape)

            @pl.when(active)
            def _():
                for near in range(2):
                    late_reducers[0][member].acc[slot, near] = parts[:, near]

            @pl.when(jnp.logical_not(active))
            def _():
                for near in range(2):
                    late_low[member, slot, near] = parts[:, near].astype(BF16)

    def late_call(late_set, member, number_of_step):
        reducer, gather = late_reducers[late_set][member], late_gathers[late_set][member]
        if number_of_step == 0:
            return reducer.begin

        def call():
            if number_of_step <= REDUCE_STEPS:
                reducer.advance(number_of_step - 1)
                if number_of_step == REDUCE_STEPS:

                    @pl.when(place.core == late_set)
                    def _():
                        piece = reducer.result() * inv_tokens
                        late_out[member] = piece
                        gather.home[...] = piece.astype(BF16)

                    gather.begin()
            else:
                gather.advance(number_of_step - REDUCE_STEPS - 1)

        return call

    def scheduled(chain, number_of_step):
        if chain < len(EARLY):
            return early_call(chain, number_of_step)
        return late_call(*divmod(chain - len(EARLY), 3), number_of_step)

    sub_steps = 4 * (total // KEY_ROWS)
    calls = [(slot, scheduled(chain, number)) for slot, chain, number in SCHEDULE if slot < sub_steps]
    calls += [(slot, functools.partial(norms.advance, stage)) for stage, slot in enumerate(NORM_SLOTS)]
    calls.append((12, lambda: start_all(fetch)))
    at = slot_calls(step, total // KEY_ROWS, calls)

    @pl.when(step == 0)
    def _():
        norm_tile[...] = norm_raw[...]
        place.meet()
        norms.begin()
        states_t[:, :rows] = own_states[...].T
        states_t[:, rows:] = twin_states[...].T

    lane = lane_in_half()
    ones = jnp.where(lane <= 3, 1.0, 0.0).astype(BF16)
    for parity in range(2):
        ka[parity] = blend(parity, k_ref[...], kx_ref[...])
        va[parity] = blend(parity, v_ref[...], ones)
        qa[parity] = blend(parity, q_ref[...], qx_ref[...])
        da[parity] = blend(parity, do_ref[...], dox_ref[...])
    dqt[...] = jnp.zeros_like(dqt)
    pair = 2 * (step % 2) + step // 2
    pair_cols = columns(pair, PAIR)
    for block in range(total // KEY_ROWS):
        at(block)
        window = pl.ds(block * KEY_ROWS, KEY_ROWS)
        key_grads = []
        value_grads = []
        for parity in range(2):
            key_block = ka[parity, window, :]
            probs = jnp.exp(mm(key_block, qa[parity], NT))
            d_probs = mm(va[parity, window, :], da[parity], NT)
            d_scores = (probs * d_probs).astype(BF16)
            value_grads.append(mm(probs.astype(BF16), da[parity]))
            key_grads.append(mm(d_scores, qa[parity]))
            dqt[parity] += mm(key_block, d_scores, TN)
        dk[window, pair_cols] = jnp.where(own_lanes(0), key_grads[0], key_grads[1]).astype(BF16)
        dv[window, pair_cols] = jnp.where(own_lanes(0), value_grads[0], value_grads[1]).astype(BF16)
    both = jnp.concatenate([dqt[0, :DH], dqt[1, DH:]], axis=0) * DH ** (-0.5)
    dq[:, pair_cols] = both.T.astype(BF16)

    late_products()
    for late_set in range(2):

        @pl.when(step == 2 * late_set + 1)
        def _():
            for member in range(3):
                late_call(late_set, member, 0)()

    @pl.when(step == pl.num_programs(0) - 1)
    def _():
        part = 256

        def twin_share():
            @pl.loop(0, rows // part)
            def _(block):
                window = pl.ds(pl.multiple_of(block * part, part), part)
                there = pl.ds(pl.multiple_of(rows + block * part, part), part)
                value = mm(dk[there, :], weights_ref[1], NT) + mm(dv[there, :], weights_ref[2], NT)
                twin_out[window, :] = value.astype(BF16)

            swap.start()

        def own_share():
            wait_all(fetch)

            @pl.loop(0, rows // part)
            def _(block):
                window = pl.ds(pl.multiple_of(block * part, part), part)
                own_sum[window, :] += (
                    mm(dq[window, :], weights_ref[0], NT)
                    + mm(dk[window, :], weights_ref[1], NT)
                    + mm(dv[window, :], weights_ref[2], NT)
                )

            outward.start()

        common = (place, counts)
        inner_steps = product_steps(inner_full, roots[2], roots[3], *common, *products[3:6], room, held_wide)
        outer_steps = product_steps(outer_full, roots[4], roots[5], *common, *products[6:9], room, held_tall)

        def member_products():
            @pl.loop(0, 4)
            def _(member):
                steps = product_steps(
                    attention_full.at[member],
                    roots[0].at[member],
                    roots[1].at[member],
                    *common,
                    *[product.at[member] for product in products[:3]],
                    room,
                    held_small,
                )
                for call in steps:
                    call()

        work = [twin_share, own_share, *outer_steps, *inner_steps, member_products]

        def square(piece):
            return jnp.sum(jnp.sum(piece * piece, axis=0, keepdims=True), axis=1, keepdims=True)

        def squares_begin():
            square_sum = square(inner_piece[...]) + square(outer_piece[...]) + square(wo_piece[...])
            for member in range(3):
                square_sum = square_sum + square(late_out[member])
            tile[...] = jnp.broadcast_to(square_sum, tile.shape)
            squares.begin()

        work.append(squares_begin)
        work += [functools.partial(squares.advance, stage) for stage in range(4)]
        for slot, chain, number in SCHEDULE:
            if slot >= sub_steps:
                (work[number] if chain < 0 else scheduled(chain, number))()
        squares_out[...] = tile[...]
        norm_total[...] = norm_tile[...] * inv_tokens
        swap.wait()
        outward.wait()


def backward(
    queries,
    query_extra,
    keys,
    values,
    key_extra,
    d_mixed,
    d_extra,
    states,
    twin_states,
    weights,
    norm_rows,
    skip,
    raws,
    lows,
    roots,
    counts,
):
    rows, width = queries.shape
    total = keys.shape[0]
    data_count, model_count = counts
    far_count = data_count // 2

    def by_pair(height):
        return pl.BlockSpec((height, PAIR), lambda j: (0, 2 * (j % 2) + j // 2))

    whole = once

    def seen(array):
        return array.reshape(far_count, 2, array.shape[0] // data_count, array.shape[1])

    def products(lead, height, wide):
        return [
            jax.ShapeDtypeStruct(lead + shape, F32)
            for shape in (
                (height // data_count, height // model_count),
                (wide // data_count, wide // model_count),
                (height // data_count, wide // model_count),
            )
        ]

    pieces = [(raw.shape[0] // data_count, raw.shape[1] // model_count) for raw in raws]
    late = pieces[2]
    tile = (8, 128)
    out_shape = [jax.ShapeDtypeStruct(piece, F32) for piece in pieces]
    out_shape += [
        jax.ShapeDtypeStruct(norm_rows.shape, F32),
        jax.ShapeDtypeStruct((3,) + late, F32),
        jax.ShapeDtypeStruct(tile, F32),
        jax.ShapeDtypeStruct((rows, width), F32),
        jax.ShapeDtypeStruct((rows, width), BF16),
    ]
    out_specs = [whole(item.shape) for item in out_shape[:6]] + [any_spec()] * 2
    tail = products((4,), D, D) + products((), D, FF) + products((), FF, D)
    out_shape += tail
    out_specs += [whole(item.shape) for item in tail]
    shard_rows = D // data_count
    scratch = [
        pltpu.VMEM((2, rows, PAIR), BF16),
        pltpu.VMEM((2, rows, PAIR), BF16),
        pltpu.VMEM((2, total, PAIR), BF16),
        pltpu.VMEM((2, total, PAIR), BF16),
        pltpu.VMEM((2, PAIR, rows), F32),
        pltpu.VMEM((rows, width), BF16),
        pltpu.VMEM((total, width), BF16),
        pltpu.VMEM((total, width), BF16),
        pltpu.VMEM((width, total), BF16),
        pltpu.VMEM((3, 2, 2, far_count) + late, BF16),
        pltpu.VMEM((rows, width), F32),
        pltpu.VMEM((rows, width), BF16),
    ]
    for (_, _, order, _), chunk in zip(EARLY, early_chunks(pieces)):
        scratch += reduce_scratch(order, far_count, *chunk.shape)
    for member in range(3):
        scratch += reduce_scratch(LATE_REDUCE[member], far_count, *late)
    scratch += [pltpu.VMEM(root.shape, F32) for root in roots]
    scratch += [
        pltpu.VMEM((4, far_count, 2, shard_rows, D), BF16),
        pltpu.VMEM((far_count, 2, shard_rows, FF), BF16),
        pltpu.VMEM((far_count, 2, FF // data_count, D), BF16),
        pltpu.VMEM((FF // model_count, FF // model_count), F32),
        pltpu.VMEM((shard_rows, D), F32),
        pltpu.VMEM((shard_rows, FF), F32),
        pltpu.VMEM((FF // data_count, D), F32),
    ]
    scratch += spread_scratch(far_count, tile) + spread_scratch(far_count, norm_rows.shape)
    chains = len(EARLY) + 6
    copies = chains * (reduce_copies(far_count) + gather_copies(far_count)) + 2 * spread_copies(far_count) + 1
    scratch += [
        pltpu.SemaphoreType.DMA((copies,)),
        pltpu.SemaphoreType.DMA((copies,)),
        pltpu.SemaphoreType.DMA((len(EARLY), 4)),
        pltpu.SemaphoreType.DMA((7,)),
    ]
    return pl.pallas_call(
        functools.partial(backward_kernel, far_count, counts, 1.0 / (rows * data_count * model_count)),
        name="backward",
        grid=(width // PAIR,),
        in_specs=[by_pair(rows), by_pair(rows), by_pair(total), by_pair(total), whole((total, PAIR))]
        + [by_pair(rows), by_pair(rows), whole((rows, width)), whole((rows, width))]
        + [whole(weights.shape), whole(norm_rows.shape)]
        + [any_spec()] * 13,
        out_specs=out_specs,
        out_shape=out_shape,
        scratch_shapes=scratch,
        compiler_params=pltpu.CompilerParams(
            vmem_limit_bytes=BACKWARD_VMEM, collective_id=2, has_side_effects=True
        ),
    )(
        queries,
        query_extra,
        keys,
        values,
        key_extra,
        d_mixed,
        d_extra,
        states,
        twin_states,
        weights,
        norm_rows,
        skip,
        *[seen(raw) for raw in raws],
        *[seen(low) for low in lows],
        *roots,
    )


def finish_kernel(limit, rate, squares_ref, norm_ref, own_ref, twin_ref, late_ref, *rest):
    (inner_piece, outer_piece, wo_piece, gains_ref, biases_ref), rest = rest[:5], rest[5:]
    stats, rest = rest[:6], rest[6:]
    products, rest = rest[:6], rest[6:]
    weights, rest = rest[:3], rest[3:]
    updates, rest = rest[:3], rest[3:]
    (states_out, norm_out, attention_grad, inner_grad, outer_grad, norm_grad), rest = rest[:6], rest[6:]
    weights_new, norm_new, stats_new = rest[:3], rest[3], rest[4:]
    norms = norm_ref[0:4, :]
    norm_square = jnp.sum(jnp.sum(norms * norms, axis=0, keepdims=True), axis=1, keepdims=True)
    grad_norm = jnp.sqrt(squares_ref[0:1, 0:1] + norm_square)
    norm_out[...] = grad_norm
    factor = jnp.minimum(1.0, limit / grad_norm)
    states_out[...] = (own_ref[...] + twin_ref[...].astype(F32)).astype(BF16)
    for member in range(3):
        attention_grad[member] = late_ref[member] * factor
    attention_grad[3] = wo_piece[...] * factor
    inner_grad[...] = inner_piece[...] * factor
    outer_grad[...] = outer_piece[...] * factor
    share = norm_grad.shape[-1]
    start = (lax.axis_index("dp") * lax.axis_size("mp") + lax.axis_index("mp")) * share
    params = jnp.concatenate([gains_ref[...], biases_ref[...]], axis=0)
    row = lax.broadcasted_iota(jnp.int32, (4, 1), 0) == start // D

    def share_of(table):
        picked = jnp.sum(jnp.where(row, table, 0.0), axis=0, keepdims=True)
        return pltpu.roll(jnp.broadcast_to(picked, (8, D)), (D - start % D) % D, 1)[0:1, :share]

    clipped = share_of(norms) * factor
    norm_grad[...] = clipped
    norm_new[...] = share_of(params) - rate * clipped
    for weight, change, out in zip(weights, updates, weights_new):
        out[...] = weight[...] - (step_rate * factor) * change[...]
    for stat, product, out in zip(stats, products, stats_new):
        out[...] = 0.5 * stat[...] + (0.5 * factor * factor) * product[...]


def finish(token_total, norm_share, squares, norm_rows, own, twin, late, pieces, gains, biases, stats, products, weights, updates):
    limit = 0.01 * math.sqrt((4 * D * D + 2 * D * FF + 4 * D) / token_total)
    rate = 20.0 * math.sqrt(token_total)
    inner_piece, outer_piece, _ = pieces
    shapes = [
        jax.ShapeDtypeStruct(own.shape, BF16),
        jax.ShapeDtypeStruct((1, 1), F32),
        jax.ShapeDtypeStruct(weights[0].shape, F32),
        jax.ShapeDtypeStruct(inner_piece.shape, F32),
        jax.ShapeDtypeStruct(outer_piece.shape, F32),
        jax.ShapeDtypeStruct((1, norm_share), F32),
    ]
    shapes += [jax.ShapeDtypeStruct(weight.shape, F32) for weight in weights]
    shapes.append(jax.ShapeDtypeStruct((1, norm_share), F32))
    shapes += [jax.ShapeDtypeStruct(stat.shape, F32) for stat in stats]
    operands = (squares, norm_rows, own, twin, late, *pieces, gains, biases)
    operands += (*stats, *products, *weights, *updates)
    return pl.pallas_call(
        functools.partial(finish_kernel, limit, rate),
        name="finish",
        in_specs=[vmem_spec()] * len(operands),
        out_specs=[vmem_spec()] * len(shapes),
        out_shape=shapes,
        compiler_params=pltpu.CompilerParams(vmem_limit_bytes=VMEM_LIMIT),
    )(*operands)


def middle_kernel(
    mixed_ref,
    states_ref,
    cotangent_ref,
    halting_ref,
    wo_ref,
    inner_ref,
    outer_ref,
    gains_ref,
    biases_ref,
    out_ref,
    dm_ref,
    dx_ref,
    skip_ref,
    inner_raw,
    outer_raw,
    wo_raw,
    norm_raw,
    inner_low,
    outer_low,
    wo_low,
    gelu_slope,
    swap_ref,
):
    @pl.when(pl.program_id(0) == 0)
    def _():
        head_row = lax.broadcasted_iota(jnp.int32, (D, D), 0) // DH
        head_col = lax.broadcasted_iota(jnp.int32, (D, D), 1) // DH
        swap_ref[...] = jnp.where(head_row + 1 - 2 * (head_row % 2) == head_col, 1.0, 0.0).astype(BF16)
        inner_raw[...] = jnp.zeros_like(inner_raw)
        outer_raw[...] = jnp.zeros_like(outer_raw)
        wo_raw[...] = jnp.zeros_like(wo_raw)
        norm_raw[...] = jnp.zeros_like(norm_raw)

    def mean(value):
        return jnp.mean(value, axis=-1, keepdims=True)

    def total(value):
        return jnp.sum(value, axis=0, keepdims=True)

    def normalize(residual):
        centered = residual - mean(residual)
        scale = lax.rsqrt(mean(centered * centered) + epsilon)
        return centered * scale, scale

    def norm_back(d_out, gain, unit, scale):
        d_unit = d_out * gain
        return (d_unit - mean(d_unit) - unit * mean(d_unit * unit)) * scale

    mixed = mixed_ref[...]
    mixed_low = mixed.astype(BF16)
    hidden = states_ref[...].astype(F32)
    upstream = cotangent_ref[...].astype(F32)
    table = halting_ref[...].astype(F32).T
    lane = lax.broadcasted_iota(jnp.int32, (1, table.shape[1]), 1)
    here = pl.program_id(0) * (TOKEN_ROWS // 128)
    flags = [
        jnp.sum(jnp.where(lane == here + row, table, 0.0), axis=1, keepdims=True) for row in range(TOKEN_ROWS // 128)
    ]
    running = jnp.concatenate(flags, axis=0) == 1.0
    gain1, gain2 = gains_ref[0:1, :], gains_ref[1:2, :]
    unit1, scale1 = normalize(hidden + mm(mixed_low, wo_ref[...]))
    normed = unit1 * gain1 + biases_ref[0:1, :]
    normed_low = normed.astype(BF16)
    inner = mm(normed_low, inner_ref[...])
    rate = math.sqrt(2.0 / math.pi)
    square = inner * inner
    bend = jnp.tanh(rate * inner * (1.0 + 0.044715 * square))
    half = 0.5 * (1.0 + bend)
    activated = (inner * half).astype(BF16)
    gelu_slope[...] = half + 0.5 * inner * (1.0 - bend * bend) * (rate * (1.0 + 3 * 0.044715 * square))
    unit2, scale2 = normalize(normed + mm(activated, outer_ref[...]))
    final = unit2 * gain2 + biases_ref[1:2, :]
    out_ref[...] = jnp.where(running, final, hidden).astype(BF16)
    d_final = jnp.where(running, upstream, 0.0)
    d_resid2 = norm_back(d_final, gain2, unit2, scale2)
    d_branch = d_resid2.astype(BF16)
    outer_raw[...] += mm(activated, d_branch, TN)
    d_inner = (mm(d_branch, outer_ref[...], NT) * gelu_slope[...]).astype(BF16)
    inner_raw[...] += mm(normed_low, d_inner, TN)
    d_normed = d_resid2 + mm(d_inner, inner_ref[...], NT)
    d_resid1 = norm_back(d_normed, gain1, unit1, scale1)
    d_attended = d_resid1.astype(BF16)
    wo_raw[...] += mm(mixed_low, d_attended, TN)
    d_mixed = mm(d_attended, wo_ref[...], NT).astype(BF16)
    dm_ref[...] = d_mixed
    skip_ref[...] = jnp.where(running, 0.0, upstream) + d_resid1
    norm_raw[0:1, :] += total(d_normed * unit1)
    norm_raw[1:2, :] += total(d_final * unit2)
    norm_raw[2:3, :] += total(d_normed)
    norm_raw[3:4, :] += total(d_final)
    high, low = split2(d_mixed.astype(F32) * mixed)
    delta = mm(high, swap_ref[...]) + mm(low, swap_ref[...])
    parts = split3(-delta)
    place = lax.broadcasted_iota(jnp.int32, (1, D), 1) % DH
    extra = jnp.zeros_like(delta)
    for number, part in enumerate(parts):
        extra = jnp.where(place == number + 1, part, extra)
    dx_ref[...] = extra.astype(BF16)

    @pl.when(pl.program_id(0) == pl.num_programs(0) - 1)
    def _():
        inner_low[...] = inner_raw[...].astype(BF16)
        outer_low[...] = outer_raw[...].astype(BF16)
        wo_low[...] = wo_raw[...].astype(BF16)


def middle(mixed, states, cotangent, halting, wo, inner, outer, gains, biases):
    rows = mixed.shape[0]

    def by_token(width):
        return pl.BlockSpec((TOKEN_ROWS, width), lambda i: (i, 0))

    def fixed(shape):
        return pl.BlockSpec(shape, lambda i: (0, 0))

    return pl.pallas_call(
        middle_kernel,
        name="middle",
        grid=(rows // TOKEN_ROWS,),
        in_specs=[
            by_token(D),
            by_token(D),
            by_token(D),
            fixed((rows // 128, 128)),
            fixed((D, D)),
            fixed((D, FF)),
            fixed((FF, D)),
            fixed((2, D)),
            fixed((2, D)),
        ],
        out_specs=[
            by_token(D),
            by_token(D),
            by_token(D),
            by_token(D),
            fixed((D, FF)),
            fixed((FF, D)),
            fixed((D, D)),
            fixed((8, D)),
            fixed((D, FF)),
            fixed((FF, D)),
            fixed((D, D)),
        ],
        out_shape=[
            jax.ShapeDtypeStruct((rows, D), BF16),
            jax.ShapeDtypeStruct((rows, D), BF16),
            jax.ShapeDtypeStruct((rows, D), BF16),
            jax.ShapeDtypeStruct((rows, D), F32),
            jax.ShapeDtypeStruct((D, FF), F32),
            jax.ShapeDtypeStruct((FF, D), F32),
            jax.ShapeDtypeStruct((D, D), F32),
            jax.ShapeDtypeStruct((8, D), F32),
            jax.ShapeDtypeStruct((D, FF), BF16),
            jax.ShapeDtypeStruct((FF, D), BF16),
            jax.ShapeDtypeStruct((D, D), BF16),
        ],
        scratch_shapes=[pltpu.VMEM((TOKEN_ROWS, FF), F32), pltpu.VMEM((D, D), BF16)],
        compiler_params=pltpu.CompilerParams(vmem_limit_bytes=VMEM_LIMIT),
    )(mixed, states, cotangent, halting.reshape(-1, 128), wo, inner, outer, gains, biases)


def per_device(
    states,
    cotangent,
    halting,
    lengths,
    attention_weights,
    inner_weight,
    outer_weight,
    norm_gains,
    norm_biases,
    attention_left,
    attention_right,
    inner_left,
    inner_right,
    outer_left,
    outer_right,
    attention_left_root,
    attention_right_root,
    inner_left_root,
    inner_right_root,
    outer_left_root,
    outer_right_root,
):
    data_count = lax.axis_size("dp")
    model_count = lax.axis_size("mp")
    counts = (data_count, model_count)
    far_count = data_count // 2
    token_total = states.shape[0] * data_count * model_count
    (
        mixed,
        query_extra,
        key_extra,
        weights,
        queries,
        keys,
        values,
        twin_states,
        inner_full,
        outer_full,
        wo_full,
    ) = front(states, attention_weights, inner_weight, outer_weight, lengths, far_count)
    output_states, d_mixed, d_extra, skip, *raws, norm_rows, inner_low, outer_low, wo_low = middle(
        mixed,
        states,
        cotangent,
        halting,
        wo_full.reshape(D, D),
        inner_full.reshape(D, FF),
        outer_full.reshape(FF, D),
        norm_gains,
        norm_biases,
    )
    roots = (
        attention_left_root,
        attention_right_root,
        inner_left_root,
        inner_right_root,
        outer_left_root,
        outer_right_root,
    )
    *pieces, norm_total, late, squares, own, twin, p0, p1, p2, p3, p4, p5, p6, p7, p8 = backward(
        queries,
        query_extra,
        keys,
        values,
        key_extra,
        d_mixed,
        d_extra,
        states,
        twin_states,
        weights.reshape(3, D, D),
        norm_rows,
        skip,
        raws,
        (inner_low, outer_low, wo_low),
        roots,
        counts,
    )
    outs = finish(
        token_total,
        4 * D // (data_count * model_count),
        squares,
        norm_total,
        own,
        twin,
        late,
        pieces,
        norm_gains,
        norm_biases,
        (attention_left, attention_right, inner_left, inner_right, outer_left, outer_right),
        (p0, p1, p3, p4, p6, p7),
        (attention_weights, inner_weight, outer_weight),
        (p2, p5, p8),
    )
    states_grad, grad_norm, attention_grad, inner_grad, outer_grad, norm_grad = outs[:6]
    attention_new, inner_new, outer_new, norm_new = outs[6:10]
    return (
        output_states,
        states_grad,
        grad_norm.reshape(()),
        attention_grad,
        inner_grad,
        outer_grad,
        norm_grad.reshape(-1),
        attention_new,
        inner_new,
        outer_new,
        norm_new.reshape(-1),
        *outs[10:],
    )


def solution(mesh):
    grid = P("dp", "mp")
    stack = P(None, "dp", "mp")
    tokens = P(("dp", "mp"), None)
    flat = P(("dp", "mp"))
    return jax.shard_map(
        per_device,
        mesh=mesh,
        in_specs=(tokens, tokens, flat, P("dp"), stack, grid, grid, P(), P())
        + (stack, stack, grid, grid, grid, grid)
        + (P(None, "dp", None), P(None, None, "mp"), P("dp", None), P(None, "mp"), P("dp", None), P(None, "mp")),
        out_specs=(tokens, tokens, P(), stack, grid, grid, flat, stack, grid, grid, flat)
        + (stack, stack, grid, grid, grid, grid),
        check_vma=False,
    )
```

```python
import functools
import math

import jax
import jax.numpy as jnp
from jax import lax
from jax.experimental import pallas as pl
from jax.experimental.pallas import tpu as pltpu
from jax.sharding import PartitionSpec as P

D = 512
HEADS = 8
DH = 64
FF = 2048
SEQ = 2048
SEQ_GRP = 2
PAIR = 2 * DH
QUERY_ROWS = 256
FORWARD_CHUNKS = 4
KEY_ROWS = 256
FF_PART = 512
TOKEN_ROWS = 512

F32 = jnp.float32
BF16 = jnp.bfloat16
epsilon = 1e-06
step_rate = 1.0
NN = (((1,), (0,)), ((), ()))
NT = (((1,), (1,)), ((), ()))
TN = (((0,), (0,)), ((), ()))
VMEM_LIMIT = 56 * 1024 * 1024
BACKWARD_VMEM = 62 * 1024 * 1024


def mm(left, right, dims=NN):
    return lax.dot_general(left, right, dims, preferred_element_type=F32)


def split2(value):
    high = value.astype(BF16)
    return high, (value - high.astype(F32)).astype(BF16)


def split3(value):
    high = value.astype(BF16).astype(F32)
    rest = value - high
    middle = rest.astype(BF16).astype(F32)
    return high, middle, rest - middle


MESH = pl.DeviceIdType.MESH


class Place:
    def __init__(self, far_count):
        data_rank = lax.axis_index("dp")
        self.far_count = far_count
        self.model = lax.axis_index("mp")
        self.far, self.near = data_rank // 2, data_rank % 2
        self.data_rank = 2 * self.far + self.near
        side, core = self.model // 2, self.model % 2
        self.side, self.core = side, core
        self.beside = 2 * (1 - side) + core
        self.twin = 2 * side + 1 - core
        self.twin_beside = 2 * (1 - side) + 1 - core
        self.to_beside = {"mp": self.beside}
        self.to_twin = {"mp": self.twin}
        self.to_near = {"dp": 2 * self.far + 1 - self.near}

    def other_far(self, step):
        return (self.far + step) % self.far_count

    def to_far(self, step):
        return {"dp": 2 * self.other_far(step) + self.near}

    def meet(self):
        barrier = pltpu.get_barrier_semaphore()
        partners = [self.to_far(step) for step in range(1, self.far_count)]
        partners += [self.to_near, self.to_beside, self.to_twin]
        for partner in partners:
            pl.semaphore_signal(barrier, inc=1, device_id=partner, device_id_type=MESH)
        pl.semaphore_wait(barrier, len(partners))


class Wires:
    def __init__(self, send_sems, recv_sems):
        self.sems = (send_sems, recv_sems)
        self.used = 0

    def copy(self, source, target, partner):
        index = self.used
        self.used += 1
        return pltpu.make_async_remote_copy(
            src_ref=source,
            dst_ref=target,
            send_sem=self.sems[0].at[index],
            recv_sem=self.sems[1].at[index],
            device_id=partner,
            device_id_type=MESH,
        )


def start_all(copies):
    for copy in copies:
        copy.start()


def wait_all(copies):
    for copy in copies:
        copy.wait()


def columns(index, size):
    return pl.ds(pl.multiple_of(index * size, size), size)


class Chunk:
    def __init__(self, rows, cols, row_size, col_size):
        self.rows, self.cols, self.row_size, self.col_size = rows, cols, row_size, col_size

    def columns(self, index):
        offset = pl.multiple_of(index * self.col_size + self.cols[0], math.gcd(self.col_size, max(self.cols[0], 128)))
        return pl.ds(offset, self.cols[1])

    @property
    def row_window(self):
        return pl.ds(*self.rows)

    @property
    def shape(self):
        return self.rows[1], self.cols[1]


def whole_chunk(rows, cols):
    return Chunk((0, rows), (0, cols), rows, cols)


class Staged:
    def __init__(self, active, twin_stage):
        self.active, self.twin_stage = active, twin_stage
        self.stages = []

    def start(self, number):
        copies = self.stages[number]
        if self.active is None:
            start_all(copies)
        elif number != self.twin_stage:
            pl.when(self.active)(lambda: start_all(copies))
        else:
            pl.when(self.sends)(lambda: start_all(copies))

    def wait(self, number):
        copies = self.stages[number]
        if self.active is None:
            wait_all(copies)
        elif number != self.twin_stage:
            pl.when(self.active)(lambda: wait_all(copies))
        else:

            @pl.when(self.sends)
            def _():
                for copy in copies:
                    copy.wait_send()

            @pl.when(jnp.logical_not(self.sends))
            def _():
                for copy in copies:
                    copy.wait_recv()


class Gather(Staged):
    def __init__(self, wires, place, full, order, chunk, active=None):
        super().__init__(active, len(order) - 1)
        self.sends = active
        mine, side = chunk.columns(place.model), chunk.columns(place.beside)
        self.home = full.at[place.far, place.near, chunk.row_window, mine]
        fars, nears, cols = place.far, place.near, [mine]

        def send(col, partner):
            view = full.at[fars, nears, chunk.row_window, col]
            return wires.copy(view, view, partner)

        for letter in order:
            if letter == "x":
                self.stages.append([send(mine, place.to_beside)])
                cols = [mine, side]
            elif letter == "y":
                self.stages.append([send(col, place.to_near) for col in cols])
                nears = slice(None)
            elif letter == "c":
                self.stages.append([send(col, place.to_twin) for col in cols])
            else:
                ways = [place.to_far(step) for step in range(1, place.far_count)]
                self.stages.append([send(col, way) for col in cols for way in ways])
                fars = slice(None)

    def begin(self):
        self.start(0)

    def advance(self, number):
        self.wait(number)
        if number + 1 < len(self.stages):
            self.start(number + 1)


GATHER_STEPS = 4


def gather_copies(far_count):
    return far_count + 6


def reduce_plan(order, far_count, rows, cols):
    slots, nears, fars = 2, 2, far_count
    plan = []
    for letter in order:
        if letter == "x":
            plan.append((letter, slots, nears, fars, (nears, fars, rows, cols)))
            slots = 1
        elif letter == "y":
            plan.append((letter, slots, nears, fars, (slots, fars, rows, cols)))
            nears = 1
        else:
            plan.append((letter, slots, nears, fars, (far_count, slots, nears, rows, cols)))
            fars = 1
    return plan


REDUCE_BUFFERS = 8
REDUCE_STEPS = 4


def reduce_copies(far_count):
    return far_count + 6


def reduce_scratch(order, far_count, rows, cols):
    shape = (2, 2, far_count, rows, cols)
    buffers = [pltpu.VMEM(shape, F32), pltpu.VMEM(shape, BF16)]
    for *_, shape in reduce_plan(order, far_count, rows, cols):
        buffers += [pltpu.VMEM(shape, BF16), pltpu.VMEM(shape, BF16)]
    return buffers


class Reducer(Staged):
    def __init__(self, wires, place, buffers, order, low=None, chunk=None, given=None, active=None):
        super().__init__(active, 0)
        self.sends = None if active is None else jnp.logical_not(active)
        self.place = place
        self.mine = None
        self.acc, self.got = buffers[:2]
        self.out, self.arrived = buffers[2::2], buffers[3::2]
        rows, size = self.acc.shape[-2:]
        self.plan = reduce_plan(order, place.far_count, rows, size)
        self.chunk = chunk
        self.kept = (place.model, place.beside)
        if given is not None:
            first = [wires.copy(given, self.got, place.to_twin)]
        else:
            twins = (place.twin, place.twin_beside)
            first = [
                wires.copy(
                    low.at[:, near, chunk.row_window, chunk.columns(twins[slot])],
                    self.got.at[slot, near],
                    place.to_twin,
                )
                for slot in range(2)
                for near in range(2)
            ]
        self.stages = [first]
        for (letter, *_), out, arrived in zip(self.plan, self.out, self.arrived):
            if letter == "z":
                stage = [
                    wires.copy(out.at[place.other_far(step)], arrived.at[step], place.to_far(step))
                    for step in range(1, place.far_count)
                ]
            else:
                stage = [wires.copy(out, arrived, place.to_beside if letter == "x" else place.to_near)]
            self.stages.append(stage)

    def loads(self, partial, mine, load_sems):
        self.mine = mine
        return [
            pltpu.make_async_copy(
                partial.at[:, near, self.chunk.row_window, self.chunk.columns(self.kept[slot])],
                mine.at[slot, near],
                load_sems.at[2 * slot + near],
            )
            for slot in range(2)
            for near in range(2)
        ]

    def begin(self):
        self.start(0)

    def held(self, number):
        letter, slots, nears, fars, _ = self.plan[number]
        place = self.place
        return (
            letter,
            range(slots),
            range(2) if nears == 2 else (place.near,),
            range(place.far_count) if fars > 1 else (place.far,),
        )

    def prepare(self, number):
        letter, slots, nears, fars = self.held(number)
        place, acc, out = self.place, self.acc, self.out[number]
        if letter == "x":
            for i, near in enumerate(nears):
                for j, far in enumerate(fars):
                    out[i, j] = acc[1, near, far].astype(BF16)
        elif letter == "y":
            for slot in slots:
                for j, far in enumerate(fars):
                    out[slot, j] = acc[slot, 1 - place.near, far].astype(BF16)
        else:
            for slot in slots:
                for i, near in enumerate(nears):
                    for far in fars:
                        out[far, slot, i] = acc[slot, near, far].astype(BF16)

    def absorb(self, number):
        letter, slots, nears, fars = self.held(number)
        place, acc, arrived = self.place, self.acc, self.arrived[number]
        if letter == "x":
            for i, near in enumerate(nears):
                for j, far in enumerate(fars):
                    acc[0, near, far] += arrived[i, j].astype(F32)
        elif letter == "y":
            for slot in slots:
                for j, far in enumerate(fars):
                    acc[slot, place.near, far] += arrived[slot, j].astype(F32)
        else:
            for slot in slots:
                for i, near in enumerate(nears):
                    total = acc[slot, near, place.far]
                    for step in range(1, place.far_count):
                        total = total + arrived[step, slot, i].astype(F32)
                    acc[slot, near, place.far] = total

    def advance(self, number):
        self.wait(number)

        def add():
            if number == 0:
                for slot in range(2):
                    for near in range(2):
                        for far in range(self.place.far_count):
                            spot = (slot, near, far)
                            own = self.acc[spot] if self.mine is None else self.mine[spot].astype(F32)
                            self.acc[spot] = own + self.got[spot].astype(F32)
            else:
                self.absorb(number - 1)
            if number < len(self.plan):
                self.prepare(number)

        if self.active is None:
            add()
        else:
            pl.when(self.active)(add)
        if number < len(self.plan):
            self.start(number + 1)

    def result(self):
        return self.acc[0, self.place.near, self.place.far]


class Spread:
    def __init__(self, wires, place, tile, stages, slots):
        self.place, self.tile, self.stages, self.slots = place, tile, stages, slots
        self.copies = [
            [wires.copy(tile, stages.at[number], partner)]
            for number, partner in enumerate((place.to_twin, place.to_beside, place.to_near))
        ]
        self.copies.append(
            [wires.copy(tile, slots.at[place.far], place.to_far(step)) for step in range(1, place.far_count)]
        )

    def begin(self):
        start_all(self.copies[0])

    def advance(self, number):
        wait_all(self.copies[number])
        if number == 3:
            self.slots[self.place.far] = self.tile[...]
            total = self.slots[0]
            for far in range(1, self.place.far_count):
                total = total + self.slots[far]
            self.tile[...] = total
        else:
            self.tile[...] += self.stages[number]
            start_all(self.copies[number + 1])


def spread_copies(far_count):
    return far_count - 1 + 3


def spread_scratch(far_count, shape):
    return [pltpu.VMEM(shape, F32), pltpu.VMEM((3,) + shape, F32), pltpu.VMEM((far_count,) + shape, F32)]


def any_spec():
    return pl.BlockSpec(memory_space=pl.ANY)


def vmem_spec():
    return pl.BlockSpec(memory_space=pltpu.VMEM)


def smem_spec():
    return pl.BlockSpec(memory_space=pltpu.SMEM)


def own_lanes(parity):
    lane = lax.broadcasted_iota(jnp.int32, (1, PAIR), 1)
    return (lane < DH) if parity == 0 else (lane >= DH)


def lane_in_half():
    return lax.broadcasted_iota(jnp.int32, (1, PAIR), 1) % DH


def blend(parity, own, extra):
    mine = jnp.where(own_lanes(parity), 1.0, 0.0)
    return own * mine.astype(BF16) + extra * (1.0 - mine).astype(BF16)


def slot_calls(step, width, calls):
    def at(sub_step):
        for slot, call in calls:
            if slot % width == sub_step:
                pl.when(step == slot // width)(call)

    return at


PROJECT_ORDERS = ("zxyc", "zyxc", "zxyc")
FORWARD_ORDERS = ("zxyc", "zyxc", "zyxc")
FORWARD_SLOTS = ((0, 8, 23), (0, 8, 24), (1, 9, 24))


def front_kernel(
    far_count,
    states_ref,
    states_any,
    attention_ref,
    inner_ref,
    outer_ref,
    lengths_ref,
    mixed_ref,
    qx_ref,
    extra_ref,
    weights_out,
    queries_out,
    keys_out,
    values_out,
    twin_out,
    inner_full,
    outer_full,
    wo_full,
    full,
    queries,
    keys,
    values,
    twin_states,
    twin_queries,
    inner_low,
    outer_low,
    wo_low,
    ka,
    va,
    score_a,
    score_b,
    send_sems,
    recv_sems,
    local_sems,
):
    rows = states_ref.shape[0]
    step = pl.program_id(0)
    here = Place(far_count)
    wires = Wires(send_sems, recv_sems)
    shard = full.shape[-2], full.shape[-1] // 4
    projections = [
        Gather(wires, here, full.at[member], PROJECT_ORDERS[member], whole_chunk(*shard)) for member in range(3)
    ]
    fulls, lows = (inner_full, outer_full, wo_full), (inner_low, outer_low, wo_low)
    gathers = [
        Gather(wires, here, target, order, whole_chunk(*low.shape))
        for target, low, order in zip(fulls, lows, FORWARD_ORDERS)
    ]
    fill = [
        pltpu.make_async_copy(low, gather.home, local_sems.at[number])
        for number, (low, gather) in enumerate(zip(lows, gathers))
    ]
    swap_states = wires.copy(states_any, twin_states, here.to_twin)
    swaps = []
    for number, block in enumerate((here.model, here.beside)):
        cols = columns(block, PAIR)
        for kept in (keys, values):
            for start, end in ((0, rows), (rows, 0)):
                swaps.append(
                    wires.copy(kept.at[pl.ds(start, rows), cols], kept.at[pl.ds(end, rows), cols], here.to_twin)
                )
        swaps.append(wires.copy(twin_queries.at[number], queries.at[:, cols], here.to_twin))
    outward = [
        pltpu.make_async_copy(source, target, local_sems.at[3 + number])
        for number, (source, target) in enumerate(
            ((queries, queries_out), (keys, keys_out), (values, values_out), (twin_states, twin_out), (full, weights_out))
        )
    ]

    @pl.when(step == 0)
    def _():
        for member in range(3):
            full[member, here.far, here.near, :, columns(here.model, shard[1])] = attention_ref[member].astype(BF16)
        inner_low[...] = inner_ref[...].astype(BF16)
        outer_low[...] = outer_ref[...].astype(BF16)
        wo_low[...] = attention_ref[3].astype(BF16)
        start_all(fill)
        here.meet()
        for gather in projections:
            gather.begin()
        swap_states.start()
        index = lax.broadcasted_iota(jnp.int32, (2 * rows, 1), 0)
        half = here.model % 2
        position = jnp.where(index < rows, index + half * rows, index - half * rows)
        bias = jnp.where(position < lengths_ref[here.side], 0.0, -1e30)
        lane = lane_in_half()
        extra_ref[...] = jnp.where(lane == 0, bias, jnp.where(lane <= 3, 1.0, 0.0)).astype(BF16)
        wait_all(fill)
        for gather in projections:
            gather.advance(0)
        for gather in gathers:
            gather.begin()
        for gather in projections:
            gather.advance(1)
        swap_states.wait()
        for gather in projections:
            gather.advance(2)
        for member, kept in ((1, keys), (2, values), (0, queries)):
            both = jnp.concatenate(
                [full[member, :, :, :, columns(block, PAIR)].reshape(D, PAIR) for block in (here.model, here.beside)],
                axis=1,
            )
            own = mm(states_ref[...], both).astype(BF16)
            twin = mm(twin_states[...], both).astype(BF16)
            if member == 0:
                own = (own * DH ** (-0.5)).astype(BF16)
                twin = (twin * DH ** (-0.5)).astype(BF16)
            for number, block in enumerate((here.model, here.beside)):
                cols = columns(block, PAIR)
                kept[:rows, cols] = own[:, number * PAIR : (number + 1) * PAIR]
                if member:
                    kept[rows:, cols] = twin[:, number * PAIR : (number + 1) * PAIR]
                else:
                    twin_queries[number] = twin[:, number * PAIR : (number + 1) * PAIR]
        start_all(swaps)

    @pl.when(step == 2)
    def _():
        wait_all(swaps)
        for gather in projections:
            gather.advance(3)
        start_all(outward)

    calls = [
        (slot, functools.partial(gather.advance, number))
        for gather, slots in zip(gathers, FORWARD_SLOTS)
        for number, slot in enumerate(slots)
    ]
    at = slot_calls(step, 2 * (rows // QUERY_ROWS), calls)
    pair_cols = columns(2 * (step % 2) + (step // 2 + here.core) % 2, PAIR)
    place = lane_in_half()
    first = jnp.where(place == 0, 1.0, 0.0).astype(BF16)
    ones = jnp.where(place <= 3, 1.0, 0.0).astype(BF16)
    for parity in range(2):
        ka[parity] = blend(parity, keys[:, pair_cols], extra_ref[...])
        va[parity] = blend(parity, values[:, pair_cols], ones)
    steps = [(parity, block) for block in range(rows // QUERY_ROWS) for parity in range(2)]
    scratch = (score_a, score_b)

    chunk = keys.shape[0] // FORWARD_CHUNKS

    def query_part(index):
        parity, block = steps[index]
        return blend(parity, queries[pl.ds(block * QUERY_ROWS, QUERY_ROWS), pair_cols], first)

    def score(index, part, number):
        window = pl.ds(number * chunk, chunk)
        scores = mm(ka[steps[index][0], window, :], part, NT)
        scratch[index % 2][window, :] = scores
        return jnp.max(scores, axis=0, keepdims=True)

    part = query_part(0)
    row_max = score(0, part, 0)
    for number in range(1, FORWARD_CHUNKS):
        row_max = jnp.maximum(row_max, score(0, part, number))
    held = [None, None]
    logs = [None, None]
    row = lax.broadcasted_iota(jnp.int32, (PAIR, 1), 0)
    for index, (parity, block) in enumerate(steps):
        at(index)
        more = index + 1 < len(steps)
        part = query_part(index + 1) if more else None
        product, next_max = None, None
        for number in range(FORWARD_CHUNKS):
            if more:
                found = score(index + 1, part, number)
                next_max = found if number == 0 else jnp.maximum(next_max, found)
            window = pl.ds(number * chunk, chunk)
            shifted = jnp.exp(scratch[index % 2][window, :] - row_max).astype(BF16)
            term = mm(va[parity, window, :], shifted, TN)
            product = term if number == 0 else product + term
        sum_row = DH if parity == 0 else 0
        total = product[sum_row : sum_row + 1, :]
        held[parity] = product / total
        logs[parity] = row_max + jnp.log(total)
        row_max = next_max
        if parity == 1:
            window = pl.ds(block * QUERY_ROWS, QUERY_ROWS)
            both = jnp.concatenate([held[0][:DH], held[1][DH:]], axis=0)
            mixed_ref[window, pair_cols] = both.T
            parts = split3(-jnp.where(row < DH, logs[1], logs[0]))
            spot = row % DH
            extra = jnp.where(spot == 0, 1.0, 0.0)
            for number, part in enumerate(parts):
                extra = jnp.where(spot == number + 1, part, extra)
            qx_ref[window, pair_cols] = extra.T.astype(BF16)

    @pl.when(step == pl.num_programs(0) - 1)
    def _():
        for gather in gathers:
            gather.advance(GATHER_STEPS - 1)
        wait_all(outward)


def once(shape):
    return pl.BlockSpec(shape, lambda j: (0,) * len(shape), pipeline_mode=pl.Buffered(1))


def front(states, attention_weights, inner_shard, outer_shard, lengths, far_count):
    rows, width = states.shape
    total = 2 * rows
    shard_rows = attention_weights.shape[1]
    fulls = [
        jax.ShapeDtypeStruct((far_count, 2, height, wide), BF16)
        for height, wide in ((inner_shard.shape[0], FF), (outer_shard.shape[0], D), (shard_rows, D))
    ]
    copies = 6 * gather_copies(far_count) + 11
    weights_shape = (3, far_count, 2, shard_rows, D)
    return pl.pallas_call(
        functools.partial(front_kernel, far_count),
        name="front",
        grid=(width // PAIR,),
        in_specs=[once(states.shape), any_spec()]
        + [once(item.shape) for item in (attention_weights, inner_shard, outer_shard)]
        + [smem_spec()],
        out_specs=[once((rows, width)), once((rows, width)), once((total, PAIR))] + [any_spec()] * 8,
        out_shape=[
            jax.ShapeDtypeStruct((rows, width), F32),
            jax.ShapeDtypeStruct((rows, width), BF16),
            jax.ShapeDtypeStruct((total, PAIR), BF16),
            jax.ShapeDtypeStruct(weights_shape, BF16),
            jax.ShapeDtypeStruct((rows, width), BF16),
            jax.ShapeDtypeStruct((total, width), BF16),
            jax.ShapeDtypeStruct((total, width), BF16),
            jax.ShapeDtypeStruct((rows, width), BF16),
        ]
        + fulls,
        scratch_shapes=[
            pltpu.VMEM(weights_shape, BF16),
            pltpu.VMEM((rows, width), BF16),
            pltpu.VMEM((total, width), BF16),
            pltpu.VMEM((total, width), BF16),
            pltpu.VMEM((rows, width), BF16),
            pltpu.VMEM((2, rows, PAIR), BF16),
            pltpu.VMEM(inner_shard.shape, BF16),
            pltpu.VMEM(outer_shard.shape, BF16),
            pltpu.VMEM(attention_weights.shape[1:], BF16),
            pltpu.VMEM((2, total, PAIR), BF16),
            pltpu.VMEM((2, total, PAIR), BF16),
            pltpu.VMEM((total, QUERY_ROWS), F32),
            pltpu.VMEM((total, QUERY_ROWS), F32),
            pltpu.SemaphoreType.DMA((copies,)),
            pltpu.SemaphoreType.DMA((copies,)),
            pltpu.SemaphoreType.DMA((8,)),
        ],
        compiler_params=pltpu.CompilerParams(
            vmem_limit_bytes=VMEM_LIMIT, collective_id=1, has_side_effects=True
        ),
    )(states, states, attention_weights, inner_shard, outer_shard, lengths)


EARLY = (
    (0, 0, "yxz", "zxyc"),
    (1, 0, "xyz", "zyxc"),
    (2, None, "xyz", "zyxc"),
    (0, 1, "yxz", "zxyc"),
    (1, 1, "xyz", "zyxc"),
)
LATE_REDUCE = ("yxz", "xyz", "yxz")
LATE_GATHER = ("zxyc", "zyxc", "zxyc")
SCHEDULE = (
    (0, 0, 0), (0, 1, 0), (5, 0, 1), (5, 1, 1), (11, 0, 2), (11, 1, 2),
    (11, 2, 0), (11, 3, 0), (11, 4, 0), (15, 2, 1), (16, 0, 3), (16, 1, 3),
    (16, 3, 1), (16, 4, 1), (18, 2, 2), (19, 5, 1), (19, 6, 1), (19, 7, 1),
    (21, 0, 4), (21, 1, 4), (23, 2, 3), (23, 4, 2), (23, 6, 2), (24, 3, 2),
    (24, 5, 2), (24, 7, 2), (26, 0, 5), (26, 1, 5), (26, 2, 4), (26, 6, 3),
    (27, 4, 3), (28, 5, 3), (28, 7, 3), (29, 6, 4), (30, 1, 6), (30, 2, 5),
    (30, 3, 3), (31, 0, 6), (31, 5, 4), (31, 7, 4), (32, 6, 5), (32, 4, 4),
    (32, 2, 6), (32, -1, 0), (32, -1, 1), (32, 5, 5), (32, 7, 5), (32, 3, 4),
    (32, 10, 1), (32, 8, 1), (32, 9, 1), (32, 6, 6), (32, 1, 7), (32, 4, 5),
    (32, 0, 7), (32, 5, 6), (32, 7, 6), (32, 3, 5), (32, 1, 8), (32, 2, 7),
    (32, 10, 2), (32, 8, 2), (32, 0, 8), (32, 6, 7), (32, 9, 2), (32, 2, 8),
    (32, 6, 8), (32, 10, 3), (32, 8, 3), (32, 5, 7), (32, 7, 7), (32, 3, 6),
    (32, 4, 6), (32, 9, 3), (32, 10, 4), (32, 8, 4), (32, 5, 8), (32, 7, 8),
    (32, 9, 4), (32, -1, 11), (32, 10, 5), (32, 8, 5), (32, -1, 12), (32, 9, 5),
    (32, 3, 7), (32, 4, 7), (32, -1, 13), (32, 10, 6), (32, 8, 6), (32, 9, 6),
    (32, -1, 14), (32, 3, 8), (32, 4, 8), (32, -1, 2), (32, -1, 3), (32, -1, 4),
    (32, 10, 7), (32, 8, 7), (32, 9, 7), (32, -1, 15), (32, -1, 5), (32, -1, 6),
    (32, -1, 7), (32, -1, 8), (32, -1, 9), (32, 10, 8), (32, 8, 8), (32, 9, 8),
    (32, -1, 10),
)
NORM_SLOTS = (4, 7, 12, 16)


def early_chunks(shapes):
    chunks = []
    for array, half, *_ in EARLY:
        rows, cols = shapes[array]
        if half is None:
            chunks.append(whole_chunk(rows, cols))
        elif array == 0:
            chunks.append(Chunk((0, rows), (half * cols // 2, cols // 2), rows, cols))
        else:
            chunks.append(Chunk((half * rows // 2, rows // 2), (0, cols), rows, cols))
    return chunks


def product_steps(grad, left_root, right_root, place, counts, left_out, right_out, update_out, room, held):
    data_count, model_count = counts
    far_count, _, shard_rows, width = grad.shape
    height = data_count * shard_rows
    part = far_count // model_count
    size = width // model_count
    share = width // data_count

    def left():
        rows_here = grad[place.far, place.near]
        rows_there = grad[pl.ds(place.model * part, part)].reshape(height // model_count, width)
        left_out[...] = mm(rows_here, rows_there, NT)

    def right():
        cols_there = grad[:, :, :, columns(place.model, size)].reshape(height, size)
        if share % 128 == 0:
            cols_here = grad[:, :, :, columns(place.data_rank, share)].reshape(height, share)
            right_out[...] = mm(cols_here, cols_there, TN)
        else:
            group = data_count // model_count
            cols_here = grad[:, :, :, columns(place.data_rank // group, size)].reshape(height, size)
            room[:size, :size] = mm(cols_here, cols_there, TN)
            window = pl.ds(pl.multiple_of((place.data_rank % group) * share, share), share)
            right_out[...] = room[window, :size]

    def once():
        whole = grad[...].reshape(height, width)
        high, low = split2(left_root[...])
        held[...] = mm(high, whole) + mm(low, whole)

    def twice():
        chunk = min(512, width)
        total = jnp.zeros(update_out.shape, F32)
        for start in range(0, width, chunk):
            high, low = split2(held[:, start : start + chunk])
            root_high, root_low = split2(right_root[start : start + chunk, :])
            total = total + (mm(high, root_high) + mm(high, root_low) + mm(low, root_high))
        update_out[...] = total

    return [left, right, once, twice]


def backward_kernel(
    far_count,
    counts,
    inv_tokens,
    q_ref,
    qx_ref,
    k_ref,
    v_ref,
    kx_ref,
    do_ref,
    dox_ref,
    own_states,
    twin_states,
    weights_ref,
    norm_raw,
    skip_any,
    inner_low,
    outer_low,
    wo_low,
    *rest,
):
    roots_any, rest = rest[:6], rest[6:]
    (inner_piece, outer_piece, wo_piece, norm_total, late_out, squares_out, own_any, twin_in), rest = rest[:8], rest[8:]
    products, rest = rest[:9], rest[9:]
    (qa, da, ka, va, dqt, dq, dk, dv, states_t, late_low, own_sum, twin_out), rest = rest[:12], rest[12:]
    mine, rest = rest[: len(EARLY)], rest[len(EARLY) :]
    count = len(EARLY) * REDUCE_BUFFERS
    early_buffers, rest = rest[:count], rest[count:]
    late_buffers, rest = rest[: 3 * REDUCE_BUFFERS], rest[3 * REDUCE_BUFFERS :]
    roots, rest = rest[:6], rest[6:]
    (attention_full, inner_full, outer_full, room, held_small, held_wide, held_tall), rest = rest[:7], rest[7:]
    tile, tile_stages, tile_slots, norm_tile, norm_stages, norm_slots = rest[:6]
    send_sems, recv_sems, load_sems, local_sems = rest[6:]

    step = pl.program_id(0)
    rows = q_ref.shape[0]
    total = k_ref.shape[0]
    place = Place(far_count)
    wires = Wires(send_sems, recv_sems)
    lows = (inner_low, outer_low, wo_low)
    pieces = (inner_piece, outer_piece, wo_piece)
    fulls = (inner_full, outer_full, attention_full.at[3])
    chunks = early_chunks([piece.shape for piece in pieces])
    reducers = []
    gathers = []
    loads = []
    for number, (array, _, reduce_order, gather_order) in enumerate(EARLY):
        buffers = early_buffers[number * REDUCE_BUFFERS : (number + 1) * REDUCE_BUFFERS]
        reducer = Reducer(wires, place, buffers, reduce_order, low=lows[array], chunk=chunks[number])
        reducers.append(reducer)
        loads.append(reducer.loads(lows[array], mine[number], load_sems.at[number]))
        gathers.append(Gather(wires, place, fulls[array], gather_order, chunks[number]))
    late_shape = wo_piece.shape
    late_reducers = []
    late_gathers = []
    for late_set in range(2):
        active = place.core == late_set
        late_reducers.append(
            [
                Reducer(
                    wires,
                    place,
                    late_buffers[member * REDUCE_BUFFERS : (member + 1) * REDUCE_BUFFERS],
                    LATE_REDUCE[member],
                    given=late_low.at[member],
                    active=active,
                )
                for member in range(3)
            ]
        )
        late_gathers.append(
            [
                Gather(
                    wires, place, attention_full.at[member], LATE_GATHER[member], whole_chunk(*late_shape), active=active
                )
                for member in range(3)
            ]
        )
    norms = Spread(wires, place, norm_tile, norm_stages, norm_slots)
    squares = Spread(wires, place, tile, tile_stages, tile_slots)
    swap = wires.copy(twin_out, twin_in, place.to_twin)
    fetch = [
        pltpu.make_async_copy(source, target, local_sems.at[number])
        for number, (source, target) in enumerate(zip((*roots_any, skip_any), (*roots, own_sum)))
    ]
    outward = pltpu.make_async_copy(own_sum, own_any, local_sems.at[0])

    def early_call(number, number_of_step):
        array, chunk = EARLY[number][0], chunks[number]
        if number_of_step == 0:

            def call():
                reducers[number].begin()
                start_all(loads[number])

        elif number_of_step <= REDUCE_STEPS:

            def call():
                if number_of_step == 1:
                    wait_all(loads[number])
                reducers[number].advance(number_of_step - 1)
                if number_of_step == REDUCE_STEPS:
                    piece = reducers[number].result() * inv_tokens
                    pieces[array][chunk.row_window, pl.ds(*chunk.cols)] = piece
                    gathers[number].home[...] = piece.astype(BF16)
                    gathers[number].begin()

        else:

            def call():
                gathers[number].advance(number_of_step - REDUCE_STEPS - 1)

        return call

    def late_products():
        slot = (step + place.side) % 2
        wide = jnp.concatenate([dk[:, pair_cols], dv[:, pair_cols]], axis=1)
        both = mm(states_t[...], wide)
        values = (mm(states_t[:, :rows], dq[:, pair_cols]), both[:, :PAIR], both[:, PAIR:])
        active = place.core == step // 2
        for member, value in enumerate(values):
            parts = value.reshape(far_count, 2, *late_shape)

            @pl.when(active)
            def _():
                for near in range(2):
                    late_reducers[0][member].acc[slot, near] = parts[:, near]

            @pl.when(jnp.logical_not(active))
            def _():
                for near in range(2):
                    late_low[member, slot, near] = parts[:, near].astype(BF16)

    def late_call(late_set, member, number_of_step):
        reducer, gather = late_reducers[late_set][member], late_gathers[late_set][member]
        if number_of_step == 0:
            return reducer.begin

        def call():
            if number_of_step <= REDUCE_STEPS:
                reducer.advance(number_of_step - 1)
                if number_of_step == REDUCE_STEPS:

                    @pl.when(place.core == late_set)
                    def _():
                        piece = reducer.result() * inv_tokens
                        late_out[member] = piece
                        gather.home[...] = piece.astype(BF16)

                    gather.begin()
            else:
                gather.advance(number_of_step - REDUCE_STEPS - 1)

        return call

    def scheduled(chain, number_of_step):
        if chain < len(EARLY):
            return early_call(chain, number_of_step)
        return late_call(*divmod(chain - len(EARLY), 3), number_of_step)

    sub_steps = 4 * (total // KEY_ROWS)
    calls = [(slot, scheduled(chain, number)) for slot, chain, number in SCHEDULE if slot < sub_steps]
    calls += [(slot, functools.partial(norms.advance, stage)) for stage, slot in enumerate(NORM_SLOTS)]
    calls.append((12, lambda: start_all(fetch)))
    at = slot_calls(step, total // KEY_ROWS, calls)

    @pl.when(step == 0)
    def _():
        norm_tile[...] = norm_raw[...]
        place.meet()
        norms.begin()
        states_t[:, :rows] = own_states[...].T
        states_t[:, rows:] = twin_states[...].T

    lane = lane_in_half()
    ones = jnp.where(lane <= 3, 1.0, 0.0).astype(BF16)
    for parity in range(2):
        ka[parity] = blend(parity, k_ref[...], kx_ref[...])
        va[parity] = blend(parity, v_ref[...], ones)
        qa[parity] = blend(parity, q_ref[...], qx_ref[...])
        da[parity] = blend(parity, do_ref[...], dox_ref[...])
    dqt[...] = jnp.zeros_like(dqt)
    pair = 2 * (step % 2) + step // 2
    pair_cols = columns(pair, PAIR)
    for block in range(total // KEY_ROWS):
        at(block)
        window = pl.ds(block * KEY_ROWS, KEY_ROWS)
        key_grads = []
        value_grads = []
        for parity in range(2):
            key_block = ka[parity, window, :]
            probs = jnp.exp(mm(key_block, qa[parity], NT))
            d_probs = mm(va[parity, window, :], da[parity], NT)
            d_scores = (probs * d_probs).astype(BF16)
            value_grads.append(mm(probs.astype(BF16), da[parity]))
            key_grads.append(mm(d_scores, qa[parity]))
            dqt[parity] += mm(key_block, d_scores, TN)
        dk[window, pair_cols] = jnp.where(own_lanes(0), key_grads[0], key_grads[1]).astype(BF16)
        dv[window, pair_cols] = jnp.where(own_lanes(0), value_grads[0], value_grads[1]).astype(BF16)
    both = jnp.concatenate([dqt[0, :DH], dqt[1, DH:]], axis=0) * DH ** (-0.5)
    dq[:, pair_cols] = both.T.astype(BF16)

    late_products()
    for late_set in range(2):

        @pl.when(step == 2 * late_set + 1)
        def _():
            for member in range(3):
                late_call(late_set, member, 0)()

    @pl.when(step == pl.num_programs(0) - 1)
    def _():
        part = 256

        def twin_share():
            @pl.loop(0, rows // part)
            def _(block):
                window = pl.ds(pl.multiple_of(block * part, part), part)
                there = pl.ds(pl.multiple_of(rows + block * part, part), part)
                value = mm(dk[there, :], weights_ref[1], NT) + mm(dv[there, :], weights_ref[2], NT)
                twin_out[window, :] = value.astype(BF16)

            swap.start()

        def own_share():
            wait_all(fetch)

            @pl.loop(0, rows // part)
            def _(block):
                window = pl.ds(pl.multiple_of(block * part, part), part)
                own_sum[window, :] += (
                    mm(dq[window, :], weights_ref[0], NT)
                    + mm(dk[window, :], weights_ref[1], NT)
                    + mm(dv[window, :], weights_ref[2], NT)
                )

            outward.start()

        common = (place, counts)
        inner_steps = product_steps(inner_full, roots[2], roots[3], *common, *products[3:6], room, held_wide)
        outer_steps = product_steps(outer_full, roots[4], roots[5], *common, *products[6:9], room, held_tall)

        def member_products():
            @pl.loop(0, 4)
            def _(member):
                steps = product_steps(
                    attention_full.at[member],
                    roots[0].at[member],
                    roots[1].at[member],
                    *common,
                    *[product.at[member] for product in products[:3]],
                    room,
                    held_small,
                )
                for call in steps:
                    call()

        work = [twin_share, own_share, *outer_steps, *inner_steps, member_products]

        def square(piece):
            return jnp.sum(jnp.sum(piece * piece, axis=0, keepdims=True), axis=1, keepdims=True)

        def squares_begin():
            square_sum = square(inner_piece[...]) + square(outer_piece[...]) + square(wo_piece[...])
            for member in range(3):
                square_sum = square_sum + square(late_out[member])
            tile[...] = jnp.broadcast_to(square_sum, tile.shape)
            squares.begin()

        work.append(squares_begin)
        work += [functools.partial(squares.advance, stage) for stage in range(4)]
        for slot, chain, number in SCHEDULE:
            if slot >= sub_steps:
                (work[number] if chain < 0 else scheduled(chain, number))()
        squares_out[...] = tile[...]
        norm_total[...] = norm_tile[...] * inv_tokens
        swap.wait()
        outward.wait()


def backward(
    queries,
    query_extra,
    keys,
    values,
    key_extra,
    d_mixed,
    d_extra,
    states,
    twin_states,
    weights,
    norm_rows,
    skip,
    lows,
    roots,
    counts,
):
    rows, width = queries.shape
    total = keys.shape[0]
    data_count, model_count = counts
    far_count = data_count // 2

    def by_pair(height):
        return pl.BlockSpec((height, PAIR), lambda j: (0, 2 * (j % 2) + j // 2))

    whole = once

    def seen(array):
        return array.reshape(far_count, 2, array.shape[0] // data_count, array.shape[1])

    def products(lead, height, wide):
        return [
            jax.ShapeDtypeStruct(lead + shape, F32)
            for shape in (
                (height // data_count, height // model_count),
                (wide // data_count, wide // model_count),
                (height // data_count, wide // model_count),
            )
        ]

    pieces = [(low.shape[0] // data_count, low.shape[1] // model_count) for low in lows]
    late = pieces[2]
    tile = (8, 128)
    out_shape = [jax.ShapeDtypeStruct(piece, F32) for piece in pieces]
    out_shape += [
        jax.ShapeDtypeStruct(norm_rows.shape, F32),
        jax.ShapeDtypeStruct((3,) + late, F32),
        jax.ShapeDtypeStruct(tile, F32),
        jax.ShapeDtypeStruct((rows, width), F32),
        jax.ShapeDtypeStruct((rows, width), BF16),
    ]
    out_specs = [whole(item.shape) for item in out_shape[:6]] + [any_spec()] * 2
    tail = products((4,), D, D) + products((), D, FF) + products((), FF, D)
    out_shape += tail
    out_specs += [whole(item.shape) for item in tail]
    shard_rows = D // data_count
    scratch = [
        pltpu.VMEM((2, rows, PAIR), BF16),
        pltpu.VMEM((2, rows, PAIR), BF16),
        pltpu.VMEM((2, total, PAIR), BF16),
        pltpu.VMEM((2, total, PAIR), BF16),
        pltpu.VMEM((2, PAIR, rows), F32),
        pltpu.VMEM((rows, width), BF16),
        pltpu.VMEM((total, width), BF16),
        pltpu.VMEM((total, width), BF16),
        pltpu.VMEM((width, total), BF16),
        pltpu.VMEM((3, 2, 2, far_count) + late, BF16),
        pltpu.VMEM((rows, width), F32),
        pltpu.VMEM((rows, width), BF16),
    ]
    scratch += [pltpu.VMEM((2, 2, far_count) + chunk.shape, BF16) for chunk in early_chunks(pieces)]
    for (_, _, order, _), chunk in zip(EARLY, early_chunks(pieces)):
        scratch += reduce_scratch(order, far_count, *chunk.shape)
    for member in range(3):
        scratch += reduce_scratch(LATE_REDUCE[member], far_count, *late)
    scratch += [pltpu.VMEM(root.shape, F32) for root in roots]
    scratch += [
        pltpu.VMEM((4, far_count, 2, shard_rows, D), BF16),
        pltpu.VMEM((far_count, 2, shard_rows, FF), BF16),
        pltpu.VMEM((far_count, 2, FF // data_count, D), BF16),
        pltpu.VMEM((FF // model_count, FF // model_count), F32),
        pltpu.VMEM((shard_rows, D), F32),
        pltpu.VMEM((shard_rows, FF), F32),
        pltpu.VMEM((FF // data_count, D), F32),
    ]
    scratch += spread_scratch(far_count, tile) + spread_scratch(far_count, norm_rows.shape)
    chains = len(EARLY) + 6
    copies = chains * (reduce_copies(far_count) + gather_copies(far_count)) + 2 * spread_copies(far_count) + 1
    scratch += [
        pltpu.SemaphoreType.DMA((copies,)),
        pltpu.SemaphoreType.DMA((copies,)),
        pltpu.SemaphoreType.DMA((len(EARLY), 4)),
        pltpu.SemaphoreType.DMA((7,)),
    ]
    return pl.pallas_call(
        functools.partial(backward_kernel, far_count, counts, 1.0 / (rows * data_count * model_count)),
        name="backward",
        grid=(width // PAIR,),
        in_specs=[by_pair(rows), by_pair(rows), by_pair(total), by_pair(total), whole((total, PAIR))]
        + [by_pair(rows), by_pair(rows), whole((rows, width)), whole((rows, width))]
        + [whole(weights.shape), whole(norm_rows.shape)]
        + [any_spec()] * 10,
        out_specs=out_specs,
        out_shape=out_shape,
        scratch_shapes=scratch,
        compiler_params=pltpu.CompilerParams(
            vmem_limit_bytes=BACKWARD_VMEM, collective_id=2, has_side_effects=True
        ),
    )(
        queries,
        query_extra,
        keys,
        values,
        key_extra,
        d_mixed,
        d_extra,
        states,
        twin_states,
        weights,
        norm_rows,
        skip,
        *[seen(low) for low in lows],
        *roots,
    )


def finish_kernel(limit, rate, squares_ref, norm_ref, own_ref, twin_ref, late_ref, *rest):
    (inner_piece, outer_piece, wo_piece, gains_ref, biases_ref), rest = rest[:5], rest[5:]
    stats, rest = rest[:6], rest[6:]
    products, rest = rest[:6], rest[6:]
    weights, rest = rest[:3], rest[3:]
    updates, rest = rest[:3], rest[3:]
    (states_out, norm_out, attention_grad, inner_grad, outer_grad, norm_grad), rest = rest[:6], rest[6:]
    weights_new, norm_new, stats_new = rest[:3], rest[3], rest[4:]
    norms = norm_ref[0:4, :]
    norm_square = jnp.sum(jnp.sum(norms * norms, axis=0, keepdims=True), axis=1, keepdims=True)
    grad_norm = jnp.sqrt(squares_ref[0:1, 0:1] + norm_square)
    norm_out[...] = grad_norm
    factor = jnp.minimum(1.0, limit / grad_norm)
    states_out[...] = (own_ref[...] + twin_ref[...].astype(F32)).astype(BF16)
    for member in range(3):
        attention_grad[member] = late_ref[member] * factor
    attention_grad[3] = wo_piece[...] * factor
    inner_grad[...] = inner_piece[...] * factor
    outer_grad[...] = outer_piece[...] * factor
    share = norm_grad.shape[-1]
    start = (lax.axis_index("dp") * lax.axis_size("mp") + lax.axis_index("mp")) * share
    params = jnp.concatenate([gains_ref[...], biases_ref[...]], axis=0)
    row = lax.broadcasted_iota(jnp.int32, (4, 1), 0) == start // D

    def share_of(table):
        picked = jnp.sum(jnp.where(row, table, 0.0), axis=0, keepdims=True)
        return pltpu.roll(jnp.broadcast_to(picked, (8, D)), (D - start % D) % D, 1)[0:1, :share]

    clipped = share_of(norms) * factor
    norm_grad[...] = clipped
    norm_new[...] = share_of(params) - rate * clipped
    for weight, change, out in zip(weights, updates, weights_new):
        out[...] = weight[...] - (step_rate * factor) * change[...]
    for stat, product, out in zip(stats, products, stats_new):
        out[...] = 0.5 * stat[...] + (0.5 * factor * factor) * product[...]


def finish(token_total, norm_share, squares, norm_rows, own, twin, late, pieces, gains, biases, stats, products, weights, updates):
    limit = 0.01 * math.sqrt((4 * D * D + 2 * D * FF + 4 * D) / token_total)
    rate = 20.0 * math.sqrt(token_total)
    inner_piece, outer_piece, _ = pieces
    shapes = [
        jax.ShapeDtypeStruct(own.shape, BF16),
        jax.ShapeDtypeStruct((1, 1), F32),
        jax.ShapeDtypeStruct(weights[0].shape, F32),
        jax.ShapeDtypeStruct(inner_piece.shape, F32),
        jax.ShapeDtypeStruct(outer_piece.shape, F32),
        jax.ShapeDtypeStruct((1, norm_share), F32),
    ]
    shapes += [jax.ShapeDtypeStruct(weight.shape, F32) for weight in weights]
    shapes.append(jax.ShapeDtypeStruct((1, norm_share), F32))
    shapes += [jax.ShapeDtypeStruct(stat.shape, F32) for stat in stats]
    operands = (squares, norm_rows, own, twin, late, *pieces, gains, biases)
    operands += (*stats, *products, *weights, *updates)
    return pl.pallas_call(
        functools.partial(finish_kernel, limit, rate),
        name="finish",
        in_specs=[vmem_spec()] * len(operands),
        out_specs=[vmem_spec()] * len(shapes),
        out_shape=shapes,
        compiler_params=pltpu.CompilerParams(vmem_limit_bytes=VMEM_LIMIT),
    )(*operands)


def middle_kernel(
    mixed_ref,
    states_ref,
    cotangent_ref,
    halting_ref,
    wo_ref,
    inner_ref,
    outer_ref,
    gains_ref,
    biases_ref,
    out_ref,
    dm_ref,
    dx_ref,
    skip_ref,
    norm_raw,
    inner_low,
    outer_low,
    wo_low,
    gelu_slope,
    activated_ref,
    d_inner_ref,
    normed_ref,
    branch_ref,
    attended_ref,
    mixed_low_ref,
):
    step = pl.program_id(0)
    tokens = pl.ds(pl.multiple_of(step * TOKEN_ROWS, TOKEN_ROWS), TOKEN_ROWS)
    head_row = lax.broadcasted_iota(jnp.int32, (D, D), 0) // DH
    head_col = lax.broadcasted_iota(jnp.int32, (D, D), 1) // DH
    swap = jnp.where(head_row + 1 - 2 * (head_row % 2) == head_col, 1.0, 0.0).astype(BF16)

    def mean(value):
        return jnp.mean(value, axis=-1, keepdims=True)

    def total(value):
        return jnp.sum(value, axis=0, keepdims=True)

    def normalize(residual):
        centered = residual - mean(residual)
        scale = lax.rsqrt(mean(centered * centered) + epsilon)
        return centered * scale, scale

    def norm_back(d_out, gain, unit, scale):
        d_unit = d_out * gain
        return (d_unit - mean(d_unit) - unit * mean(d_unit * unit)) * scale

    mixed = mixed_ref[...]
    mixed_low = mixed.astype(BF16)
    hidden = states_ref[...].astype(F32)
    upstream = cotangent_ref[...].astype(F32)
    table = halting_ref[...].astype(F32).T
    lane = lax.broadcasted_iota(jnp.int32, (1, table.shape[1]), 1)
    here = step * (TOKEN_ROWS // 128)
    flags = [
        jnp.sum(jnp.where(lane == here + row, table, 0.0), axis=1, keepdims=True) for row in range(TOKEN_ROWS // 128)
    ]
    running = jnp.concatenate(flags, axis=0) == 1.0
    gain1, gain2 = gains_ref[0:1, :], gains_ref[1:2, :]
    unit1, scale1 = normalize(hidden + mm(mixed_low, wo_ref[...]))
    normed = unit1 * gain1 + biases_ref[0:1, :]
    normed_low = normed.astype(BF16)
    rate = math.sqrt(2.0 / math.pi)
    parts = [pl.ds(start, FF_PART) for start in range(0, FF, FF_PART)]
    branch = None
    inner = mm(normed_low, inner_ref[:, parts[0]])
    for number, part in enumerate(parts):
        ahead = mm(normed_low, inner_ref[:, parts[number + 1]]) if number + 1 < len(parts) else None
        square = inner * inner
        bend = jnp.tanh(rate * inner * (1.0 + 0.044715 * square))
        half = 0.5 * (1.0 + bend)
        value = (inner * half).astype(BF16)
        activated_ref[tokens, part] = value
        gelu_slope[:, part] = half + 0.5 * inner * (1.0 - bend * bend) * (rate * (1.0 + 3 * 0.044715 * square))
        term = mm(value, outer_ref[part, :])
        branch = term if number == 0 else branch + term
        inner = ahead
    unit2, scale2 = normalize(normed + branch)
    final = unit2 * gain2 + biases_ref[1:2, :]
    out_ref[...] = jnp.where(running, final, hidden).astype(BF16)
    d_final = jnp.where(running, upstream, 0.0)
    d_resid2 = norm_back(d_final, gain2, unit2, scale2)
    d_branch = d_resid2.astype(BF16)
    d_normed = d_resid2
    d_act = mm(d_branch, outer_ref[parts[0], :], NT)
    for number, part in enumerate(parts):
        ahead = mm(d_branch, outer_ref[parts[number + 1], :], NT) if number + 1 < len(parts) else None
        d_inner = (d_act * gelu_slope[:, part]).astype(BF16)
        d_inner_ref[tokens, part] = d_inner
        d_normed = d_normed + mm(d_inner, inner_ref[:, part], NT)
        d_act = ahead
    d_resid1 = norm_back(d_normed, gain1, unit1, scale1)
    d_attended = d_resid1.astype(BF16)
    normed_ref[tokens, :] = normed_low
    branch_ref[tokens, :] = d_branch
    attended_ref[tokens, :] = d_attended
    mixed_low_ref[tokens, :] = mixed_low
    d_mixed = mm(d_attended, wo_ref[...], NT).astype(BF16)
    dm_ref[...] = d_mixed
    skip_ref[...] = jnp.where(running, 0.0, upstream) + d_resid1

    @pl.when(step == 0)
    def _():
        norm_raw[...] = jnp.zeros_like(norm_raw)

    norm_raw[0:1, :] += total(d_normed * unit1)
    norm_raw[1:2, :] += total(d_final * unit2)
    norm_raw[2:3, :] += total(d_normed)
    norm_raw[3:4, :] += total(d_final)
    high, low = split2(d_mixed.astype(F32) * mixed)
    delta = mm(high, swap) + mm(low, swap)
    pieces = split3(-delta)
    place = lax.broadcasted_iota(jnp.int32, (1, D), 1) % DH
    extra = jnp.zeros_like(delta)
    for number, part in enumerate(pieces):
        extra = jnp.where(place == number + 1, part, extra)
    dx_ref[...] = extra.astype(BF16)

    @pl.when(step == pl.num_programs(0) - 1)
    def _():
        wo_low[...] = mm(mixed_low_ref[...], attended_ref[...], TN).astype(BF16)
        for part in parts:
            outer_low[part, :] = mm(activated_ref[:, part], branch_ref[...], TN).astype(BF16)
            inner_low[:, part] = mm(normed_ref[...], d_inner_ref[:, part], TN).astype(BF16)


def middle(mixed, states, cotangent, halting, wo, inner, outer, gains, biases):
    rows = mixed.shape[0]
    shapes = [jax.ShapeDtypeStruct((rows, D), BF16)] * 3
    shapes += [jax.ShapeDtypeStruct((rows, D), F32), jax.ShapeDtypeStruct((8, D), F32)]
    shapes += [jax.ShapeDtypeStruct(shape, BF16) for shape in ((D, FF), (FF, D), (D, D))]
    def by_token(item):
        return pl.BlockSpec((TOKEN_ROWS, D), lambda i: (i, 0))

    operands = (mixed, states, cotangent, halting.reshape(-1, 128), wo, inner, outer, gains, biases)
    return pl.pallas_call(
        middle_kernel,
        name="middle",
        grid=(rows // TOKEN_ROWS,),
        in_specs=[by_token(item) for item in operands[:3]] + [once(item.shape) for item in operands[3:]],
        out_specs=[by_token(item) for item in shapes[:4]] + [once(item.shape) for item in shapes[4:]],
        out_shape=shapes,
        scratch_shapes=[
            pltpu.VMEM((TOKEN_ROWS, FF), F32),
            pltpu.VMEM((rows, FF), BF16),
            pltpu.VMEM((rows, FF), BF16),
            pltpu.VMEM((rows, D), BF16),
            pltpu.VMEM((rows, D), BF16),
            pltpu.VMEM((rows, D), BF16),
            pltpu.VMEM((rows, D), BF16),
        ],
        compiler_params=pltpu.CompilerParams(vmem_limit_bytes=VMEM_LIMIT),
    )(*operands)


def per_device(
    states,
    cotangent,
    halting,
    lengths,
    attention_weights,
    inner_weight,
    outer_weight,
    norm_gains,
    norm_biases,
    attention_left,
    attention_right,
    inner_left,
    inner_right,
    outer_left,
    outer_right,
    attention_left_root,
    attention_right_root,
    inner_left_root,
    inner_right_root,
    outer_left_root,
    outer_right_root,
):
    data_count = lax.axis_size("dp")
    model_count = lax.axis_size("mp")
    counts = (data_count, model_count)
    far_count = data_count // 2
    token_total = states.shape[0] * data_count * model_count
    (
        mixed,
        query_extra,
        key_extra,
        weights,
        queries,
        keys,
        values,
        twin_states,
        inner_full,
        outer_full,
        wo_full,
    ) = front(states, attention_weights, inner_weight, outer_weight, lengths, far_count)
    output_states, d_mixed, d_extra, skip, norm_rows, *lows = middle(
        mixed,
        states,
        cotangent,
        halting,
        wo_full.reshape(D, D),
        inner_full.reshape(D, FF),
        outer_full.reshape(FF, D),
        norm_gains,
        norm_biases,
    )
    roots = (
        attention_left_root,
        attention_right_root,
        inner_left_root,
        inner_right_root,
        outer_left_root,
        outer_right_root,
    )
    *pieces, norm_total, late, squares, own, twin, p0, p1, p2, p3, p4, p5, p6, p7, p8 = backward(
        queries,
        query_extra,
        keys,
        values,
        key_extra,
        d_mixed,
        d_extra,
        states,
        twin_states,
        weights.reshape(3, D, D),
        norm_rows,
        skip,
        lows,
        roots,
        counts,
    )
    outs = finish(
        token_total,
        4 * D // (data_count * model_count),
        squares,
        norm_total,
        own,
        twin,
        late,
        pieces,
        norm_gains,
        norm_biases,
        (attention_left, attention_right, inner_left, inner_right, outer_left, outer_right),
        (p0, p1, p3, p4, p6, p7),
        (attention_weights, inner_weight, outer_weight),
        (p2, p5, p8),
    )
    states_grad, grad_norm, attention_grad, inner_grad, outer_grad, norm_grad = outs[:6]
    attention_new, inner_new, outer_new, norm_new = outs[6:10]
    return (
        output_states,
        states_grad,
        grad_norm.reshape(()),
        attention_grad,
        inner_grad,
        outer_grad,
        norm_grad.reshape(-1),
        attention_new,
        inner_new,
        outer_new,
        norm_new.reshape(-1),
        *outs[10:],
    )


def solution(mesh):
    grid = P("dp", "mp")
    stack = P(None, "dp", "mp")
    tokens = P(("dp", "mp"), None)
    flat = P(("dp", "mp"))
    return jax.shard_map(
        per_device,
        mesh=mesh,
        in_specs=(tokens, tokens, flat, P("dp"), stack, grid, grid, P(), P())
        + (stack, stack, grid, grid, grid, grid)
        + (P(None, "dp", None), P(None, None, "mp"), P("dp", None), P(None, "mp"), P("dp", None), P(None, "mp")),
        out_specs=(tokens, tokens, P(), stack, grid, grid, flat, stack, grid, grid, flat)
        + (stack, stack, grid, grid, grid, grid),
        check_vma=False,
    )
```

```python
import functools
import math

import jax
import jax.numpy as jnp
from jax import lax
from jax.experimental import pallas as pl
from jax.experimental.pallas import tpu as pltpu
from jax.sharding import PartitionSpec as P

D = 512
HEADS = 8
DH = 64
FF = 2048
SEQ = 2048
SEQ_GRP = 2
PAIR = 2 * DH
QUERY_ROWS = 256
FORWARD_CHUNKS = 1
KEY_ROWS = 256
FF_PART = 256
TOKEN_ROWS = 512

F32 = jnp.float32
BF16 = jnp.bfloat16
epsilon = 1e-06
step_rate = 1.0
NN = (((1,), (0,)), ((), ()))
NT = (((1,), (1,)), ((), ()))
TN = (((0,), (0,)), ((), ()))
VMEM_LIMIT = 56 * 1024 * 1024
BACKWARD_VMEM = 62 * 1024 * 1024


def mm(left, right, dims=NN):
    return lax.dot_general(left, right, dims, preferred_element_type=F32)


def split2(value):
    high = value.astype(BF16)
    return high, (value - high.astype(F32)).astype(BF16)


def split3(value):
    high = value.astype(BF16).astype(F32)
    rest = value - high
    middle = rest.astype(BF16).astype(F32)
    return high, middle, rest - middle


MESH = pl.DeviceIdType.MESH


class Place:
    def __init__(self, far_count):
        data_rank = lax.axis_index("dp")
        self.far_count = far_count
        self.model = lax.axis_index("mp")
        self.far, self.near = data_rank // 2, data_rank % 2
        self.data_rank = 2 * self.far + self.near
        side, core = self.model // 2, self.model % 2
        self.side, self.core = side, core
        self.beside = 2 * (1 - side) + core
        self.twin = 2 * side + 1 - core
        self.twin_beside = 2 * (1 - side) + 1 - core
        self.to_beside = {"mp": self.beside}
        self.to_twin = {"mp": self.twin}
        self.to_near = {"dp": 2 * self.far + 1 - self.near}

    def other_far(self, step):
        return (self.far + step) % self.far_count

    def to_far(self, step):
        return {"dp": 2 * self.other_far(step) + self.near}

    def meet(self):
        barrier = pltpu.get_barrier_semaphore()
        partners = [self.to_far(step) for step in range(1, self.far_count)]
        partners += [self.to_near, self.to_beside, self.to_twin]
        for partner in partners:
            pl.semaphore_signal(barrier, inc=1, device_id=partner, device_id_type=MESH)
        pl.semaphore_wait(barrier, len(partners))


class Wires:
    def __init__(self, send_sems, recv_sems):
        self.sems = (send_sems, recv_sems)
        self.used = 0

    def copy(self, source, target, partner):
        index = self.used
        self.used += 1
        return pltpu.make_async_remote_copy(
            src_ref=source,
            dst_ref=target,
            send_sem=self.sems[0].at[index],
            recv_sem=self.sems[1].at[index],
            device_id=partner,
            device_id_type=MESH,
        )


def start_all(copies):
    for copy in copies:
        copy.start()


def wait_all(copies):
    for copy in copies:
        copy.wait()


def columns(index, size):
    return pl.ds(pl.multiple_of(index * size, size), size)


class Chunk:
    def __init__(self, rows, cols, row_size, col_size):
        self.rows, self.cols, self.row_size, self.col_size = rows, cols, row_size, col_size

    def columns(self, index):
        offset = pl.multiple_of(index * self.col_size + self.cols[0], math.gcd(self.col_size, max(self.cols[0], 128)))
        return pl.ds(offset, self.cols[1])

    @property
    def row_window(self):
        return pl.ds(*self.rows)

    @property
    def shape(self):
        return self.rows[1], self.cols[1]


def whole_chunk(rows, cols):
    return Chunk((0, rows), (0, cols), rows, cols)


class Staged:
    def __init__(self, active, twin_stage):
        self.active, self.twin_stage = active, twin_stage
        self.stages = []

    def start(self, number):
        copies = self.stages[number]
        if self.active is None:
            start_all(copies)
        elif number != self.twin_stage:
            pl.when(self.active)(lambda: start_all(copies))
        else:
            pl.when(self.sends)(lambda: start_all(copies))

    def wait(self, number):
        copies = self.stages[number]
        if self.active is None:
            wait_all(copies)
        elif number != self.twin_stage:
            pl.when(self.active)(lambda: wait_all(copies))
        else:

            @pl.when(self.sends)
            def _():
                for copy in copies:
                    copy.wait_send()

            @pl.when(jnp.logical_not(self.sends))
            def _():
                for copy in copies:
                    copy.wait_recv()


class Gather(Staged):
    def __init__(self, wires, place, full, order, chunk, active=None):
        super().__init__(active, len(order) - 1)
        self.sends = active
        mine, side = chunk.columns(place.model), chunk.columns(place.beside)
        self.home = full.at[place.far, place.near, chunk.row_window, mine]
        fars, nears, cols = place.far, place.near, [mine]

        def send(col, partner):
            view = full.at[fars, nears, chunk.row_window, col]
            return wires.copy(view, view, partner)

        for letter in order:
            if letter == "x":
                self.stages.append([send(mine, place.to_beside)])
                cols = [mine, side]
            elif letter == "y":
                self.stages.append([send(col, place.to_near) for col in cols])
                nears = slice(None)
            elif letter == "c":
                self.stages.append([send(col, place.to_twin) for col in cols])
            else:
                ways = [place.to_far(step) for step in range(1, place.far_count)]
                self.stages.append([send(col, way) for col in cols for way in ways])
                fars = slice(None)

    def begin(self):
        self.start(0)

    def advance(self, number):
        self.wait(number)
        if number + 1 < len(self.stages):
            self.start(number + 1)


GATHER_STEPS = 4


def gather_copies(far_count):
    return far_count + 6


def reduce_plan(order, far_count, rows, cols):
    slots, nears, fars = 2, 2, far_count
    plan = []
    for letter in order:
        if letter == "x":
            plan.append((letter, slots, nears, fars, (nears, fars, rows, cols)))
            slots = 1
        elif letter == "y":
            plan.append((letter, slots, nears, fars, (slots, fars, rows, cols)))
            nears = 1
        else:
            plan.append((letter, slots, nears, fars, (far_count, slots, nears, rows, cols)))
            fars = 1
    return plan


REDUCE_BUFFERS = 8
REDUCE_STEPS = 4


def reduce_copies(far_count):
    return far_count + 6


def reduce_scratch(order, far_count, rows, cols):
    shape = (2, 2, far_count, rows, cols)
    buffers = [pltpu.VMEM(shape, F32), pltpu.VMEM(shape, BF16)]
    for *_, shape in reduce_plan(order, far_count, rows, cols):
        buffers += [pltpu.VMEM(shape, BF16), pltpu.VMEM(shape, BF16)]
    return buffers


class Reducer(Staged):
    def __init__(self, wires, place, buffers, order, low=None, chunk=None, given=None, active=None):
        super().__init__(active, 0)
        self.sends = None if active is None else jnp.logical_not(active)
        self.place = place
        self.mine = None
        self.acc, self.got = buffers[:2]
        self.out, self.arrived = buffers[2::2], buffers[3::2]
        rows, size = self.acc.shape[-2:]
        self.plan = reduce_plan(order, place.far_count, rows, size)
        self.chunk = chunk
        self.kept = (place.model, place.beside)
        if given is not None:
            first = [wires.copy(given, self.got, place.to_twin)]
        else:
            twins = (place.twin, place.twin_beside)
            first = [
                wires.copy(
                    low.at[:, near, chunk.row_window, chunk.columns(twins[slot])],
                    self.got.at[slot, near],
                    place.to_twin,
                )
                for slot in range(2)
                for near in range(2)
            ]
        self.stages = [first]
        for (letter, *_), out, arrived in zip(self.plan, self.out, self.arrived):
            if letter == "z":
                stage = [
                    wires.copy(out.at[place.other_far(step)], arrived.at[step], place.to_far(step))
                    for step in range(1, place.far_count)
                ]
            else:
                stage = [wires.copy(out, arrived, place.to_beside if letter == "x" else place.to_near)]
            self.stages.append(stage)

    def loads(self, partial, mine, load_sems):
        self.mine = mine
        return [
            pltpu.make_async_copy(
                partial.at[:, near, self.chunk.row_window, self.chunk.columns(self.kept[slot])],
                mine.at[slot, near],
                load_sems.at[2 * slot + near],
            )
            for slot in range(2)
            for near in range(2)
        ]

    def begin(self):
        self.start(0)

    def held(self, number):
        letter, slots, nears, fars, _ = self.plan[number]
        place = self.place
        return (
            letter,
            range(slots),
            range(2) if nears == 2 else (place.near,),
            range(place.far_count) if fars > 1 else (place.far,),
        )

    def prepare(self, number):
        letter, slots, nears, fars = self.held(number)
        place, acc, out = self.place, self.acc, self.out[number]
        if letter == "x":
            for i, near in enumerate(nears):
                for j, far in enumerate(fars):
                    out[i, j] = acc[1, near, far].astype(BF16)
        elif letter == "y":
            for slot in slots:
                for j, far in enumerate(fars):
                    out[slot, j] = acc[slot, 1 - place.near, far].astype(BF16)
        else:
            for slot in slots:
                for i, near in enumerate(nears):
                    for far in fars:
                        out[far, slot, i] = acc[slot, near, far].astype(BF16)

    def absorb(self, number):
        letter, slots, nears, fars = self.held(number)
        place, acc, arrived = self.place, self.acc, self.arrived[number]
        if letter == "x":
            for i, near in enumerate(nears):
                for j, far in enumerate(fars):
                    acc[0, near, far] += arrived[i, j].astype(F32)
        elif letter == "y":
            for slot in slots:
                for j, far in enumerate(fars):
                    acc[slot, place.near, far] += arrived[slot, j].astype(F32)
        else:
            for slot in slots:
                for i, near in enumerate(nears):
                    total = acc[slot, near, place.far]
                    for step in range(1, place.far_count):
                        total = total + arrived[step, slot, i].astype(F32)
                    acc[slot, near, place.far] = total

    def advance(self, number):
        self.wait(number)

        def add():
            if number == 0:
                for slot in range(2):
                    for near in range(2):
                        for far in range(self.place.far_count):
                            spot = (slot, near, far)
                            own = self.acc[spot] if self.mine is None else self.mine[spot].astype(F32)
                            self.acc[spot] = own + self.got[spot].astype(F32)
            else:
                self.absorb(number - 1)
            if number < len(self.plan):
                self.prepare(number)

        if self.active is None:
            add()
        else:
            pl.when(self.active)(add)
        if number < len(self.plan):
            self.start(number + 1)

    def result(self):
        return self.acc[0, self.place.near, self.place.far]


class Spread:
    def __init__(self, wires, place, tile, stages, slots):
        self.place, self.tile, self.stages, self.slots = place, tile, stages, slots
        self.copies = [
            [wires.copy(tile, stages.at[number], partner)]
            for number, partner in enumerate((place.to_twin, place.to_beside, place.to_near))
        ]
        self.copies.append(
            [wires.copy(tile, slots.at[place.far], place.to_far(step)) for step in range(1, place.far_count)]
        )

    def begin(self):
        start_all(self.copies[0])

    def advance(self, number):
        wait_all(self.copies[number])
        if number == 3:
            self.slots[self.place.far] = self.tile[...]
            total = self.slots[0]
            for far in range(1, self.place.far_count):
                total = total + self.slots[far]
            self.tile[...] = total
        else:
            self.tile[...] += self.stages[number]
            start_all(self.copies[number + 1])


def spread_copies(far_count):
    return far_count - 1 + 3


def spread_scratch(far_count, shape):
    return [pltpu.VMEM(shape, F32), pltpu.VMEM((3,) + shape, F32), pltpu.VMEM((far_count,) + shape, F32)]


def any_spec():
    return pl.BlockSpec(memory_space=pl.ANY)


def vmem_spec():
    return pl.BlockSpec(memory_space=pltpu.VMEM)


def smem_spec():
    return pl.BlockSpec(memory_space=pltpu.SMEM)


def own_lanes(parity):
    lane = lax.broadcasted_iota(jnp.int32, (1, PAIR), 1)
    return (lane < DH) if parity == 0 else (lane >= DH)


def lane_in_half():
    return lax.broadcasted_iota(jnp.int32, (1, PAIR), 1) % DH


def blend(parity, own, extra):
    mine = jnp.where(own_lanes(parity), 1.0, 0.0)
    return own * mine.astype(BF16) + extra * (1.0 - mine).astype(BF16)


def slot_calls(step, width, calls):
    def at(sub_step):
        for slot, call in calls:
            if slot % width == sub_step:
                pl.when(step == slot // width)(call)

    return at


PROJECT_ORDERS = ("zxyc", "zyxc")
FORWARD_ORDERS = ("zxyc", "zyxc", "zyxc")
FORWARD_SLOTS = ((2, 10, 25), (2, 10, 26), (3, 11, 26))


def front_kernel(
    far_count,
    states_ref,
    states_any,
    attention_ref,
    inner_ref,
    outer_ref,
    lengths_ref,
    mixed_ref,
    qx_ref,
    extra_ref,
    weights_out,
    queries_out,
    keys_out,
    values_out,
    twin_out,
    inner_full,
    outer_full,
    wo_full,
    full,
    queries,
    keys,
    values,
    twin_states,
    twin_queries,
    inner_low,
    outer_low,
    wo_low,
    ka,
    va,
    score_a,
    score_b,
    send_sems,
    recv_sems,
    local_sems,
):
    rows = states_ref.shape[0]
    step = pl.program_id(0)
    here = Place(far_count)
    wires = Wires(send_sems, recv_sems)
    shard = full.shape[-2], full.shape[-1] // 4
    projections = [
        Gather(wires, here, full.at[member], PROJECT_ORDERS[member], whole_chunk(*shard)) for member in range(2)
    ]
    projections += [
        Gather(wires, here, full.at[2], PROJECT_ORDERS[core], whole_chunk(*shard), active=here.core == core)
        for core in range(2)
    ]
    fulls, lows = (inner_full, outer_full, wo_full), (inner_low, outer_low, wo_low)
    gathers = [
        Gather(wires, here, target, order, whole_chunk(*low.shape))
        for target, low, order in zip(fulls, lows, FORWARD_ORDERS)
    ]
    fill = [
        pltpu.make_async_copy(low, gather.home, local_sems.at[number])
        for number, (low, gather) in enumerate(zip(lows, gathers))
    ]
    swap_states = wires.copy(states_any, twin_states, here.to_twin)
    swaps = []
    for number, block in enumerate((here.model, here.beside)):
        cols = columns(block, PAIR)
        for kept in (keys, values):
            for start, end in ((0, rows), (rows, 0)):
                swaps.append(
                    wires.copy(kept.at[pl.ds(start, rows), cols], kept.at[pl.ds(end, rows), cols], here.to_twin)
                )
        swaps.append(wires.copy(twin_queries.at[number], queries.at[:, cols], here.to_twin))
    outward = [
        pltpu.make_async_copy(source, target, local_sems.at[3 + number])
        for number, (source, target) in enumerate(
            ((queries, queries_out), (keys, keys_out), (values, values_out), (twin_states, twin_out), (full, weights_out))
        )
    ]

    @pl.when(step == 0)
    def _():
        for member in range(3):
            full[member, here.far, here.near, :, columns(here.model, shard[1])] = attention_ref[member].astype(BF16)
        inner_low[...] = inner_ref[...].astype(BF16)
        outer_low[...] = outer_ref[...].astype(BF16)
        wo_low[...] = attention_ref[3].astype(BF16)
        start_all(fill)
        here.meet()
        for gather in projections:
            gather.begin()
        swap_states.start()
        index = lax.broadcasted_iota(jnp.int32, (2 * rows, 1), 0)
        half = here.model % 2
        position = jnp.where(index < rows, index + half * rows, index - half * rows)
        bias = jnp.where(position < lengths_ref[here.side], 0.0, -1e30)
        lane = lane_in_half()
        extra_ref[...] = jnp.where(lane == 0, bias, jnp.where(lane <= 3, 1.0, 0.0)).astype(BF16)
        wait_all(fill)
        for gather in projections:
            gather.advance(0)
        for gather in gathers:
            gather.begin()
        for gather in projections:
            gather.advance(1)
        swap_states.wait()
        for gather in projections:
            gather.advance(2)
        for member, kept in ((1, keys), (2, values), (0, queries)):
            both = jnp.concatenate(
                [full[member, :, :, :, columns(block, PAIR)].reshape(D, PAIR) for block in (here.model, here.beside)],
                axis=1,
            )
            own = mm(states_ref[...], both).astype(BF16)
            twin = mm(twin_states[...], both).astype(BF16)
            if member == 0:
                own = (own * DH ** (-0.5)).astype(BF16)
                twin = (twin * DH ** (-0.5)).astype(BF16)
            for number, block in enumerate((here.model, here.beside)):
                cols = columns(block, PAIR)
                kept[:rows, cols] = own[:, number * PAIR : (number + 1) * PAIR]
                if member:
                    kept[rows:, cols] = twin[:, number * PAIR : (number + 1) * PAIR]
                else:
                    twin_queries[number] = twin[:, number * PAIR : (number + 1) * PAIR]
        start_all(swaps)

    @pl.when(step == 2)
    def _():
        wait_all(swaps)
        for gather in projections:
            gather.advance(3)
        start_all(outward)

    calls = [
        (slot, functools.partial(gather.advance, number))
        for gather, slots in zip(gathers, FORWARD_SLOTS)
        for number, slot in enumerate(slots)
    ]
    at = slot_calls(step, 2 * (rows // QUERY_ROWS), calls)
    pair_cols = columns(2 * (step % 2) + (step // 2 + here.core) % 2, PAIR)
    place = lane_in_half()
    first = jnp.where(place == 0, 1.0, 0.0).astype(BF16)
    ones = jnp.where(place <= 3, 1.0, 0.0).astype(BF16)
    for parity in range(2):
        ka[parity] = blend(parity, keys[:, pair_cols], extra_ref[...])
        va[parity] = blend(parity, values[:, pair_cols], ones)
    steps = [(parity, block) for block in range(rows // QUERY_ROWS) for parity in range(2)]
    scratch = (score_a, score_b)

    chunk = keys.shape[0] // FORWARD_CHUNKS

    def query_part(index):
        parity, block = steps[index]
        return blend(parity, queries[pl.ds(block * QUERY_ROWS, QUERY_ROWS), pair_cols], first)

    def score(index, part, number):
        window = pl.ds(number * chunk, chunk)
        scores = mm(ka[steps[index][0], window, :], part, NT)
        scratch[index % 2][window, :] = scores
        return jnp.max(scores, axis=0, keepdims=True)

    part = query_part(0)
    row_max = score(0, part, 0)
    for number in range(1, FORWARD_CHUNKS):
        row_max = jnp.maximum(row_max, score(0, part, number))
    held = [None, None]
    logs = [None, None]
    row = lax.broadcasted_iota(jnp.int32, (PAIR, 1), 0)
    for index, (parity, block) in enumerate(steps):
        at(index)
        more = index + 1 < len(steps)
        part = query_part(index + 1) if more else None
        product, next_max = None, None
        for number in range(FORWARD_CHUNKS):
            if more:
                found = score(index + 1, part, number)
                next_max = found if number == 0 else jnp.maximum(next_max, found)
            window = pl.ds(number * chunk, chunk)
            shifted = jnp.exp(scratch[index % 2][window, :] - row_max).astype(BF16)
            term = mm(va[parity, window, :], shifted, TN)
            product = term if number == 0 else product + term
        sum_row = DH if parity == 0 else 0
        total = product[sum_row : sum_row + 1, :]
        held[parity] = product / total
        logs[parity] = row_max + jnp.log(total)
        row_max = next_max
        if parity == 1:
            window = pl.ds(block * QUERY_ROWS, QUERY_ROWS)
            both = jnp.concatenate([held[0][:DH], held[1][DH:]], axis=0)
            mixed_ref[window, pair_cols] = both.T
            parts = split3(-jnp.where(row < DH, logs[1], logs[0]))
            spot = row % DH
            extra = jnp.where(spot == 0, 1.0, 0.0)
            for number, part in enumerate(parts):
                extra = jnp.where(spot == number + 1, part, extra)
            qx_ref[window, pair_cols] = extra.T.astype(BF16)

    @pl.when(step == pl.num_programs(0) - 1)
    def _():
        for gather in gathers:
            gather.advance(GATHER_STEPS - 1)
        wait_all(outward)


def once(shape):
    return pl.BlockSpec(shape, lambda j: (0,) * len(shape), pipeline_mode=pl.Buffered(1))


def front(states, attention_weights, inner_shard, outer_shard, lengths, far_count):
    rows, width = states.shape
    total = 2 * rows
    shard_rows = attention_weights.shape[1]
    fulls = [
        jax.ShapeDtypeStruct((far_count, 2, height, wide), BF16)
        for height, wide in ((inner_shard.shape[0], FF), (outer_shard.shape[0], D), (shard_rows, D))
    ]
    copies = 7 * gather_copies(far_count) + 11
    weights_shape = (3, far_count, 2, shard_rows, D)
    return pl.pallas_call(
        functools.partial(front_kernel, far_count),
        name="front",
        grid=(width // PAIR,),
        in_specs=[once(states.shape), any_spec()]
        + [once(item.shape) for item in (attention_weights, inner_shard, outer_shard)]
        + [smem_spec()],
        out_specs=[once((rows, width)), once((rows, width)), once((total, PAIR))] + [any_spec()] * 8,
        out_shape=[
            jax.ShapeDtypeStruct((rows, width), F32),
            jax.ShapeDtypeStruct((rows, width), BF16),
            jax.ShapeDtypeStruct((total, PAIR), BF16),
            jax.ShapeDtypeStruct(weights_shape, BF16),
            jax.ShapeDtypeStruct((rows, width), BF16),
            jax.ShapeDtypeStruct((total, width), BF16),
            jax.ShapeDtypeStruct((total, width), BF16),
            jax.ShapeDtypeStruct((rows, width), BF16),
        ]
        + fulls,
        scratch_shapes=[
            pltpu.VMEM(weights_shape, BF16),
            pltpu.VMEM((rows, width), BF16),
            pltpu.VMEM((total, width), BF16),
            pltpu.VMEM((total, width), BF16),
            pltpu.VMEM((rows, width), BF16),
            pltpu.VMEM((2, rows, PAIR), BF16),
            pltpu.VMEM(inner_shard.shape, BF16),
            pltpu.VMEM(outer_shard.shape, BF16),
            pltpu.VMEM(attention_weights.shape[1:], BF16),
            pltpu.VMEM((2, total, PAIR), BF16),
            pltpu.VMEM((2, total, PAIR), BF16),
            pltpu.VMEM((total, QUERY_ROWS), F32),
            pltpu.VMEM((total, QUERY_ROWS), F32),
            pltpu.SemaphoreType.DMA((copies,)),
            pltpu.SemaphoreType.DMA((copies,)),
            pltpu.SemaphoreType.DMA((8,)),
        ],
        compiler_params=pltpu.CompilerParams(
            vmem_limit_bytes=VMEM_LIMIT, collective_id=1, has_side_effects=True
        ),
    )(states, states, attention_weights, inner_shard, outer_shard, lengths)


EARLY = (
    (0, 0, "yxz", "zyxc"),
    (1, 0, "xyz", "zxyc"),
    (2, None, "xyz", "zxyc"),
    (0, 1, "yxz", "zyxc"),
    (1, 1, "xyz", "zxyc"),
)
LATE_REDUCE = ("yxz", "xyz", "yxz")
LATE_GATHER = ("zyxc", "zxyc", "zyxc")
SCHEDULE = (
    (0, 0, 0), (0, 1, 0), (5, 0, 1), (5, 1, 1), (11, 0, 2), (11, 1, 2),
    (11, 2, 0), (11, 3, 0), (11, 4, 0), (15, 2, 1), (16, 0, 3), (16, 1, 3),
    (16, 3, 1), (16, 4, 1), (18, 2, 2), (19, 5, 1), (19, 6, 1), (19, 7, 1),
    (21, 0, 4), (21, 1, 4), (23, 2, 3), (23, 4, 2), (23, 6, 2), (24, 3, 2),
    (24, 5, 2), (24, 7, 2), (26, 0, 5), (26, 1, 5), (26, 2, 4), (26, 6, 3),
    (27, 4, 3), (28, 5, 3), (28, 7, 3), (29, 6, 4), (30, 1, 6), (30, 2, 5),
    (30, 3, 3), (31, 0, 6), (31, 5, 4), (31, 7, 4), (32, 6, 5), (32, 4, 4),
    (32, 2, 6), (32, -1, 0), (32, -1, 1), (32, 5, 5), (32, 7, 5), (32, 3, 4),
    (32, 10, 1), (32, 8, 1), (32, 9, 1), (32, 6, 6), (32, 1, 7), (32, 4, 5),
    (32, 0, 7), (32, 5, 6), (32, 7, 6), (32, 3, 5), (32, 1, 8), (32, 2, 7),
    (32, 10, 2), (32, 8, 2), (32, 0, 8), (32, 6, 7), (32, 9, 2), (32, 2, 8),
    (32, 6, 8), (32, 10, 3), (32, 8, 3), (32, 5, 7), (32, 7, 7), (32, 3, 6),
    (32, 4, 6), (32, 9, 3), (32, 10, 4), (32, 8, 4), (32, 5, 8), (32, 7, 8),
    (32, 9, 4), (32, -1, 11), (32, 10, 5), (32, 8, 5), (32, -1, 12), (32, 9, 5),
    (32, 3, 7), (32, 4, 7), (32, -1, 13), (32, 10, 6), (32, 8, 6), (32, 9, 6),
    (32, -1, 14), (32, 3, 8), (32, 4, 8), (32, -1, 2), (32, -1, 3), (32, -1, 4),
    (32, 10, 7), (32, 8, 7), (32, 9, 7), (32, -1, 15), (32, -1, 5), (32, -1, 6),
    (32, -1, 7), (32, -1, 8), (32, -1, 9), (32, 10, 8), (32, 8, 8), (32, 9, 8),
    (32, -1, 10),
)
NORM_SLOTS = (4, 7, 12, 16)


def early_chunks(shapes):
    chunks = []
    for array, half, *_ in EARLY:
        rows, cols = shapes[array]
        if half is None:
            chunks.append(whole_chunk(rows, cols))
        elif array == 0:
            chunks.append(Chunk((0, rows), (half * cols // 2, cols // 2), rows, cols))
        else:
            chunks.append(Chunk((half * rows // 2, rows // 2), (0, cols), rows, cols))
    return chunks


def product_steps(grad, left_root, right_root, place, counts, left_out, right_out, update_out, room, held):
    data_count, model_count = counts
    far_count, _, shard_rows, width = grad.shape
    height = data_count * shard_rows
    part = far_count // model_count
    size = width // model_count
    share = width // data_count

    def left():
        rows_here = grad[place.far, place.near]
        rows_there = grad[pl.ds(place.model * part, part)].reshape(height // model_count, width)
        left_out[...] = mm(rows_here, rows_there, NT)

    def right():
        cols_there = grad[:, :, :, columns(place.model, size)].reshape(height, size)
        if share % 128 == 0:
            cols_here = grad[:, :, :, columns(place.data_rank, share)].reshape(height, share)
            right_out[...] = mm(cols_here, cols_there, TN)
        else:
            group = data_count // model_count
            cols_here = grad[:, :, :, columns(place.data_rank // group, size)].reshape(height, size)
            room[:size, :size] = mm(cols_here, cols_there, TN)
            window = pl.ds(pl.multiple_of((place.data_rank % group) * share, share), share)
            right_out[...] = room[window, :size]

    def once():
        whole = grad[...].reshape(height, width)
        high, low = split2(left_root[...])
        held[...] = mm(high, whole) + mm(low, whole)

    def twice():
        chunk = min(512, width)
        total = jnp.zeros(update_out.shape, F32)
        for start in range(0, width, chunk):
            high, low = split2(held[:, start : start + chunk])
            root_high, root_low = split2(right_root[start : start + chunk, :])
            total = total + (mm(high, root_high) + mm(high, root_low) + mm(low, root_high))
        update_out[...] = total

    return [left, right, once, twice]


def backward_kernel(
    far_count,
    counts,
    inv_tokens,
    q_ref,
    qx_ref,
    k_ref,
    v_ref,
    kx_ref,
    do_ref,
    dox_ref,
    own_any_states,
    twin_any_states,
    weights_any,
    norm_raw,
    skip_any,
    inner_low,
    outer_low,
    wo_low,
    *rest,
):
    roots_any, rest = rest[:6], rest[6:]
    (inner_piece, outer_piece, wo_piece, norm_total, late_out, squares_out, own_any, twin_in), rest = rest[:8], rest[8:]
    products, rest = rest[:9], rest[9:]
    (qa, da, ka, va, dqt, dq, dk, dv, states_t, late_low, own_sum, twin_out), rest = rest[:12], rest[12:]
    mine, rest = rest[: len(EARLY)], rest[len(EARLY) :]
    count = len(EARLY) * REDUCE_BUFFERS
    early_buffers, rest = rest[:count], rest[count:]
    late_buffers, rest = rest[: 3 * REDUCE_BUFFERS], rest[3 * REDUCE_BUFFERS :]
    roots, rest = rest[:6], rest[6:]
    (own_states, twin_states, weights_ref), rest = rest[:3], rest[3:]
    (attention_full, inner_full, outer_full, room, held_small, held_wide, held_tall), rest = rest[:7], rest[7:]
    tile, tile_stages, tile_slots, norm_tile, norm_stages, norm_slots = rest[:6]
    send_sems, recv_sems, load_sems, local_sems = rest[6:]

    step = pl.program_id(0)
    rows = q_ref.shape[0]
    total = k_ref.shape[0]
    place = Place(far_count)
    wires = Wires(send_sems, recv_sems)
    lows = (inner_low, outer_low, wo_low)
    pieces = (inner_piece, outer_piece, wo_piece)
    fulls = (inner_full, outer_full, attention_full.at[3])
    chunks = early_chunks([piece.shape for piece in pieces])
    reducers = []
    gathers = []
    loads = []
    for number, (array, _, reduce_order, gather_order) in enumerate(EARLY):
        buffers = early_buffers[number * REDUCE_BUFFERS : (number + 1) * REDUCE_BUFFERS]
        reducer = Reducer(wires, place, buffers, reduce_order, low=lows[array], chunk=chunks[number])
        reducers.append(reducer)
        loads.append(reducer.loads(lows[array], mine[number], load_sems.at[number]))
        gathers.append(Gather(wires, place, fulls[array], gather_order, chunks[number]))
    late_shape = wo_piece.shape
    late_reducers = []
    late_gathers = []
    for late_set in range(2):
        active = place.core == late_set
        late_reducers.append(
            [
                Reducer(
                    wires,
                    place,
                    late_buffers[member * REDUCE_BUFFERS : (member + 1) * REDUCE_BUFFERS],
                    LATE_REDUCE[member],
                    given=late_low.at[member],
                    active=active,
                )
                for member in range(3)
            ]
        )
        late_gathers.append(
            [
                Gather(
                    wires, place, attention_full.at[member], LATE_GATHER[member], whole_chunk(*late_shape), active=active
                )
                for member in range(3)
            ]
        )
    norms = Spread(wires, place, norm_tile, norm_stages, norm_slots)
    squares = Spread(wires, place, tile, tile_stages, tile_slots)
    swap = wires.copy(twin_out, twin_in, place.to_twin)
    fetch = [
        pltpu.make_async_copy(source, target, local_sems.at[number])
        for number, (source, target) in enumerate(
            zip((*roots_any, skip_any, weights_any), (*roots, own_sum, weights_ref))
        )
    ]
    outward = pltpu.make_async_copy(own_sum, own_any, local_sems.at[0])
    bring = [
        pltpu.make_async_copy(own_any_states, own_states, local_sems.at[8]),
        pltpu.make_async_copy(twin_any_states, twin_states, local_sems.at[9]),
    ]

    def turn_states():
        wait_all(bring)
        states_t[:, :rows] = own_states[...].T
        states_t[:, rows:] = twin_states[...].T


    def early_call(number, number_of_step):
        array, chunk = EARLY[number][0], chunks[number]
        if number_of_step == 0:

            def call():
                reducers[number].begin()
                start_all(loads[number])

        elif number_of_step <= REDUCE_STEPS:

            def call():
                if number_of_step == 1:
                    wait_all(loads[number])
                reducers[number].advance(number_of_step - 1)
                if number_of_step == REDUCE_STEPS:
                    piece = reducers[number].result() * inv_tokens
                    pieces[array][chunk.row_window, pl.ds(*chunk.cols)] = piece
                    gathers[number].home[...] = piece.astype(BF16)
                    gathers[number].begin()

        else:

            def call():
                gathers[number].advance(number_of_step - REDUCE_STEPS - 1)

        return call

    def late_products():
        slot = (step + place.side) % 2
        wide = jnp.concatenate([dk[:, pair_cols], dv[:, pair_cols]], axis=1)
        both = mm(states_t[...], wide)
        values = (mm(states_t[:, :rows], dq[:, pair_cols]), both[:, :PAIR], both[:, PAIR:])
        active = place.core == step // 2
        for member, value in enumerate(values):
            parts = value.reshape(far_count, 2, *late_shape)

            @pl.when(active)
            def _():
                for near in range(2):
                    late_reducers[0][member].acc[slot, near] = parts[:, near]

            @pl.when(jnp.logical_not(active))
            def _():
                for near in range(2):
                    late_low[member, slot, near] = parts[:, near].astype(BF16)

    def late_call(late_set, member, number_of_step):
        reducer, gather = late_reducers[late_set][member], late_gathers[late_set][member]
        if number_of_step == 0:
            return reducer.begin

        def call():
            if number_of_step <= REDUCE_STEPS:
                reducer.advance(number_of_step - 1)
                if number_of_step == REDUCE_STEPS:

                    @pl.when(place.core == late_set)
                    def _():
                        piece = reducer.result() * inv_tokens
                        late_out[member] = piece
                        gather.home[...] = piece.astype(BF16)

                    gather.begin()
            else:
                gather.advance(number_of_step - REDUCE_STEPS - 1)

        return call

    def scheduled(chain, number_of_step):
        if chain < len(EARLY):
            return early_call(chain, number_of_step)
        return late_call(*divmod(chain - len(EARLY), 3), number_of_step)

    sub_steps = 4 * (total // KEY_ROWS)
    calls = [(slot, scheduled(chain, number)) for slot, chain, number in SCHEDULE if slot < sub_steps]
    calls += [(slot, functools.partial(norms.advance, stage)) for stage, slot in enumerate(NORM_SLOTS)]
    calls.append((12, lambda: start_all(fetch)))
    calls.append((6, turn_states))
    at = slot_calls(step, total // KEY_ROWS, calls)

    @pl.when(step == 0)
    def _():
        norm_tile[...] = norm_raw[...]
        place.meet()
        norms.begin()
        start_all(bring)

    lane = lane_in_half()
    ones = jnp.where(lane <= 3, 1.0, 0.0).astype(BF16)
    for parity in range(2):
        ka[parity] = blend(parity, k_ref[...], kx_ref[...])
        va[parity] = blend(parity, v_ref[...], ones)
        qa[parity] = blend(parity, q_ref[...], qx_ref[...])
        da[parity] = blend(parity, do_ref[...], dox_ref[...])
    dqt[...] = jnp.zeros_like(dqt)
    pair = 2 * (step % 2) + step // 2
    pair_cols = columns(pair, PAIR)
    for block in range(total // KEY_ROWS):
        at(block)
        window = pl.ds(block * KEY_ROWS, KEY_ROWS)
        key_grads = []
        value_grads = []
        for parity in range(2):
            key_block = ka[parity, window, :]
            probs = jnp.exp(mm(key_block, qa[parity], NT))
            d_probs = mm(va[parity, window, :], da[parity], NT)
            d_scores = (probs * d_probs).astype(BF16)
            value_grads.append(mm(probs.astype(BF16), da[parity]))
            key_grads.append(mm(d_scores, qa[parity]))
            dqt[parity] += mm(key_block, d_scores, TN)
        dk[window, pair_cols] = jnp.where(own_lanes(0), key_grads[0], key_grads[1]).astype(BF16)
        dv[window, pair_cols] = jnp.where(own_lanes(0), value_grads[0], value_grads[1]).astype(BF16)
    both = jnp.concatenate([dqt[0, :DH], dqt[1, DH:]], axis=0) * DH ** (-0.5)
    dq[:, pair_cols] = both.T.astype(BF16)

    late_products()
    for late_set in range(2):

        @pl.when(step == 2 * late_set + 1)
        def _():
            for member in range(3):
                late_call(late_set, member, 0)()

    @pl.when(step == pl.num_programs(0) - 1)
    def _():
        part = 256

        def twin_share():
            wait_all(fetch)

            @pl.loop(0, rows // part)
            def _(block):
                window = pl.ds(pl.multiple_of(block * part, part), part)
                there = pl.ds(pl.multiple_of(rows + block * part, part), part)
                value = mm(dk[there, :], weights_ref[1], NT) + mm(dv[there, :], weights_ref[2], NT)
                twin_out[window, :] = value.astype(BF16)

            swap.start()

        def own_share():
            @pl.loop(0, rows // part)
            def _(block):
                window = pl.ds(pl.multiple_of(block * part, part), part)
                own_sum[window, :] += (
                    mm(dq[window, :], weights_ref[0], NT)
                    + mm(dk[window, :], weights_ref[1], NT)
                    + mm(dv[window, :], weights_ref[2], NT)
                )

            outward.start()

        common = (place, counts)
        inner_steps = product_steps(inner_full, roots[2], roots[3], *common, *products[3:6], room, held_wide)
        outer_steps = product_steps(outer_full, roots[4], roots[5], *common, *products[6:9], room, held_tall)

        def member_products():
            @pl.loop(0, 4)
            def _(member):
                steps = product_steps(
                    attention_full.at[member],
                    roots[0].at[member],
                    roots[1].at[member],
                    *common,
                    *[product.at[member] for product in products[:3]],
                    room,
                    held_small,
                )
                for call in steps:
                    call()

        work = [twin_share, own_share, *outer_steps, *inner_steps, member_products]

        def square(piece):
            return jnp.sum(jnp.sum(piece * piece, axis=0, keepdims=True), axis=1, keepdims=True)

        def squares_begin():
            square_sum = square(inner_piece[...]) + square(outer_piece[...]) + square(wo_piece[...])
            for member in range(3):
                square_sum = square_sum + square(late_out[member])
            tile[...] = jnp.broadcast_to(square_sum, tile.shape)
            squares.begin()

        work.append(squares_begin)
        work += [functools.partial(squares.advance, stage) for stage in range(4)]
        for slot, chain, number in SCHEDULE:
            if slot >= sub_steps:
                (work[number] if chain < 0 else scheduled(chain, number))()
        squares_out[...] = tile[...]
        norm_total[...] = norm_tile[...] * inv_tokens
        swap.wait()
        outward.wait()


def backward(
    queries,
    query_extra,
    keys,
    values,
    key_extra,
    d_mixed,
    d_extra,
    states,
    twin_states,
    weights,
    norm_rows,
    skip,
    lows,
    roots,
    counts,
):
    rows, width = queries.shape
    total = keys.shape[0]
    data_count, model_count = counts
    far_count = data_count // 2

    def by_pair(height):
        return pl.BlockSpec((height, PAIR), lambda j: (0, 2 * (j % 2) + j // 2))

    whole = once

    def seen(array):
        return array.reshape(far_count, 2, array.shape[0] // data_count, array.shape[1])

    def products(lead, height, wide):
        return [
            jax.ShapeDtypeStruct(lead + shape, F32)
            for shape in (
                (height // data_count, height // model_count),
                (wide // data_count, wide // model_count),
                (height // data_count, wide // model_count),
            )
        ]

    pieces = [(low.shape[0] // data_count, low.shape[1] // model_count) for low in lows]
    late = pieces[2]
    tile = (8, 128)
    out_shape = [jax.ShapeDtypeStruct(piece, F32) for piece in pieces]
    out_shape += [
        jax.ShapeDtypeStruct(norm_rows.shape, F32),
        jax.ShapeDtypeStruct((3,) + late, F32),
        jax.ShapeDtypeStruct(tile, F32),
        jax.ShapeDtypeStruct((rows, width), F32),
        jax.ShapeDtypeStruct((rows, width), BF16),
    ]
    out_specs = [whole(item.shape) for item in out_shape[:6]] + [any_spec()] * 2
    tail = products((4,), D, D) + products((), D, FF) + products((), FF, D)
    out_shape += tail
    out_specs += [whole(item.shape) for item in tail]
    shard_rows = D // data_count
    scratch = [
        pltpu.VMEM((2, rows, PAIR), BF16),
        pltpu.VMEM((2, rows, PAIR), BF16),
        pltpu.VMEM((2, total, PAIR), BF16),
        pltpu.VMEM((2, total, PAIR), BF16),
        pltpu.VMEM((2, PAIR, rows), F32),
        pltpu.VMEM((rows, width), BF16),
        pltpu.VMEM((total, width), BF16),
        pltpu.VMEM((total, width), BF16),
        pltpu.VMEM((width, total), BF16),
        pltpu.VMEM((3, 2, 2, far_count) + late, BF16),
        pltpu.VMEM((rows, width), F32),
        pltpu.VMEM((rows, width), BF16),
    ]
    scratch += [pltpu.VMEM((2, 2, far_count) + chunk.shape, BF16) for chunk in early_chunks(pieces)]
    for (_, _, order, _), chunk in zip(EARLY, early_chunks(pieces)):
        scratch += reduce_scratch(order, far_count, *chunk.shape)
    for member in range(3):
        scratch += reduce_scratch(LATE_REDUCE[member], far_count, *late)
    scratch += [pltpu.VMEM(root.shape, F32) for root in roots]
    scratch += [pltpu.VMEM(item.shape, BF16) for item in (states, twin_states, weights)]
    scratch += [
        pltpu.VMEM((4, far_count, 2, shard_rows, D), BF16),
        pltpu.VMEM((far_count, 2, shard_rows, FF), BF16),
        pltpu.VMEM((far_count, 2, FF // data_count, D), BF16),
        pltpu.VMEM((FF // model_count, FF // model_count), F32),
        pltpu.VMEM((shard_rows, D), F32),
        pltpu.VMEM((shard_rows, FF), F32),
        pltpu.VMEM((FF // data_count, D), F32),
    ]
    scratch += spread_scratch(far_count, tile) + spread_scratch(far_count, norm_rows.shape)
    chains = len(EARLY) + 6
    copies = chains * (reduce_copies(far_count) + gather_copies(far_count)) + 2 * spread_copies(far_count) + 1
    scratch += [
        pltpu.SemaphoreType.DMA((copies,)),
        pltpu.SemaphoreType.DMA((copies,)),
        pltpu.SemaphoreType.DMA((len(EARLY), 4)),
        pltpu.SemaphoreType.DMA((10,)),
    ]
    return pl.pallas_call(
        functools.partial(backward_kernel, far_count, counts, 1.0 / (rows * data_count * model_count)),
        name="backward",
        grid=(width // PAIR,),
        in_specs=[by_pair(rows), by_pair(rows), by_pair(total), by_pair(total), whole((total, PAIR))]
        + [by_pair(rows), by_pair(rows)]
        + [any_spec()] * 3
        + [whole(norm_rows.shape)]
        + [any_spec()] * 10,
        out_specs=out_specs,
        out_shape=out_shape,
        scratch_shapes=scratch,
        compiler_params=pltpu.CompilerParams(
            vmem_limit_bytes=BACKWARD_VMEM, collective_id=2, has_side_effects=True
        ),
    )(
        queries,
        query_extra,
        keys,
        values,
        key_extra,
        d_mixed,
        d_extra,
        states,
        twin_states,
        weights,
        norm_rows,
        skip,
        *[seen(low) for low in lows],
        *roots,
    )


def finish_kernel(limit, rate, squares_ref, norm_ref, own_ref, twin_ref, late_ref, *rest):
    (inner_piece, outer_piece, wo_piece, gains_ref, biases_ref), rest = rest[:5], rest[5:]
    stats, rest = rest[:6], rest[6:]
    products, rest = rest[:6], rest[6:]
    weights, rest = rest[:3], rest[3:]
    updates, rest = rest[:3], rest[3:]
    (states_out, norm_out, attention_grad, inner_grad, outer_grad, norm_grad), rest = rest[:6], rest[6:]
    weights_new, norm_new, stats_new = rest[:3], rest[3], rest[4:]
    norms = norm_ref[0:4, :]
    norm_square = jnp.sum(jnp.sum(norms * norms, axis=0, keepdims=True), axis=1, keepdims=True)
    grad_norm = jnp.sqrt(squares_ref[0:1, 0:1] + norm_square)
    norm_out[...] = grad_norm
    factor = jnp.minimum(1.0, limit / grad_norm)
    states_out[...] = (own_ref[...] + twin_ref[...].astype(F32)).astype(BF16)
    for member in range(3):
        attention_grad[member] = late_ref[member] * factor
    attention_grad[3] = wo_piece[...] * factor
    inner_grad[...] = inner_piece[...] * factor
    outer_grad[...] = outer_piece[...] * factor
    share = norm_grad.shape[-1]
    start = (lax.axis_index("dp") * lax.axis_size("mp") + lax.axis_index("mp")) * share
    params = jnp.concatenate([gains_ref[...], biases_ref[...]], axis=0)
    row = lax.broadcasted_iota(jnp.int32, (4, 1), 0) == start // D

    def share_of(table):
        picked = jnp.sum(jnp.where(row, table, 0.0), axis=0, keepdims=True)
        return pltpu.roll(jnp.broadcast_to(picked, (8, D)), (D - start % D) % D, 1)[0:1, :share]

    clipped = share_of(norms) * factor
    norm_grad[...] = clipped
    norm_new[...] = share_of(params) - rate * clipped
    for weight, change, out in zip(weights, updates, weights_new):
        out[...] = weight[...] - (step_rate * factor) * change[...]
    for stat, product, out in zip(stats, products, stats_new):
        out[...] = 0.5 * stat[...] + (0.5 * factor * factor) * product[...]


def finish(token_total, norm_share, squares, norm_rows, own, twin, late, pieces, gains, biases, stats, products, weights, updates):
    limit = 0.01 * math.sqrt((4 * D * D + 2 * D * FF + 4 * D) / token_total)
    rate = 20.0 * math.sqrt(token_total)
    inner_piece, outer_piece, _ = pieces
    shapes = [
        jax.ShapeDtypeStruct(own.shape, BF16),
        jax.ShapeDtypeStruct((1, 1), F32),
        jax.ShapeDtypeStruct(weights[0].shape, F32),
        jax.ShapeDtypeStruct(inner_piece.shape, F32),
        jax.ShapeDtypeStruct(outer_piece.shape, F32),
        jax.ShapeDtypeStruct((1, norm_share), F32),
    ]
    shapes += [jax.ShapeDtypeStruct(weight.shape, F32) for weight in weights]
    shapes.append(jax.ShapeDtypeStruct((1, norm_share), F32))
    shapes += [jax.ShapeDtypeStruct(stat.shape, F32) for stat in stats]
    operands = (squares, norm_rows, own, twin, late, *pieces, gains, biases)
    operands += (*stats, *products, *weights, *updates)
    return pl.pallas_call(
        functools.partial(finish_kernel, limit, rate),
        name="finish",
        in_specs=[vmem_spec()] * len(operands),
        out_specs=[vmem_spec()] * len(shapes),
        out_shape=shapes,
        compiler_params=pltpu.CompilerParams(vmem_limit_bytes=VMEM_LIMIT),
    )(*operands)


def middle_kernel(
    mixed_ref,
    states_ref,
    cotangent_ref,
    halting_ref,
    wo_ref,
    inner_any,
    outer_any,
    gains_ref,
    biases_ref,
    out_ref,
    dm_ref,
    dx_ref,
    skip_ref,
    norm_raw,
    inner_out,
    outer_out,
    wo_low,
    inner_ref,
    outer_ref,
    inner_low,
    outer_low,
    sems,
    gelu_slope,
    activated_ref,
    d_inner_ref,
    normed_ref,
    branch_ref,
    attended_ref,
    mixed_low_ref,
):
    step = pl.program_id(0)
    bring = [
        pltpu.make_async_copy(inner_any, inner_ref, sems.at[0]),
        pltpu.make_async_copy(outer_any, outer_ref, sems.at[1]),
    ]
    pl.when(step == 0)(lambda: start_all(bring))
    tokens = pl.ds(pl.multiple_of(step * TOKEN_ROWS, TOKEN_ROWS), TOKEN_ROWS)
    head_row = lax.broadcasted_iota(jnp.int32, (D, D), 0) // DH
    head_col = lax.broadcasted_iota(jnp.int32, (D, D), 1) // DH
    swap = jnp.where(head_row + 1 - 2 * (head_row % 2) == head_col, 1.0, 0.0).astype(BF16)

    def mean(value):
        return jnp.mean(value, axis=-1, keepdims=True)

    def total(value):
        return jnp.sum(value, axis=0, keepdims=True)

    def normalize(residual):
        centered = residual - mean(residual)
        scale = lax.rsqrt(mean(centered * centered) + epsilon)
        return centered * scale, scale

    def norm_back(d_out, gain, unit, scale):
        d_unit = d_out * gain
        return (d_unit - mean(d_unit) - unit * mean(d_unit * unit)) * scale

    mixed = mixed_ref[...]
    mixed_low = mixed.astype(BF16)
    hidden = states_ref[...].astype(F32)
    upstream = cotangent_ref[...].astype(F32)
    table = halting_ref[...].astype(F32).T
    lane = lax.broadcasted_iota(jnp.int32, (1, table.shape[1]), 1)
    here = step * (TOKEN_ROWS // 128)
    flags = [
        jnp.sum(jnp.where(lane == here + row, table, 0.0), axis=1, keepdims=True) for row in range(TOKEN_ROWS // 128)
    ]
    running = jnp.concatenate(flags, axis=0) == 1.0
    gain1, gain2 = gains_ref[0:1, :], gains_ref[1:2, :]
    unit1, scale1 = normalize(hidden + mm(mixed_low, wo_ref[...]))
    normed = unit1 * gain1 + biases_ref[0:1, :]
    normed_low = normed.astype(BF16)
    rate = math.sqrt(2.0 / math.pi)
    parts = [pl.ds(start, FF_PART) for start in range(0, FF, FF_PART)]
    branch = None
    pl.when(step == 0)(lambda: wait_all(bring))
    inner = mm(normed_low, inner_ref[:, parts[0]])
    for number, part in enumerate(parts):
        ahead = mm(normed_low, inner_ref[:, parts[number + 1]]) if number + 1 < len(parts) else None
        square = inner * inner
        bend = jnp.tanh(rate * inner * (1.0 + 0.044715 * square))
        half = 0.5 * (1.0 + bend)
        value = (inner * half).astype(BF16)
        activated_ref[tokens, part] = value
        gelu_slope[:, part] = half + 0.5 * inner * (1.0 - bend * bend) * (rate * (1.0 + 3 * 0.044715 * square))
        term = mm(value, outer_ref[part, :])
        branch = term if number == 0 else branch + term
        inner = ahead
    unit2, scale2 = normalize(normed + branch)
    final = unit2 * gain2 + biases_ref[1:2, :]
    out_ref[...] = jnp.where(running, final, hidden).astype(BF16)
    d_final = jnp.where(running, upstream, 0.0)
    d_resid2 = norm_back(d_final, gain2, unit2, scale2)
    d_branch = d_resid2.astype(BF16)
    d_normed = d_resid2
    d_act = mm(d_branch, outer_ref[parts[0], :], NT)
    for number, part in enumerate(parts):
        ahead = mm(d_branch, outer_ref[parts[number + 1], :], NT) if number + 1 < len(parts) else None
        d_inner = (d_act * gelu_slope[:, part]).astype(BF16)
        d_inner_ref[tokens, part] = d_inner
        d_normed = d_normed + mm(d_inner, inner_ref[:, part], NT)
        d_act = ahead
    d_resid1 = norm_back(d_normed, gain1, unit1, scale1)
    d_attended = d_resid1.astype(BF16)
    normed_ref[tokens, :] = normed_low
    branch_ref[tokens, :] = d_branch
    attended_ref[tokens, :] = d_attended
    mixed_low_ref[tokens, :] = mixed_low
    d_mixed = mm(d_attended, wo_ref[...], NT).astype(BF16)
    dm_ref[...] = d_mixed
    skip_ref[...] = jnp.where(running, 0.0, upstream) + d_resid1

    @pl.when(step == 0)
    def _():
        norm_raw[...] = jnp.zeros_like(norm_raw)

    norm_raw[0:1, :] += total(d_normed * unit1)
    norm_raw[1:2, :] += total(d_final * unit2)
    norm_raw[2:3, :] += total(d_normed)
    norm_raw[3:4, :] += total(d_final)
    high, low = split2(d_mixed.astype(F32) * mixed)
    delta = mm(high, swap) + mm(low, swap)
    pieces = split3(-delta)
    place = lax.broadcasted_iota(jnp.int32, (1, D), 1) % DH
    extra = jnp.zeros_like(delta)
    for number, part in enumerate(pieces):
        extra = jnp.where(place == number + 1, part, extra)
    dx_ref[...] = extra.astype(BF16)

    @pl.when(step == pl.num_programs(0) - 1)
    def _():
        wo_low[...] = mm(mixed_low_ref[...], attended_ref[...], TN).astype(BF16)
        outward = []
        for number, part in enumerate(parts):
            outer_low[part, :] = mm(activated_ref[:, part], branch_ref[...], TN).astype(BF16)
            outward.append(
                pltpu.make_async_copy(outer_low.at[part, :], outer_out.at[part, :], sems.at[2 + 2 * number])
            )
            outward[-1].start()
            inner_low[:, part] = mm(normed_ref[...], d_inner_ref[:, part], TN).astype(BF16)
            outward.append(
                pltpu.make_async_copy(inner_low.at[:, part], inner_out.at[:, part], sems.at[3 + 2 * number])
            )
            outward[-1].start()
        wait_all(outward)


def middle(mixed, states, cotangent, halting, wo, inner, outer, gains, biases):
    rows = mixed.shape[0]
    shapes = [jax.ShapeDtypeStruct((rows, D), BF16)] * 3
    shapes += [jax.ShapeDtypeStruct((rows, D), F32), jax.ShapeDtypeStruct((8, D), F32)]
    shapes += [jax.ShapeDtypeStruct(shape, BF16) for shape in ((D, FF), (FF, D), (D, D))]
    def by_token(item):
        return pl.BlockSpec((TOKEN_ROWS, D), lambda i: (i, 0))

    operands = (mixed, states, cotangent, halting.reshape(-1, 128), wo, inner, outer, gains, biases)
    return pl.pallas_call(
        middle_kernel,
        name="middle",
        grid=(rows // TOKEN_ROWS,),
        in_specs=[by_token(item) for item in operands[:3]]
        + [once(item.shape) for item in operands[3:5]]
        + [any_spec()] * 2
        + [once(item.shape) for item in operands[7:]],
        out_specs=[by_token(item) for item in shapes[:4]]
        + [once(shapes[4].shape), any_spec(), any_spec(), once(shapes[7].shape)],
        out_shape=shapes,
        scratch_shapes=[
            pltpu.VMEM((D, FF), BF16),
            pltpu.VMEM((FF, D), BF16),
            pltpu.VMEM((D, FF), BF16),
            pltpu.VMEM((FF, D), BF16),
            pltpu.SemaphoreType.DMA((2 + 2 * (FF // FF_PART),)),
            pltpu.VMEM((TOKEN_ROWS, FF), F32),
            pltpu.VMEM((rows, FF), BF16),
            pltpu.VMEM((rows, FF), BF16),
            pltpu.VMEM((rows, D), BF16),
            pltpu.VMEM((rows, D), BF16),
            pltpu.VMEM((rows, D), BF16),
            pltpu.VMEM((rows, D), BF16),
        ],
        compiler_params=pltpu.CompilerParams(vmem_limit_bytes=VMEM_LIMIT),
    )(*operands)


def per_device(
    states,
    cotangent,
    halting,
    lengths,
    attention_weights,
    inner_weight,
    outer_weight,
    norm_gains,
    norm_biases,
    attention_left,
    attention_right,
    inner_left,
    inner_right,
    outer_left,
    outer_right,
    attention_left_root,
    attention_right_root,
    inner_left_root,
    inner_right_root,
    outer_left_root,
    outer_right_root,
):
    data_count = lax.axis_size("dp")
    model_count = lax.axis_size("mp")
    counts = (data_count, model_count)
    far_count = data_count // 2
    token_total = states.shape[0] * data_count * model_count
    (
        mixed,
        query_extra,
        key_extra,
        weights,
        queries,
        keys,
        values,
        twin_states,
        inner_full,
        outer_full,
        wo_full,
    ) = front(states, attention_weights, inner_weight, outer_weight, lengths, far_count)
    output_states, d_mixed, d_extra, skip, norm_rows, *lows = middle(
        mixed,
        states,
        cotangent,
        halting,
        wo_full.reshape(D, D),
        inner_full.reshape(D, FF),
        outer_full.reshape(FF, D),
        norm_gains,
        norm_biases,
    )
    roots = (
        attention_left_root,
        attention_right_root,
        inner_left_root,
        inner_right_root,
        outer_left_root,
        outer_right_root,
    )
    *pieces, norm_total, late, squares, own, twin, p0, p1, p2, p3, p4, p5, p6, p7, p8 = backward(
        queries,
        query_extra,
        keys,
        values,
        key_extra,
        d_mixed,
        d_extra,
        states,
        twin_states,
        weights.reshape(3, D, D),
        norm_rows,
        skip,
        lows,
        roots,
        counts,
    )
    outs = finish(
        token_total,
        4 * D // (data_count * model_count),
        squares,
        norm_total,
        own,
        twin,
        late,
        pieces,
        norm_gains,
        norm_biases,
        (attention_left, attention_right, inner_left, inner_right, outer_left, outer_right),
        (p0, p1, p3, p4, p6, p7),
        (attention_weights, inner_weight, outer_weight),
        (p2, p5, p8),
    )
    states_grad, grad_norm, attention_grad, inner_grad, outer_grad, norm_grad = outs[:6]
    attention_new, inner_new, outer_new, norm_new = outs[6:10]
    return (
        output_states,
        states_grad,
        grad_norm.reshape(()),
        attention_grad,
        inner_grad,
        outer_grad,
        norm_grad.reshape(-1),
        attention_new,
        inner_new,
        outer_new,
        norm_new.reshape(-1),
        *outs[10:],
    )


def solution(mesh):
    grid = P("dp", "mp")
    stack = P(None, "dp", "mp")
    tokens = P(("dp", "mp"), None)
    flat = P(("dp", "mp"))
    return jax.shard_map(
        per_device,
        mesh=mesh,
        in_specs=(tokens, tokens, flat, P("dp"), stack, grid, grid, P(), P())
        + (stack, stack, grid, grid, grid, grid)
        + (P(None, "dp", None), P(None, None, "mp"), P("dp", None), P(None, "mp"), P("dp", None), P(None, "mp")),
        out_specs=(tokens, tokens, P(), stack, grid, grid, flat, stack, grid, grid, flat)
        + (stack, stack, grid, grid, grid, grid),
        check_vma=False,
    )
```

```python
import functools
import math

import jax
import jax.numpy as jnp
from jax import lax
from jax.experimental import pallas as pl
from jax.experimental.pallas import tpu as pltpu
from jax.sharding import PartitionSpec as P

D = 512
HEADS = 8
DH = 64
FF = 2048
SEQ = 2048
SEQ_GRP = 2
PAIR = 2 * DH
QUERY_ROWS = 256
FORWARD_CHUNKS = 1
KEY_ROWS = 256
FF_PART = 1024
TOKEN_ROWS = 512

F32 = jnp.float32
BF16 = jnp.bfloat16
epsilon = 1e-06
step_rate = 1.0
NN = (((1,), (0,)), ((), ()))
NT = (((1,), (1,)), ((), ()))
TN = (((0,), (0,)), ((), ()))
VMEM_LIMIT = 56 * 1024 * 1024
BACKWARD_VMEM = 62 * 1024 * 1024


def mm(left, right, dims=NN):
    return lax.dot_general(left, right, dims, preferred_element_type=F32)


def split2(value):
    high = value.astype(BF16)
    return high, (value - high.astype(F32)).astype(BF16)


def split3(value):
    high = value.astype(BF16).astype(F32)
    rest = value - high
    middle = rest.astype(BF16).astype(F32)
    return high, middle, rest - middle


MESH = pl.DeviceIdType.MESH


class Place:
    def __init__(self, far_count):
        data_rank = lax.axis_index("dp")
        self.far_count = far_count
        self.model = lax.axis_index("mp")
        self.far, self.near = data_rank // 2, data_rank % 2
        self.data_rank = 2 * self.far + self.near
        side, core = self.model // 2, self.model % 2
        self.side, self.core = side, core
        self.beside = 2 * (1 - side) + core
        self.twin = 2 * side + 1 - core
        self.twin_beside = 2 * (1 - side) + 1 - core
        self.to_beside = {"mp": self.beside}
        self.to_twin = {"mp": self.twin}
        self.to_near = {"dp": 2 * self.far + 1 - self.near}

    def other_far(self, step):
        return (self.far + step) % self.far_count

    def to_far(self, step):
        return {"dp": 2 * self.other_far(step) + self.near}

    def meet(self):
        barrier = pltpu.get_barrier_semaphore()
        partners = [self.to_far(step) for step in range(1, self.far_count)]
        partners += [self.to_near, self.to_beside, self.to_twin]
        for partner in partners:
            pl.semaphore_signal(barrier, inc=1, device_id=partner, device_id_type=MESH)
        pl.semaphore_wait(barrier, len(partners))


class Wires:
    def __init__(self, send_sems, recv_sems):
        self.sems = (send_sems, recv_sems)
        self.used = 0

    def copy(self, source, target, partner):
        index = self.used
        self.used += 1
        return pltpu.make_async_remote_copy(
            src_ref=source,
            dst_ref=target,
            send_sem=self.sems[0].at[index],
            recv_sem=self.sems[1].at[index],
            device_id=partner,
            device_id_type=MESH,
        )


def start_all(copies):
    for copy in copies:
        copy.start()


def wait_all(copies):
    for copy in copies:
        copy.wait()


def columns(index, size):
    return pl.ds(pl.multiple_of(index * size, size), size)


class Chunk:
    def __init__(self, rows, cols, row_size, col_size):
        self.rows, self.cols, self.row_size, self.col_size = rows, cols, row_size, col_size

    def columns(self, index):
        offset = pl.multiple_of(index * self.col_size + self.cols[0], math.gcd(self.col_size, max(self.cols[0], 128)))
        return pl.ds(offset, self.cols[1])

    @property
    def row_window(self):
        return pl.ds(*self.rows)

    @property
    def shape(self):
        return self.rows[1], self.cols[1]


def whole_chunk(rows, cols):
    return Chunk((0, rows), (0, cols), rows, cols)


class Staged:
    def __init__(self, active, twin_stage):
        self.active, self.twin_stage = active, twin_stage
        self.stages = []

    def start(self, number):
        copies = self.stages[number]
        if self.active is None:
            start_all(copies)
        elif number != self.twin_stage:
            pl.when(self.active)(lambda: start_all(copies))
        else:
            pl.when(self.sends)(lambda: start_all(copies))

    def wait(self, number):
        copies = self.stages[number]
        if self.active is None:
            wait_all(copies)
        elif number != self.twin_stage:
            pl.when(self.active)(lambda: wait_all(copies))
        else:

            @pl.when(self.sends)
            def _():
                for copy in copies:
                    copy.wait_send()

            @pl.when(jnp.logical_not(self.sends))
            def _():
                for copy in copies:
                    copy.wait_recv()


class Gather(Staged):
    def __init__(self, wires, place, full, order, chunk, active=None):
        super().__init__(active, len(order) - 1)
        self.sends = active
        mine, side = chunk.columns(place.model), chunk.columns(place.beside)
        self.home = full.at[place.far, place.near, chunk.row_window, mine]
        fars, nears, cols = place.far, place.near, [mine]

        def send(col, partner):
            view = full.at[fars, nears, chunk.row_window, col]
            return wires.copy(view, view, partner)

        for letter in order:
            if letter == "x":
                self.stages.append([send(mine, place.to_beside)])
                cols = [mine, side]
            elif letter == "y":
                self.stages.append([send(col, place.to_near) for col in cols])
                nears = slice(None)
            elif letter == "c":
                self.stages.append([send(col, place.to_twin) for col in cols])
            else:
                ways = [place.to_far(step) for step in range(1, place.far_count)]
                self.stages.append([send(col, way) for col in cols for way in ways])
                fars = slice(None)

    def begin(self):
        self.start(0)

    def advance(self, number):
        self.wait(number)
        if number + 1 < len(self.stages):
            self.start(number + 1)


GATHER_STEPS = 4


def gather_copies(far_count):
    return far_count + 6


def reduce_plan(order, far_count, rows, cols):
    slots, nears, fars = 2, 2, far_count
    plan = []
    for letter in order:
        if letter == "x":
            plan.append((letter, slots, nears, fars, (nears, fars, rows, cols)))
            slots = 1
        elif letter == "y":
            plan.append((letter, slots, nears, fars, (slots, fars, rows, cols)))
            nears = 1
        else:
            plan.append((letter, slots, nears, fars, (far_count, slots, nears, rows, cols)))
            fars = 1
    return plan


REDUCE_BUFFERS = 8
REDUCE_STEPS = 4


def reduce_copies(far_count):
    return far_count + 6


def reduce_scratch(order, far_count, rows, cols):
    shape = (2, 2, far_count, rows, cols)
    buffers = [pltpu.VMEM(shape, F32), pltpu.VMEM(shape, BF16)]
    for *_, shape in reduce_plan(order, far_count, rows, cols):
        buffers += [pltpu.VMEM(shape, BF16), pltpu.VMEM(shape, BF16)]
    return buffers


class Reducer(Staged):
    def __init__(self, wires, place, buffers, order, low=None, chunk=None, given=None, active=None):
        super().__init__(active, 0)
        self.sends = None if active is None else jnp.logical_not(active)
        self.place = place
        self.mine = None
        self.acc, self.got = buffers[:2]
        self.out, self.arrived = buffers[2::2], buffers[3::2]
        rows, size = self.acc.shape[-2:]
        self.plan = reduce_plan(order, place.far_count, rows, size)
        self.chunk = chunk
        self.kept = (place.model, place.beside)
        if given is not None:
            first = [wires.copy(given, self.got, place.to_twin)]
        else:
            twins = (place.twin, place.twin_beside)
            first = [
                wires.copy(
                    low.at[:, near, chunk.row_window, chunk.columns(twins[slot])],
                    self.got.at[slot, near],
                    place.to_twin,
                )
                for slot in range(2)
                for near in range(2)
            ]
        self.stages = [first]
        for (letter, *_), out, arrived in zip(self.plan, self.out, self.arrived):
            if letter == "z":
                stage = [
                    wires.copy(out.at[place.other_far(step)], arrived.at[step], place.to_far(step))
                    for step in range(1, place.far_count)
                ]
            else:
                stage = [wires.copy(out, arrived, place.to_beside if letter == "x" else place.to_near)]
            self.stages.append(stage)

    def loads(self, partial, mine, load_sems):
        self.mine = mine
        return [
            pltpu.make_async_copy(
                partial.at[:, near, self.chunk.row_window, self.chunk.columns(self.kept[slot])],
                mine.at[slot, near],
                load_sems.at[2 * slot + near],
            )
            for slot in range(2)
            for near in range(2)
        ]

    def begin(self):
        self.start(0)

    def held(self, number):
        letter, slots, nears, fars, _ = self.plan[number]
        place = self.place
        return (
            letter,
            range(slots),
            range(2) if nears == 2 else (place.near,),
            range(place.far_count) if fars > 1 else (place.far,),
        )

    def prepare(self, number):
        letter, slots, nears, fars = self.held(number)
        place, acc, out = self.place, self.acc, self.out[number]
        if letter == "x":
            for i, near in enumerate(nears):
                for j, far in enumerate(fars):
                    out[i, j] = acc[1, near, far].astype(BF16)
        elif letter == "y":
            for slot in slots:
                for j, far in enumerate(fars):
                    out[slot, j] = acc[slot, 1 - place.near, far].astype(BF16)
        else:
            for slot in slots:
                for i, near in enumerate(nears):
                    for far in fars:
                        out[far, slot, i] = acc[slot, near, far].astype(BF16)

    def absorb(self, number):
        letter, slots, nears, fars = self.held(number)
        place, acc, arrived = self.place, self.acc, self.arrived[number]
        if letter == "x":
            for i, near in enumerate(nears):
                for j, far in enumerate(fars):
                    acc[0, near, far] += arrived[i, j].astype(F32)
        elif letter == "y":
            for slot in slots:
                for j, far in enumerate(fars):
                    acc[slot, place.near, far] += arrived[slot, j].astype(F32)
        else:
            for slot in slots:
                for i, near in enumerate(nears):
                    total = acc[slot, near, place.far]
                    for step in range(1, place.far_count):
                        total = total + arrived[step, slot, i].astype(F32)
                    acc[slot, near, place.far] = total

    def advance(self, number):
        self.wait(number)

        def add():
            if number == 0:
                for slot in range(2):
                    for near in range(2):
                        for far in range(self.place.far_count):
                            spot = (slot, near, far)
                            own = self.acc[spot] if self.mine is None else self.mine[spot].astype(F32)
                            self.acc[spot] = own + self.got[spot].astype(F32)
            else:
                self.absorb(number - 1)
            if number < len(self.plan):
                self.prepare(number)

        if self.active is None:
            add()
        else:
            pl.when(self.active)(add)
        if number < len(self.plan):
            self.start(number + 1)

    def result(self):
        return self.acc[0, self.place.near, self.place.far]


class Spread:
    def __init__(self, wires, place, tile, stages, slots):
        self.place, self.tile, self.stages, self.slots = place, tile, stages, slots
        self.copies = [
            [wires.copy(tile, stages.at[number], partner)]
            for number, partner in enumerate((place.to_twin, place.to_beside, place.to_near))
        ]
        self.copies.append(
            [wires.copy(tile, slots.at[place.far], place.to_far(step)) for step in range(1, place.far_count)]
        )

    def begin(self):
        start_all(self.copies[0])

    def advance(self, number):
        wait_all(self.copies[number])
        if number == 3:
            self.slots[self.place.far] = self.tile[...]
            total = self.slots[0]
            for far in range(1, self.place.far_count):
                total = total + self.slots[far]
            self.tile[...] = total
        else:
            self.tile[...] += self.stages[number]
            start_all(self.copies[number + 1])


def spread_copies(far_count):
    return far_count - 1 + 3


def spread_scratch(far_count, shape):
    return [pltpu.VMEM(shape, F32), pltpu.VMEM((3,) + shape, F32), pltpu.VMEM((far_count,) + shape, F32)]


def any_spec():
    return pl.BlockSpec(memory_space=pl.ANY)


def vmem_spec():
    return pl.BlockSpec(memory_space=pltpu.VMEM)


def smem_spec():
    return pl.BlockSpec(memory_space=pltpu.SMEM)


def own_lanes(parity):
    lane = lax.broadcasted_iota(jnp.int32, (1, PAIR), 1)
    return (lane < DH) if parity == 0 else (lane >= DH)


def lane_in_half():
    return lax.broadcasted_iota(jnp.int32, (1, PAIR), 1) % DH


def blend(parity, own, extra):
    mine = jnp.where(own_lanes(parity), 1.0, 0.0)
    return own * mine.astype(BF16) + extra * (1.0 - mine).astype(BF16)


def slot_calls(step, width, calls):
    def at(sub_step):
        for slot, call in calls:
            if slot % width == sub_step:
                pl.when(step == slot // width)(call)

    return at


PROJECT_ORDERS = ("zxyc", "zyxc")
FORWARD_ORDERS = ("zxyc", "zyxc", "zyxc")
FORWARD_SLOTS = ((2, 10, 25), (2, 10, 26), (3, 11, 26))


def front_kernel(
    far_count,
    states_ref,
    states_any,
    attention_ref,
    inner_ref,
    outer_ref,
    lengths_ref,
    mixed_ref,
    qx_ref,
    extra_ref,
    weights_out,
    queries_out,
    keys_out,
    values_out,
    twin_out,
    inner_full,
    outer_full,
    wo_full,
    full,
    queries,
    keys,
    values,
    twin_states,
    twin_queries,
    inner_low,
    outer_low,
    wo_low,
    ka,
    va,
    score_a,
    score_b,
    send_sems,
    recv_sems,
    local_sems,
):
    rows = states_ref.shape[0]
    step = pl.program_id(0)
    here = Place(far_count)
    wires = Wires(send_sems, recv_sems)
    shard = full.shape[-2], full.shape[-1] // 4
    projections = [
        Gather(wires, here, full.at[member], PROJECT_ORDERS[member], whole_chunk(*shard)) for member in range(2)
    ]
    projections += [
        Gather(wires, here, full.at[2], PROJECT_ORDERS[core], whole_chunk(*shard), active=here.core == core)
        for core in range(2)
    ]
    fulls, lows = (inner_full, outer_full, wo_full), (inner_low, outer_low, wo_low)
    gathers = [
        Gather(wires, here, target, order, whole_chunk(*low.shape))
        for target, low, order in zip(fulls, lows, FORWARD_ORDERS)
    ]
    fill = [
        pltpu.make_async_copy(low, gather.home, local_sems.at[number])
        for number, (low, gather) in enumerate(zip(lows, gathers))
    ]
    swap_states = wires.copy(states_any, twin_states, here.to_twin)
    swaps = []
    for number, block in enumerate((here.model, here.beside)):
        cols = columns(block, PAIR)
        for kept in (keys, values):
            for start, end in ((0, rows), (rows, 0)):
                swaps.append(
                    wires.copy(kept.at[pl.ds(start, rows), cols], kept.at[pl.ds(end, rows), cols], here.to_twin)
                )
        swaps.append(wires.copy(twin_queries.at[number], queries.at[:, cols], here.to_twin))
    outward = [
        pltpu.make_async_copy(source, target, local_sems.at[3 + number])
        for number, (source, target) in enumerate(
            ((queries, queries_out), (keys, keys_out), (values, values_out), (twin_states, twin_out), (full, weights_out))
        )
    ]

    @pl.when(step == 0)
    def _():
        for member in range(3):
            full[member, here.far, here.near, :, columns(here.model, shard[1])] = attention_ref[member].astype(BF16)
        inner_low[...] = inner_ref[...].astype(BF16)
        outer_low[...] = outer_ref[...].astype(BF16)
        wo_low[...] = attention_ref[3].astype(BF16)
        start_all(fill)
        here.meet()
        for gather in projections:
            gather.begin()
        swap_states.start()
        index = lax.broadcasted_iota(jnp.int32, (2 * rows, 1), 0)
        half = here.model % 2
        position = jnp.where(index < rows, index + half * rows, index - half * rows)
        bias = jnp.where(position < lengths_ref[here.side], 0.0, -1e30)
        lane = lane_in_half()
        extra_ref[...] = jnp.where(lane == 0, bias, jnp.where(lane <= 3, 1.0, 0.0)).astype(BF16)
        wait_all(fill)
        for gather in projections:
            gather.advance(0)
        for gather in gathers:
            gather.begin()
        for gather in projections:
            gather.advance(1)
        swap_states.wait()
        for gather in projections:
            gather.advance(2)
        for member, kept in ((1, keys), (2, values), (0, queries)):
            both = jnp.concatenate(
                [full[member, :, :, :, columns(block, PAIR)].reshape(D, PAIR) for block in (here.model, here.beside)],
                axis=1,
            )
            own = mm(states_ref[...], both).astype(BF16)
            twin = mm(twin_states[...], both).astype(BF16)
            if member == 0:
                own = (own * DH ** (-0.5)).astype(BF16)
                twin = (twin * DH ** (-0.5)).astype(BF16)
            for number, block in enumerate((here.model, here.beside)):
                cols = columns(block, PAIR)
                kept[:rows, cols] = own[:, number * PAIR : (number + 1) * PAIR]
                if member:
                    kept[rows:, cols] = twin[:, number * PAIR : (number + 1) * PAIR]
                else:
                    twin_queries[number] = twin[:, number * PAIR : (number + 1) * PAIR]
        start_all(swaps)

    @pl.when(step == 2)
    def _():
        wait_all(swaps)
        for gather in projections:
            gather.advance(3)
        start_all(outward)

    calls = [
        (slot, functools.partial(gather.advance, number))
        for gather, slots in zip(gathers, FORWARD_SLOTS)
        for number, slot in enumerate(slots)
    ]
    at = slot_calls(step, 2 * (rows // QUERY_ROWS), calls)
    pair_cols = columns(2 * (step % 2) + (step // 2 + here.core) % 2, PAIR)
    place = lane_in_half()
    first = jnp.where(place == 0, 1.0, 0.0).astype(BF16)
    ones = jnp.where(place <= 3, 1.0, 0.0).astype(BF16)
    for parity in range(2):
        ka[parity] = blend(parity, keys[:, pair_cols], extra_ref[...])
        va[parity] = blend(parity, values[:, pair_cols], ones)
    steps = [(parity, block) for block in range(rows // QUERY_ROWS) for parity in range(2)]
    scratch = (score_a, score_b)

    chunk = keys.shape[0] // FORWARD_CHUNKS

    def query_part(index):
        parity, block = steps[index]
        return blend(parity, queries[pl.ds(block * QUERY_ROWS, QUERY_ROWS), pair_cols], first)

    def score(index, part, number):
        window = pl.ds(number * chunk, chunk)
        scores = mm(ka[steps[index][0], window, :], part, NT)
        scratch[index % 2][window, :] = scores
        return jnp.max(scores, axis=0, keepdims=True)

    part = query_part(0)
    row_max = score(0, part, 0)
    for number in range(1, FORWARD_CHUNKS):
        row_max = jnp.maximum(row_max, score(0, part, number))
    held = [None, None]
    logs = [None, None]
    row = lax.broadcasted_iota(jnp.int32, (PAIR, 1), 0)
    for index, (parity, block) in enumerate(steps):
        at(index)
        more = index + 1 < len(steps)
        part = query_part(index + 1) if more else None
        product, next_max = None, None
        for number in range(FORWARD_CHUNKS):
            if more:
                found = score(index + 1, part, number)
                next_max = found if number == 0 else jnp.maximum(next_max, found)
            window = pl.ds(number * chunk, chunk)
            shifted = jnp.exp(scratch[index % 2][window, :] - row_max).astype(BF16)
            term = mm(va[parity, window, :], shifted, TN)
            product = term if number == 0 else product + term
        sum_row = DH if parity == 0 else 0
        total = product[sum_row : sum_row + 1, :]
        held[parity] = product / total
        logs[parity] = row_max + jnp.log(total)
        row_max = next_max
        if parity == 1:
            window = pl.ds(block * QUERY_ROWS, QUERY_ROWS)
            both = jnp.concatenate([held[0][:DH], held[1][DH:]], axis=0)
            mixed_ref[window, pair_cols] = both.T
            parts = split3(-jnp.where(row < DH, logs[1], logs[0]))
            spot = row % DH
            extra = jnp.where(spot == 0, 1.0, 0.0)
            for number, part in enumerate(parts):
                extra = jnp.where(spot == number + 1, part, extra)
            qx_ref[window, pair_cols] = extra.T.astype(BF16)

    @pl.when(step == pl.num_programs(0) - 1)
    def _():
        for gather in gathers:
            gather.advance(GATHER_STEPS - 1)
        wait_all(outward)


def once(shape):
    return pl.BlockSpec(shape, lambda j: (0,) * len(shape), pipeline_mode=pl.Buffered(1))


def front(states, attention_weights, inner_shard, outer_shard, lengths, far_count):
    rows, width = states.shape
    total = 2 * rows
    shard_rows = attention_weights.shape[1]
    fulls = [
        jax.ShapeDtypeStruct((far_count, 2, height, wide), BF16)
        for height, wide in ((inner_shard.shape[0], FF), (outer_shard.shape[0], D), (shard_rows, D))
    ]
    copies = 7 * gather_copies(far_count) + 11
    weights_shape = (3, far_count, 2, shard_rows, D)
    return pl.pallas_call(
        functools.partial(front_kernel, far_count),
        name="front",
        grid=(width // PAIR,),
        in_specs=[once(states.shape), any_spec()]
        + [once(item.shape) for item in (attention_weights, inner_shard, outer_shard)]
        + [smem_spec()],
        out_specs=[once((rows, width)), once((rows, width)), once((total, PAIR))] + [any_spec()] * 8,
        out_shape=[
            jax.ShapeDtypeStruct((rows, width), F32),
            jax.ShapeDtypeStruct((rows, width), BF16),
            jax.ShapeDtypeStruct((total, PAIR), BF16),
            jax.ShapeDtypeStruct(weights_shape, BF16),
            jax.ShapeDtypeStruct((rows, width), BF16),
            jax.ShapeDtypeStruct((total, width), BF16),
            jax.ShapeDtypeStruct((total, width), BF16),
            jax.ShapeDtypeStruct((rows, width), BF16),
        ]
        + fulls,
        scratch_shapes=[
            pltpu.VMEM(weights_shape, BF16),
            pltpu.VMEM((rows, width), BF16),
            pltpu.VMEM((total, width), BF16),
            pltpu.VMEM((total, width), BF16),
            pltpu.VMEM((rows, width), BF16),
            pltpu.VMEM((2, rows, PAIR), BF16),
            pltpu.VMEM(inner_shard.shape, BF16),
            pltpu.VMEM(outer_shard.shape, BF16),
            pltpu.VMEM(attention_weights.shape[1:], BF16),
            pltpu.VMEM((2, total, PAIR), BF16),
            pltpu.VMEM((2, total, PAIR), BF16),
            pltpu.VMEM((total, QUERY_ROWS), F32),
            pltpu.VMEM((total, QUERY_ROWS), F32),
            pltpu.SemaphoreType.DMA((copies,)),
            pltpu.SemaphoreType.DMA((copies,)),
            pltpu.SemaphoreType.DMA((8,)),
        ],
        compiler_params=pltpu.CompilerParams(
            vmem_limit_bytes=VMEM_LIMIT, collective_id=1, has_side_effects=True
        ),
    )(states, states, attention_weights, inner_shard, outer_shard, lengths)


EARLY = (
    (0, 0, "yxz", "zyxc"),
    (1, 0, "xyz", "zxyc"),
    (2, None, "xyz", "zxyc"),
    (0, 1, "yxz", "zyxc"),
    (1, 1, "xyz", "zxyc"),
)
LATE_REDUCE = ("yxz", "xyz", "yxz")
LATE_GATHER = ("zyxc", "zxyc", "zyxc")
SCHEDULE = (
    (0, 0, 0), (0, 1, 0), (5, 0, 1), (5, 1, 1), (11, 0, 2), (11, 1, 2),
    (11, 2, 0), (11, 3, 0), (11, 4, 0), (15, 2, 1), (16, 0, 3), (16, 1, 3),
    (16, 3, 1), (16, 4, 1), (18, 2, 2), (19, 5, 1), (19, 6, 1), (19, 7, 1),
    (21, 0, 4), (21, 1, 4), (23, 2, 3), (23, 4, 2), (23, 6, 2), (24, 3, 2),
    (24, 5, 2), (24, 7, 2), (26, 0, 5), (26, 1, 5), (26, 2, 4), (26, 6, 3),
    (27, 4, 3), (28, 5, 3), (28, 7, 3), (29, 6, 4), (30, 1, 6), (30, 2, 5),
    (30, 3, 3), (31, 0, 6), (31, 5, 4), (31, 7, 4), (32, 6, 5), (32, 4, 4),
    (32, 2, 6), (32, -1, 0), (32, -1, 1), (32, 5, 5), (32, 7, 5), (32, 3, 4),
    (32, 10, 1), (32, 8, 1), (32, 9, 1), (32, 6, 6), (32, 1, 7), (32, 4, 5),
    (32, 0, 7), (32, 5, 6), (32, 7, 6), (32, 3, 5), (32, 1, 8), (32, 2, 7),
    (32, 10, 2), (32, 8, 2), (32, 0, 8), (32, 6, 7), (32, 9, 2), (32, 2, 8),
    (32, 6, 8), (32, 10, 3), (32, 8, 3), (32, 5, 7), (32, 7, 7), (32, 3, 6),
    (32, 4, 6), (32, 9, 3), (32, 10, 4), (32, 8, 4), (32, 5, 8), (32, 7, 8),
    (32, 9, 4), (32, -1, 11), (32, 10, 5), (32, 8, 5), (32, -1, 12), (32, 9, 5),
    (32, 3, 7), (32, 4, 7), (32, -1, 13), (32, 10, 6), (32, 8, 6), (32, 9, 6),
    (32, -1, 14), (32, 3, 8), (32, 4, 8), (32, -1, 2), (32, -1, 3), (32, -1, 4),
    (32, 10, 7), (32, 8, 7), (32, 9, 7), (32, -1, 15), (32, -1, 5), (32, -1, 6),
    (32, -1, 7), (32, -1, 8), (32, -1, 9), (32, 10, 8), (32, 8, 8), (32, 9, 8),
    (32, -1, 10),
)
NORM_SLOTS = (4, 7, 12, 16)


def early_chunks(shapes):
    chunks = []
    for array, half, *_ in EARLY:
        rows, cols = shapes[array]
        if half is None:
            chunks.append(whole_chunk(rows, cols))
        elif array == 0:
            chunks.append(Chunk((0, rows), (half * cols // 2, cols // 2), rows, cols))
        else:
            chunks.append(Chunk((half * rows // 2, rows // 2), (0, cols), rows, cols))
    return chunks


def product_steps(grad, left_root, right_root, place, counts, left_out, right_out, update_out, room, held):
    data_count, model_count = counts
    far_count, _, shard_rows, width = grad.shape
    height = data_count * shard_rows
    part = far_count // model_count
    size = width // model_count
    share = width // data_count

    def left():
        rows_here = grad[place.far, place.near]
        rows_there = grad[pl.ds(place.model * part, part)].reshape(height // model_count, width)
        left_out[...] = mm(rows_here, rows_there, NT)

    def right():
        cols_there = grad[:, :, :, columns(place.model, size)].reshape(height, size)
        if share % 128 == 0:
            cols_here = grad[:, :, :, columns(place.data_rank, share)].reshape(height, share)
            right_out[...] = mm(cols_here, cols_there, TN)
        else:
            group = data_count // model_count
            cols_here = grad[:, :, :, columns(place.data_rank // group, size)].reshape(height, size)
            room[:size, :size] = mm(cols_here, cols_there, TN)
            window = pl.ds(pl.multiple_of((place.data_rank % group) * share, share), share)
            right_out[...] = room[window, :size]

    def once():
        whole = grad[...].reshape(height, width)
        high, low = split2(left_root[...])
        held[...] = mm(high, whole) + mm(low, whole)

    def twice():
        chunk = min(512, width)
        total = jnp.zeros(update_out.shape, F32)
        for start in range(0, width, chunk):
            high, low = split2(held[:, start : start + chunk])
            root_high, root_low = split2(right_root[start : start + chunk, :])
            total = total + (mm(high, root_high) + mm(high, root_low) + mm(low, root_high))
        update_out[...] = total

    return [left, right, once, twice]


def backward_kernel(
    far_count,
    counts,
    inv_tokens,
    q_ref,
    qx_ref,
    k_ref,
    v_ref,
    kx_ref,
    do_ref,
    dox_ref,
    own_any_states,
    twin_any_states,
    weights_any,
    norm_raw,
    skip_any,
    inner_low,
    outer_low,
    wo_low,
    *rest,
):
    roots_any, rest = rest[:6], rest[6:]
    (inner_piece, outer_piece, wo_piece, norm_total, late_out, squares_out, own_any, twin_in), rest = rest[:8], rest[8:]
    products, rest = rest[:9], rest[9:]
    (qa, da, ka, va, dqt, dq, dk, dv, states_t, late_low, own_sum, twin_out), rest = rest[:12], rest[12:]
    mine, rest = rest[: len(EARLY)], rest[len(EARLY) :]
    count = len(EARLY) * REDUCE_BUFFERS
    early_buffers, rest = rest[:count], rest[count:]
    late_buffers, rest = rest[: 3 * REDUCE_BUFFERS], rest[3 * REDUCE_BUFFERS :]
    roots, rest = rest[:6], rest[6:]
    (own_states, twin_states, weights_ref), rest = rest[:3], rest[3:]
    (attention_full, inner_full, outer_full, room, held_small, held_wide, held_tall), rest = rest[:7], rest[7:]
    tile, tile_stages, tile_slots, norm_tile, norm_stages, norm_slots = rest[:6]
    send_sems, recv_sems, load_sems, local_sems = rest[6:]

    step = pl.program_id(0)
    rows = q_ref.shape[0]
    total = k_ref.shape[0]
    place = Place(far_count)
    wires = Wires(send_sems, recv_sems)
    lows = (inner_low, outer_low, wo_low)
    pieces = (inner_piece, outer_piece, wo_piece)
    fulls = (inner_full, outer_full, attention_full.at[3])
    chunks = early_chunks([piece.shape for piece in pieces])
    reducers = []
    gathers = []
    loads = []
    for number, (array, _, reduce_order, gather_order) in enumerate(EARLY):
        buffers = early_buffers[number * REDUCE_BUFFERS : (number + 1) * REDUCE_BUFFERS]
        reducer = Reducer(wires, place, buffers, reduce_order, low=lows[array], chunk=chunks[number])
        reducers.append(reducer)
        loads.append(reducer.loads(lows[array], mine[number], load_sems.at[number]))
        gathers.append(Gather(wires, place, fulls[array], gather_order, chunks[number]))
    late_shape = wo_piece.shape
    late_reducers = []
    late_gathers = []
    for late_set in range(2):
        active = place.core == late_set
        late_reducers.append(
            [
                Reducer(
                    wires,
                    place,
                    late_buffers[member * REDUCE_BUFFERS : (member + 1) * REDUCE_BUFFERS],
                    LATE_REDUCE[member],
                    given=late_low.at[member],
                    active=active,
                )
                for member in range(3)
            ]
        )
        late_gathers.append(
            [
                Gather(
                    wires, place, attention_full.at[member], LATE_GATHER[member], whole_chunk(*late_shape), active=active
                )
                for member in range(3)
            ]
        )
    norms = Spread(wires, place, norm_tile, norm_stages, norm_slots)
    squares = Spread(wires, place, tile, tile_stages, tile_slots)
    swap = wires.copy(twin_out, twin_in, place.to_twin)
    fetch = [
        pltpu.make_async_copy(source, target, local_sems.at[number])
        for number, (source, target) in enumerate(
            zip((*roots_any, skip_any, weights_any), (*roots, own_sum, weights_ref))
        )
    ]
    outward = pltpu.make_async_copy(own_sum, own_any, local_sems.at[0])
    bring = [
        pltpu.make_async_copy(own_any_states, own_states, local_sems.at[8]),
        pltpu.make_async_copy(twin_any_states, twin_states, local_sems.at[9]),
    ]

    def turn_states():
        wait_all(bring)
        states_t[:, :rows] = own_states[...].T
        states_t[:, rows:] = twin_states[...].T


    def early_call(number, number_of_step):
        array, chunk = EARLY[number][0], chunks[number]
        if number_of_step == 0:

            def call():
                reducers[number].begin()
                start_all(loads[number])

        elif number_of_step <= REDUCE_STEPS:

            def call():
                if number_of_step == 1:
                    wait_all(loads[number])
                reducers[number].advance(number_of_step - 1)
                if number_of_step == REDUCE_STEPS:
                    piece = reducers[number].result() * inv_tokens
                    pieces[array][chunk.row_window, pl.ds(*chunk.cols)] = piece
                    gathers[number].home[...] = piece.astype(BF16)
                    gathers[number].begin()

        else:

            def call():
                gathers[number].advance(number_of_step - REDUCE_STEPS - 1)

        return call

    def late_products():
        slot = (step + place.side) % 2
        wide = jnp.concatenate([dk[:, pair_cols], dv[:, pair_cols]], axis=1)
        both = mm(states_t[...], wide)
        values = (mm(states_t[:, :rows], dq[:, pair_cols]), both[:, :PAIR], both[:, PAIR:])
        active = place.core == step // 2
        for member, value in enumerate(values):
            parts = value.reshape(far_count, 2, *late_shape)

            @pl.when(active)
            def _():
                for near in range(2):
                    late_reducers[0][member].acc[slot, near] = parts[:, near]

            @pl.when(jnp.logical_not(active))
            def _():
                for near in range(2):
                    late_low[member, slot, near] = parts[:, near].astype(BF16)

    def late_call(late_set, member, number_of_step):
        reducer, gather = late_reducers[late_set][member], late_gathers[late_set][member]
        if number_of_step == 0:
            return reducer.begin

        def call():
            if number_of_step <= REDUCE_STEPS:
                reducer.advance(number_of_step - 1)
                if number_of_step == REDUCE_STEPS:

                    @pl.when(place.core == late_set)
                    def _():
                        piece = reducer.result() * inv_tokens
                        late_out[member] = piece
                        gather.home[...] = piece.astype(BF16)

                    gather.begin()
            else:
                gather.advance(number_of_step - REDUCE_STEPS - 1)

        return call

    def scheduled(chain, number_of_step):
        if chain < len(EARLY):
            return early_call(chain, number_of_step)
        return late_call(*divmod(chain - len(EARLY), 3), number_of_step)

    sub_steps = 4 * (total // KEY_ROWS)
    calls = [(slot, scheduled(chain, number)) for slot, chain, number in SCHEDULE if slot < sub_steps]
    calls += [(slot, functools.partial(norms.advance, stage)) for stage, slot in enumerate(NORM_SLOTS)]
    calls.append((12, lambda: start_all(fetch)))
    calls.append((6, turn_states))
    at = slot_calls(step, total // KEY_ROWS, calls)

    @pl.when(step == 0)
    def _():
        norm_tile[...] = norm_raw[...]
        place.meet()
        norms.begin()
        start_all(bring)

    lane = lane_in_half()
    ones = jnp.where(lane <= 3, 1.0, 0.0).astype(BF16)
    for parity in range(2):
        ka[parity] = blend(parity, k_ref[...], kx_ref[...])
        va[parity] = blend(parity, v_ref[...], ones)
        qa[parity] = blend(parity, q_ref[...], qx_ref[...])
        da[parity] = blend(parity, do_ref[...], dox_ref[...])
    dqt[...] = jnp.zeros_like(dqt)
    pair = 2 * (step % 2) + step // 2
    pair_cols = columns(pair, PAIR)
    for block in range(total // KEY_ROWS):
        at(block)
        window = pl.ds(block * KEY_ROWS, KEY_ROWS)
        key_grads = []
        value_grads = []
        for parity in range(2):
            key_block = ka[parity, window, :]
            probs = jnp.exp(mm(key_block, qa[parity], NT))
            d_probs = mm(va[parity, window, :], da[parity], NT)
            d_scores = (probs * d_probs).astype(BF16)
            value_grads.append(mm(probs.astype(BF16), da[parity]))
            key_grads.append(mm(d_scores, qa[parity]))
            dqt[parity] += mm(key_block, d_scores, TN)
        dk[window, pair_cols] = jnp.where(own_lanes(0), key_grads[0], key_grads[1]).astype(BF16)
        dv[window, pair_cols] = jnp.where(own_lanes(0), value_grads[0], value_grads[1]).astype(BF16)
    both = jnp.concatenate([dqt[0, :DH], dqt[1, DH:]], axis=0) * DH ** (-0.5)
    dq[:, pair_cols] = both.T.astype(BF16)

    late_products()
    for late_set in range(2):

        @pl.when(step == 2 * late_set + 1)
        def _():
            for member in range(3):
                late_call(late_set, member, 0)()

    @pl.when(step == pl.num_programs(0) - 1)
    def _():
        part = 256

        def twin_share():
            wait_all(fetch)

            @pl.loop(0, rows // part)
            def _(block):
                window = pl.ds(pl.multiple_of(block * part, part), part)
                there = pl.ds(pl.multiple_of(rows + block * part, part), part)
                value = mm(dk[there, :], weights_ref[1], NT) + mm(dv[there, :], weights_ref[2], NT)
                twin_out[window, :] = value.astype(BF16)

            swap.start()

        def own_share():
            @pl.loop(0, rows // part)
            def _(block):
                window = pl.ds(pl.multiple_of(block * part, part), part)
                own_sum[window, :] += (
                    mm(dq[window, :], weights_ref[0], NT)
                    + mm(dk[window, :], weights_ref[1], NT)
                    + mm(dv[window, :], weights_ref[2], NT)
                )

            outward.start()

        common = (place, counts)
        inner_steps = product_steps(inner_full, roots[2], roots[3], *common, *products[3:6], room, held_wide)
        outer_steps = product_steps(outer_full, roots[4], roots[5], *common, *products[6:9], room, held_tall)

        def member_products():
            @pl.loop(0, 4)
            def _(member):
                steps = product_steps(
                    attention_full.at[member],
                    roots[0].at[member],
                    roots[1].at[member],
                    *common,
                    *[product.at[member] for product in products[:3]],
                    room,
                    held_small,
                )
                for call in steps:
                    call()

        work = [twin_share, own_share, *outer_steps, *inner_steps, member_products]

        def square(piece):
            return jnp.sum(jnp.sum(piece * piece, axis=0, keepdims=True), axis=1, keepdims=True)

        def squares_begin():
            square_sum = square(inner_piece[...]) + square(outer_piece[...]) + square(wo_piece[...])
            for member in range(3):
                square_sum = square_sum + square(late_out[member])
            tile[...] = jnp.broadcast_to(square_sum, tile.shape)
            squares.begin()

        work.append(squares_begin)
        work += [functools.partial(squares.advance, stage) for stage in range(4)]
        for slot, chain, number in SCHEDULE:
            if slot >= sub_steps:
                (work[number] if chain < 0 else scheduled(chain, number))()
        squares_out[...] = tile[...]
        norm_total[...] = norm_tile[...] * inv_tokens
        swap.wait()
        outward.wait()


def backward(
    queries,
    query_extra,
    keys,
    values,
    key_extra,
    d_mixed,
    d_extra,
    states,
    twin_states,
    weights,
    norm_rows,
    skip,
    lows,
    roots,
    counts,
):
    rows, width = queries.shape
    total = keys.shape[0]
    data_count, model_count = counts
    far_count = data_count // 2

    def by_pair(height):
        return pl.BlockSpec((height, PAIR), lambda j: (0, 2 * (j % 2) + j // 2))

    whole = once

    def seen(array):
        return array.reshape(far_count, 2, array.shape[0] // data_count, array.shape[1])

    def products(lead, height, wide):
        return [
            jax.ShapeDtypeStruct(lead + shape, F32)
            for shape in (
                (height // data_count, height // model_count),
                (wide // data_count, wide // model_count),
                (height // data_count, wide // model_count),
            )
        ]

    pieces = [(low.shape[0] // data_count, low.shape[1] // model_count) for low in lows]
    late = pieces[2]
    tile = (8, 128)
    out_shape = [jax.ShapeDtypeStruct(piece, F32) for piece in pieces]
    out_shape += [
        jax.ShapeDtypeStruct(norm_rows.shape, F32),
        jax.ShapeDtypeStruct((3,) + late, F32),
        jax.ShapeDtypeStruct(tile, F32),
        jax.ShapeDtypeStruct((rows, width), F32),
        jax.ShapeDtypeStruct((rows, width), BF16),
    ]
    out_specs = [whole(item.shape) for item in out_shape[:6]] + [any_spec()] * 2
    tail = products((4,), D, D) + products((), D, FF) + products((), FF, D)
    out_shape += tail
    out_specs += [whole(item.shape) for item in tail]
    shard_rows = D // data_count
    scratch = [
        pltpu.VMEM((2, rows, PAIR), BF16),
        pltpu.VMEM((2, rows, PAIR), BF16),
        pltpu.VMEM((2, total, PAIR), BF16),
        pltpu.VMEM((2, total, PAIR), BF16),
        pltpu.VMEM((2, PAIR, rows), F32),
        pltpu.VMEM((rows, width), BF16),
        pltpu.VMEM((total, width), BF16),
        pltpu.VMEM((total, width), BF16),
        pltpu.VMEM((width, total), BF16),
        pltpu.VMEM((3, 2, 2, far_count) + late, BF16),
        pltpu.VMEM((rows, width), F32),
        pltpu.VMEM((rows, width), BF16),
    ]
    scratch += [pltpu.VMEM((2, 2, far_count) + chunk.shape, BF16) for chunk in early_chunks(pieces)]
    for (_, _, order, _), chunk in zip(EARLY, early_chunks(pieces)):
        scratch += reduce_scratch(order, far_count, *chunk.shape)
    for member in range(3):
        scratch += reduce_scratch(LATE_REDUCE[member], far_count, *late)
    scratch += [pltpu.VMEM(root.shape, F32) for root in roots]
    scratch += [pltpu.VMEM(item.shape, BF16) for item in (states, twin_states, weights)]
    scratch += [
        pltpu.VMEM((4, far_count, 2, shard_rows, D), BF16),
        pltpu.VMEM((far_count, 2, shard_rows, FF), BF16),
        pltpu.VMEM((far_count, 2, FF // data_count, D), BF16),
        pltpu.VMEM((FF // model_count, FF // model_count), F32),
        pltpu.VMEM((shard_rows, D), F32),
        pltpu.VMEM((shard_rows, FF), F32),
        pltpu.VMEM((FF // data_count, D), F32),
    ]
    scratch += spread_scratch(far_count, tile) + spread_scratch(far_count, norm_rows.shape)
    chains = len(EARLY) + 6
    copies = chains * (reduce_copies(far_count) + gather_copies(far_count)) + 2 * spread_copies(far_count) + 1
    scratch += [
        pltpu.SemaphoreType.DMA((copies,)),
        pltpu.SemaphoreType.DMA((copies,)),
        pltpu.SemaphoreType.DMA((len(EARLY), 4)),
        pltpu.SemaphoreType.DMA((10,)),
    ]
    return pl.pallas_call(
        functools.partial(backward_kernel, far_count, counts, 1.0 / (rows * data_count * model_count)),
        name="backward",
        grid=(width // PAIR,),
        in_specs=[by_pair(rows), by_pair(rows), by_pair(total), by_pair(total), whole((total, PAIR))]
        + [by_pair(rows), by_pair(rows)]
        + [any_spec()] * 3
        + [whole(norm_rows.shape)]
        + [any_spec()] * 10,
        out_specs=out_specs,
        out_shape=out_shape,
        scratch_shapes=scratch,
        compiler_params=pltpu.CompilerParams(
            vmem_limit_bytes=BACKWARD_VMEM, collective_id=2, has_side_effects=True
        ),
    )(
        queries,
        query_extra,
        keys,
        values,
        key_extra,
        d_mixed,
        d_extra,
        states,
        twin_states,
        weights,
        norm_rows,
        skip,
        *[seen(low) for low in lows],
        *roots,
    )


def finish_kernel(limit, rate, squares_ref, norm_ref, own_ref, twin_ref, late_ref, *rest):
    (inner_piece, outer_piece, wo_piece, gains_ref, biases_ref), rest = rest[:5], rest[5:]
    stats, rest = rest[:6], rest[6:]
    products, rest = rest[:6], rest[6:]
    weights, rest = rest[:3], rest[3:]
    updates, rest = rest[:3], rest[3:]
    (states_out, norm_out, attention_grad, inner_grad, outer_grad, norm_grad), rest = rest[:6], rest[6:]
    weights_new, norm_new, stats_new = rest[:3], rest[3], rest[4:]
    norms = norm_ref[0:4, :]
    norm_square = jnp.sum(jnp.sum(norms * norms, axis=0, keepdims=True), axis=1, keepdims=True)
    grad_norm = jnp.sqrt(squares_ref[0:1, 0:1] + norm_square)
    norm_out[...] = grad_norm
    factor = jnp.minimum(1.0, limit / grad_norm)
    states_out[...] = (own_ref[...] + twin_ref[...].astype(F32)).astype(BF16)
    for member in range(3):
        attention_grad[member] = late_ref[member] * factor
    attention_grad[3] = wo_piece[...] * factor
    inner_grad[...] = inner_piece[...] * factor
    outer_grad[...] = outer_piece[...] * factor
    share = norm_grad.shape[-1]
    start = (lax.axis_index("dp") * lax.axis_size("mp") + lax.axis_index("mp")) * share
    params = jnp.concatenate([gains_ref[...], biases_ref[...]], axis=0)
    row = lax.broadcasted_iota(jnp.int32, (4, 1), 0) == start // D

    def share_of(table):
        picked = jnp.sum(jnp.where(row, table, 0.0), axis=0, keepdims=True)
        return pltpu.roll(jnp.broadcast_to(picked, (8, D)), (D - start % D) % D, 1)[0:1, :share]

    clipped = share_of(norms) * factor
    norm_grad[...] = clipped
    norm_new[...] = share_of(params) - rate * clipped
    for weight, change, out in zip(weights, updates, weights_new):
        out[...] = weight[...] - (step_rate * factor) * change[...]
    for stat, product, out in zip(stats, products, stats_new):
        out[...] = 0.5 * stat[...] + (0.5 * factor * factor) * product[...]


def finish(token_total, norm_share, squares, norm_rows, own, twin, late, pieces, gains, biases, stats, products, weights, updates):
    limit = 0.01 * math.sqrt((4 * D * D + 2 * D * FF + 4 * D) / token_total)
    rate = 20.0 * math.sqrt(token_total)
    inner_piece, outer_piece, _ = pieces
    shapes = [
        jax.ShapeDtypeStruct(own.shape, BF16),
        jax.ShapeDtypeStruct((1, 1), F32),
        jax.ShapeDtypeStruct(weights[0].shape, F32),
        jax.ShapeDtypeStruct(inner_piece.shape, F32),
        jax.ShapeDtypeStruct(outer_piece.shape, F32),
        jax.ShapeDtypeStruct((1, norm_share), F32),
    ]
    shapes += [jax.ShapeDtypeStruct(weight.shape, F32) for weight in weights]
    shapes.append(jax.ShapeDtypeStruct((1, norm_share), F32))
    shapes += [jax.ShapeDtypeStruct(stat.shape, F32) for stat in stats]
    operands = (squares, norm_rows, own, twin, late, *pieces, gains, biases)
    operands += (*stats, *products, *weights, *updates)
    return pl.pallas_call(
        functools.partial(finish_kernel, limit, rate),
        name="finish",
        in_specs=[vmem_spec()] * len(operands),
        out_specs=[vmem_spec()] * len(shapes),
        out_shape=shapes,
        compiler_params=pltpu.CompilerParams(vmem_limit_bytes=VMEM_LIMIT),
    )(*operands)


def middle_kernel(
    mixed_ref,
    states_ref,
    cotangent_ref,
    halting_ref,
    wo_ref,
    inner_any,
    outer_any,
    gains_ref,
    biases_ref,
    out_ref,
    dm_ref,
    dx_ref,
    skip_ref,
    norm_raw,
    inner_out,
    outer_out,
    wo_low,
    inner_ref,
    outer_ref,
    inner_low,
    outer_low,
    sems,
    gelu_slope,
    activated_ref,
    d_inner_ref,
    normed_ref,
    branch_ref,
    attended_ref,
    mixed_low_ref,
):
    step = pl.program_id(0)
    bring = [
        pltpu.make_async_copy(inner_any, inner_ref, sems.at[0]),
        pltpu.make_async_copy(outer_any, outer_ref, sems.at[1]),
    ]
    pl.when(step == 0)(lambda: start_all(bring))
    tokens = pl.ds(pl.multiple_of(step * TOKEN_ROWS, TOKEN_ROWS), TOKEN_ROWS)
    head_row = lax.broadcasted_iota(jnp.int32, (D, D), 0) // DH
    head_col = lax.broadcasted_iota(jnp.int32, (D, D), 1) // DH
    swap = jnp.where(head_row + 1 - 2 * (head_row % 2) == head_col, 1.0, 0.0).astype(BF16)

    def mean(value):
        return jnp.mean(value, axis=-1, keepdims=True)

    def total(value):
        return jnp.sum(value, axis=0, keepdims=True)

    def normalize(residual):
        centered = residual - mean(residual)
        scale = lax.rsqrt(mean(centered * centered) + epsilon)
        return centered * scale, scale

    def norm_back(d_out, gain, unit, scale):
        d_unit = d_out * gain
        return (d_unit - mean(d_unit) - unit * mean(d_unit * unit)) * scale

    mixed = mixed_ref[...]
    mixed_low = mixed.astype(BF16)
    hidden = states_ref[...].astype(F32)
    upstream = cotangent_ref[...].astype(F32)
    table = halting_ref[...].astype(F32).T
    lane = lax.broadcasted_iota(jnp.int32, (1, table.shape[1]), 1)
    here = step * (TOKEN_ROWS // 128)
    flags = [
        jnp.sum(jnp.where(lane == here + row, table, 0.0), axis=1, keepdims=True) for row in range(TOKEN_ROWS // 128)
    ]
    running = jnp.concatenate(flags, axis=0) == 1.0
    gain1, gain2 = gains_ref[0:1, :], gains_ref[1:2, :]
    unit1, scale1 = normalize(hidden + mm(mixed_low, wo_ref[...]))
    normed = unit1 * gain1 + biases_ref[0:1, :]
    normed_low = normed.astype(BF16)
    rate = math.sqrt(2.0 / math.pi)
    parts = [pl.ds(start, FF_PART) for start in range(0, FF, FF_PART)]
    branch = None
    pl.when(step == 0)(lambda: wait_all(bring))
    inner = mm(normed_low, inner_ref[:, parts[0]])
    for number, part in enumerate(parts):
        ahead = mm(normed_low, inner_ref[:, parts[number + 1]]) if number + 1 < len(parts) else None
        square = inner * inner
        bend = jnp.tanh(rate * inner * (1.0 + 0.044715 * square))
        half = 0.5 * (1.0 + bend)
        value = (inner * half).astype(BF16)
        activated_ref[tokens, part] = value
        gelu_slope[:, part] = half + 0.5 * inner * (1.0 - bend * bend) * (rate * (1.0 + 3 * 0.044715 * square))
        term = mm(value, outer_ref[part, :])
        branch = term if number == 0 else branch + term
        inner = ahead
    unit2, scale2 = normalize(normed + branch)
    final = unit2 * gain2 + biases_ref[1:2, :]
    out_ref[...] = jnp.where(running, final, hidden).astype(BF16)
    d_final = jnp.where(running, upstream, 0.0)
    d_resid2 = norm_back(d_final, gain2, unit2, scale2)
    d_branch = d_resid2.astype(BF16)
    d_normed = d_resid2
    d_act = mm(d_branch, outer_ref[parts[0], :], NT)
    for number, part in enumerate(parts):
        ahead = mm(d_branch, outer_ref[parts[number + 1], :], NT) if number + 1 < len(parts) else None
        d_inner = (d_act * gelu_slope[:, part]).astype(BF16)
        d_inner_ref[tokens, part] = d_inner
        d_normed = d_normed + mm(d_inner, inner_ref[:, part], NT)
        d_act = ahead
    d_resid1 = norm_back(d_normed, gain1, unit1, scale1)
    d_attended = d_resid1.astype(BF16)
    normed_ref[tokens, :] = normed_low
    branch_ref[tokens, :] = d_branch
    attended_ref[tokens, :] = d_attended
    mixed_low_ref[tokens, :] = mixed_low
    d_mixed = mm(d_attended, wo_ref[...], NT).astype(BF16)
    dm_ref[...] = d_mixed
    skip_ref[...] = jnp.where(running, 0.0, upstream) + d_resid1

    @pl.when(step == 0)
    def _():
        norm_raw[...] = jnp.zeros_like(norm_raw)

    norm_raw[0:1, :] += total(d_normed * unit1)
    norm_raw[1:2, :] += total(d_final * unit2)
    norm_raw[2:3, :] += total(d_normed)
    norm_raw[3:4, :] += total(d_final)
    high, low = split2(d_mixed.astype(F32) * mixed)
    delta = mm(high, swap) + mm(low, swap)
    pieces = split3(-delta)
    place = lax.broadcasted_iota(jnp.int32, (1, D), 1) % DH
    extra = jnp.zeros_like(delta)
    for number, part in enumerate(pieces):
        extra = jnp.where(place == number + 1, part, extra)
    dx_ref[...] = extra.astype(BF16)

    @pl.when(step == pl.num_programs(0) - 1)
    def _():
        wo_low[...] = mm(mixed_low_ref[...], attended_ref[...], TN).astype(BF16)
        outward = []
        for number, part in enumerate(parts):
            outer_low[part, :] = mm(activated_ref[:, part], branch_ref[...], TN).astype(BF16)
            outward.append(
                pltpu.make_async_copy(outer_low.at[part, :], outer_out.at[part, :], sems.at[2 + 2 * number])
            )
            outward[-1].start()
            inner_low[:, part] = mm(normed_ref[...], d_inner_ref[:, part], TN).astype(BF16)
            outward.append(
                pltpu.make_async_copy(inner_low.at[:, part], inner_out.at[:, part], sems.at[3 + 2 * number])
            )
            outward[-1].start()
        wait_all(outward)


def middle(mixed, states, cotangent, halting, wo, inner, outer, gains, biases):
    rows = mixed.shape[0]
    shapes = [jax.ShapeDtypeStruct((rows, D), BF16)] * 3
    shapes += [jax.ShapeDtypeStruct((rows, D), F32), jax.ShapeDtypeStruct((8, D), F32)]
    shapes += [jax.ShapeDtypeStruct(shape, BF16) for shape in ((D, FF), (FF, D), (D, D))]
    def by_token(item):
        return pl.BlockSpec((TOKEN_ROWS, D), lambda i: (i, 0))

    operands = (mixed, states, cotangent, halting.reshape(-1, 128), wo, inner, outer, gains, biases)
    return pl.pallas_call(
        middle_kernel,
        name="middle",
        grid=(rows // TOKEN_ROWS,),
        in_specs=[by_token(item) for item in operands[:3]]
        + [once(item.shape) for item in operands[3:5]]
        + [any_spec()] * 2
        + [once(item.shape) for item in operands[7:]],
        out_specs=[by_token(item) for item in shapes[:4]]
        + [once(shapes[4].shape), any_spec(), any_spec(), once(shapes[7].shape)],
        out_shape=shapes,
        scratch_shapes=[
            pltpu.VMEM((D, FF), BF16),
            pltpu.VMEM((FF, D), BF16),
            pltpu.VMEM((D, FF), BF16),
            pltpu.VMEM((FF, D), BF16),
            pltpu.SemaphoreType.DMA((2 + 2 * (FF // FF_PART),)),
            pltpu.VMEM((TOKEN_ROWS, FF), F32),
            pltpu.VMEM((rows, FF), BF16),
            pltpu.VMEM((rows, FF), BF16),
            pltpu.VMEM((rows, D), BF16),
            pltpu.VMEM((rows, D), BF16),
            pltpu.VMEM((rows, D), BF16),
            pltpu.VMEM((rows, D), BF16),
        ],
        compiler_params=pltpu.CompilerParams(vmem_limit_bytes=VMEM_LIMIT),
    )(*operands)


def per_device(
    states,
    cotangent,
    halting,
    lengths,
    attention_weights,
    inner_weight,
    outer_weight,
    norm_gains,
    norm_biases,
    attention_left,
    attention_right,
    inner_left,
    inner_right,
    outer_left,
    outer_right,
    attention_left_root,
    attention_right_root,
    inner_left_root,
    inner_right_root,
    outer_left_root,
    outer_right_root,
):
    data_count = lax.axis_size("dp")
    model_count = lax.axis_size("mp")
    counts = (data_count, model_count)
    far_count = data_count // 2
    token_total = states.shape[0] * data_count * model_count
    (
        mixed,
        query_extra,
        key_extra,
        weights,
        queries,
        keys,
        values,
        twin_states,
        inner_full,
        outer_full,
        wo_full,
    ) = front(states, attention_weights, inner_weight, outer_weight, lengths, far_count)
    output_states, d_mixed, d_extra, skip, norm_rows, *lows = middle(
        mixed,
        states,
        cotangent,
        halting,
        wo_full.reshape(D, D),
        inner_full.reshape(D, FF),
        outer_full.reshape(FF, D),
        norm_gains,
        norm_biases,
    )
    roots = (
        attention_left_root,
        attention_right_root,
        inner_left_root,
        inner_right_root,
        outer_left_root,
        outer_right_root,
    )
    *pieces, norm_total, late, squares, own, twin, p0, p1, p2, p3, p4, p5, p6, p7, p8 = backward(
        queries,
        query_extra,
        keys,
        values,
        key_extra,
        d_mixed,
        d_extra,
        states,
        twin_states,
        weights.reshape(3, D, D),
        norm_rows,
        skip,
        lows,
        roots,
        counts,
    )
    outs = finish(
        token_total,
        4 * D // (data_count * model_count),
        squares,
        norm_total,
        own,
        twin,
        late,
        pieces,
        norm_gains,
        norm_biases,
        (attention_left, attention_right, inner_left, inner_right, outer_left, outer_right),
        (p0, p1, p3, p4, p6, p7),
        (attention_weights, inner_weight, outer_weight),
        (p2, p5, p8),
    )
    states_grad, grad_norm, attention_grad, inner_grad, outer_grad, norm_grad = outs[:6]
    attention_new, inner_new, outer_new, norm_new = outs[6:10]
    return (
        output_states,
        states_grad,
        grad_norm.reshape(()),
        attention_grad,
        inner_grad,
        outer_grad,
        norm_grad.reshape(-1),
        attention_new,
        inner_new,
        outer_new,
        norm_new.reshape(-1),
        *outs[10:],
    )


def solution(mesh):
    grid = P("dp", "mp")
    stack = P(None, "dp", "mp")
    tokens = P(("dp", "mp"), None)
    flat = P(("dp", "mp"))
    return jax.shard_map(
        per_device,
        mesh=mesh,
        in_specs=(tokens, tokens, flat, P("dp"), stack, grid, grid, P(), P())
        + (stack, stack, grid, grid, grid, grid)
        + (P(None, "dp", None), P(None, None, "mp"), P("dp", None), P(None, "mp"), P("dp", None), P(None, "mp")),
        out_specs=(tokens, tokens, P(), stack, grid, grid, flat, stack, grid, grid, flat)
        + (stack, stack, grid, grid, grid, grid),
        check_vma=False,
    )
```
